512 devices in a mesh: kgrp: 16 (over y, x), energy: 32 (over z, core).
Axes of the slice: x: 4, y: 4, z: 16, core: 2. Of those that a mesh axis runs over, the one named last changes fastest.
Arguments:
- greens: float32 [2, 2, 2, 1024, 4096], P(None, None, None, 'kgrp', 'energy'), may hold values from -6 to 6
- current: float32 [2, 2, 2, 1024, 4096], P(None, None, None, ('kgrp', 'energy')), may hold values from -6 to 6
- past_inputs: float32 [5, 2, 2, 2, 1024, 4096], P(None, None, None, None, ('kgrp', 'energy')), may hold values from -6 to 6
- past_residuals: float32 [5, 2, 2, 2, 1024, 4096], P(None, None, None, None, ('kgrp', 'energy')), may hold values from -40 to 40
- slot_order: int32 [5], replicated, may hold values from 0 to 4, each once
- neighbour: int32 [1024, 5], P('kgrp'), may hold values from 0 to 1023, as said below
- momentum_class: int32 [1024], P('kgrp'), may hold values from 0 to 3
- stencil_weight: float32 [5], replicated, may hold values from 0.1 to 0.4
- acoustic_coupling: float32 [4], replicated, may hold values from 0.3 to 1.5
- optical_coupling: float32 [2], replicated, may hold values from 0.2 to 0.6
- occupation: float32 [2], replicated, may hold values from 0.1 to 1
- phonon_shift: int32 [2], replicated, may hold values from 32 to 96, as said below
Outputs:
- mixed: float32 [2, 2, 2, 1024, 4096], P(None, None, None, ('kgrp', 'energy'))
The draws below stay inside these ranges and needn't reach their ends.
Inputs may be any that keep to these rules, and one draw needn't show every extreme that they name: `neighbour`: each index names a momentum of the row's own group of 64 consecutive momenta or of the group just before or after it, counted periodically over all groups. `phonon_shift`: the larger of the two shifts is exactly 96.
All inputs are finite; a program needn't handle non-finite values.
Results may differ from the reference program's by a relative error of at most 0.000053.
Values sent between devices are 32-bit elements; how exact they have to be, the bound alone decides.
A program may use at most 64 MiB of HBM per device.

```python
import math
import jax
import jax.numpy as jnp
from jax import lax

POS = 2
K_GRP = 64
SHIFT_MAX = 96
NCLS = 4
HIST = 5
NK = 1024
NE = 4096


def draw_past_residuals(key, part):
    shape = (HIST, 2, 2, POS, NK, NE)
    subkeys = jax.random.split(key, 3)
    row_log = jax.random.uniform(subkeys[1], (HIST, 1, 1, 1, NK, 1), jnp.float32)
    column_log = jax.random.uniform(subkeys[2], (1, 1, 1, 1, 1, NE), jnp.float32)
    position = jnp.arange(NK, dtype=jnp.float32).reshape(1, 1, 1, 1, NK, 1) / max(NK - 1, 1)
    values = jnp.clip(jax.random.normal(subkeys[0], shape, jnp.float32), -4.0, 4.0)
    slope_scale = jnp.exp(position * math.log(3.0))
    divisor = 30.0
    scales = jnp.exp(row_log * math.log(10.0)) * jnp.exp(column_log * math.log(10.0)) * slope_scale
    return (values * scales / divisor).astype(jnp.float32)


def draw_neighbour(key, part):
    subkeys = jax.random.split(key, 2)
    groups = NK // K_GRP
    row_ids = jnp.arange(NK, dtype=jnp.int32)[:, None]
    offset_group = jax.random.randint(subkeys[0], (NK, 5), -1, 2, dtype=jnp.int32)
    member = jax.random.randint(subkeys[1], (NK, 5), 0, K_GRP, dtype=jnp.int32)
    target = (row_ids // K_GRP + offset_group + groups) % groups * K_GRP + member
    target = target.at[0, 0].set(NK - 1).at[NK - 1, 0].set(0)
    return target.astype(jnp.int32)


def draw_phonon_shift(key, part):
    subkeys = jax.random.split(key, 2)
    smaller = jax.random.randint(subkeys[0], (1,), SHIFT_MAX // 3, SHIFT_MAX, dtype=jnp.int32)
    swapped = jax.random.randint(subkeys[1], (1,), 0, 2, dtype=jnp.int32)
    largest = jnp.full((1,), SHIFT_MAX, jnp.int32)
    shifts_pair = jnp.concatenate([largest, smaller])
    return jnp.where(swapped == 1, shifts_pair[::-1], shifts_pair).astype(jnp.int32)


def plant(result, stream_key, least, high):
    extent = result.shape
    index_at = [jax.random.randint(jax.random.fold_in(stream_key, axis), (), 0, extent[axis]) for axis in range(len(extent))]
    result = result.at[tuple(index_at)].set(least)
    longest = extent.index(max(extent))
    index_at[longest] = (index_at[longest] + 1) % extent[longest]
    return result.at[tuple(index_at)].set(high)


def block_scale(stream_key, dims, shards, low, top_value):
    gain, own = 1.0, jax.random.fold_in(stream_key, 6)
    for dim, blocks in shards:
        steps = jnp.exp(jax.random.uniform(jax.random.fold_in(own, dim), (blocks,), jnp.float32, low / len(shards), top_value / len(shards)))
        gain = gain * jnp.repeat(steps, dims[dim] // blocks).reshape([-1 if axis == dim else 1 for axis in range(len(dims))])
    return gain


def noise(rng, dims, scale, bound, shards=(), held_as=jnp.bfloat16):
    factor_of = block_scale(rng, dims, shards, -0.22, 0.18) if shards else 1.0
    result = jax.random.normal(rng, dims, jnp.float32) * scale * factor_of
    return jnp.minimum(jnp.maximum(result, -bound), bound).astype(held_as)


def setup_inputs(seed: int = 0) -> dict:
    arg_keys = jax.random.split(jax.random.key(seed), 13)
    return {
        "greens": noise(arg_keys[0], (2, 2, POS, NK, NE), 1.0, 6.0, ((3, 16), (4, 32)), jnp.float32),
        "current": noise(arg_keys[1], (2, 2, POS, NK, NE), 1.0, 6.0, ((3, 512),), jnp.float32),
        "past_inputs": noise(arg_keys[2], (HIST, 2, 2, POS, NK, NE), 1.0, 6.0, ((4, 512),), jnp.float32),
        "past_residuals": draw_past_residuals(jax.random.fold_in(arg_keys[12], 71), 0),
        "slot_order": jax.random.permutation(arg_keys[4], HIST).astype(jnp.int32),
        "neighbour": draw_neighbour(jax.random.fold_in(arg_keys[12], 71), 0),
        "momentum_class": plant(jax.random.randint(arg_keys[6], (NK,), 0, NCLS), jax.random.fold_in(arg_keys[6], 1), 0, NCLS - 1).astype(jnp.int32),
        "stencil_weight": jnp.clip(jax.random.uniform(arg_keys[7], (5,), jnp.float32, 0.1, 0.4), 0.1, 0.4),
        "acoustic_coupling": jnp.clip(jnp.exp(jax.random.uniform(arg_keys[8], (NCLS,), jnp.float32, math.log(0.3), math.log(1.5))), 0.3, 1.5),
        "optical_coupling": jnp.clip(jnp.exp(jax.random.uniform(arg_keys[9], (2,), jnp.float32, math.log(0.2), math.log(0.6))), 0.2, 0.6),
        "occupation": jnp.clip(jnp.exp(jax.random.uniform(arg_keys[10], (2,), jnp.float32, math.log(0.1), math.log(1.0))), 0.1, 1.0),
        "phonon_shift": draw_phonon_shift(jax.random.fold_in(arg_keys[12], 71), 0),
    }


mixing_share = 0.5
ridge_share = 0.1

def emit(padded, margin, length, coupling_row, optical, occupation, shifts):
    lesser = padded[0]
    greater = padded[1]

    def energy_view(source, offset):
        return lax.dynamic_slice_in_dim(source, margin + offset, length, axis=source.ndim - 1)
    sigma_less = coupling_row[:, None] * energy_view(lesser, 0)
    sigma_more = coupling_row[:, None] * energy_view(greater, 0)
    for column in range(2):
        strength = optical[column]
        number = occupation[column]
        offset = shifts[column]
        sigma_less = sigma_less + strength * ((number + 1.0) * energy_view(lesser, offset) + number * energy_view(lesser, -offset))
        sigma_more = sigma_more + strength * ((number + 1.0) * energy_view(greater, -offset) + number * energy_view(greater, offset))
    return jnp.stack([sigma_less, sigma_more])

def solve_spd(matrix, vector):
    factor = jnp.linalg.cholesky(matrix)
    size_n = matrix.shape[0]
    forward = []
    for column in range(size_n):
        summed = vector[column]
        for earlier in range(column):
            summed = summed - factor[column, earlier] * forward[earlier]
        forward.append(summed / factor[column, column])
    backward = [None] * size_n
    for column in range(size_n - 1, -1, -1):
        summed = forward[column]
        for earlier in range(column + 1, size_n):
            summed = summed - factor[earlier, column] * backward[earlier]
        backward[column] = summed / factor[column, column]
    return jnp.stack(backward)

def mix_weights(products):
    size_n = products.shape[0] - 1
    differ_rows = jnp.eye(size_n, size_n + 1, dtype=jnp.float32) - jnp.eye(size_n, size_n + 1, k=1, dtype=jnp.float32)
    system = jnp.dot(jnp.dot(differ_rows, products, precision=lax.Precision.HIGHEST), differ_rows.T, precision=lax.Precision.HIGHEST)
    target = jnp.dot(differ_rows, products[:, 0], precision=lax.Precision.HIGHEST)
    ridge = ridge_share * jnp.trace(system) / size_n + 1e-06
    gamma = solve_spd(system + ridge * jnp.eye(size_n, dtype=jnp.float32), target)
    unit = jnp.zeros((size_n + 1,), jnp.float32).at[0].set(1.0)
    return unit - jnp.dot(differ_rows.T, gamma, precision=lax.Precision.HIGHEST)

def reference(greens, current, past_inputs, past_residuals, slot_order, neighbour, momentum_class, stencil_weight, acoustic_coupling, optical_coupling, occupation, phonon_shift):
    smeared = jnp.zeros_like(greens)
    for column in range(5):
        smeared = smeared + stencil_weight[column] * jnp.take(greens, neighbour[:, column], axis=3)
    coupling_row = acoustic_coupling[momentum_class]
    padded = jnp.pad(smeared, [(0, 0)] * 4 + [(SHIFT_MAX, SHIFT_MAX)])
    sigma_new = emit(padded, SHIFT_MAX, NE, coupling_row, optical_coupling, occupation, phonon_shift)
    residual_now = sigma_new - current
    older_res = jnp.take(past_residuals, slot_order, axis=0)
    older_in = jnp.take(past_inputs, slot_order, axis=0)
    stacked = jnp.concatenate([residual_now.reshape(1, -1), older_res.reshape(HIST, -1)], axis=0)
    products = jnp.dot(stacked, stacked.T, precision=lax.Precision.HIGHEST) / stacked.shape[1]
    weights = mix_weights(products)
    mixed = weights[0] * (current + mixing_share * residual_now)
    for column in range(HIST):
        mixed = mixed + weights[column + 1] * (older_in[column] + mixing_share * older_res[column])
    return mixed
```

```python
import functools

import jax
import jax.numpy as jnp
from jax import lax
from jax.experimental import pallas as pl
from jax.experimental.pallas import tpu as pltpu
from jax.sharding import PartitionSpec as P

SHIFT_MAX = 96
HIST = 5

mixing_share = 0.5
ridge_share = 0.1

MESH = pl.DeviceIdType.MESH


def padded_2(block, sides, width, periodic):
    for axis, dim in sides:
        count = lax.axis_size(axis)
        forward = [(i, i + 1) for i in range(count - 1)]
        if periodic:
            forward.append((count - 1, 0))
        backward = [(target, source) for source, target in forward]
        low = lax.ppermute(
            lax.slice_in_dim(block, block.shape[dim] - width, None, axis=dim), axis, forward
        )
        high = lax.ppermute(lax.slice_in_dim(block, 0, width, axis=dim), axis, backward)
        block = jnp.concatenate([low, block, high], axis=dim)
    return block


def emit(padded, margin, length, coupling_row, optical, occupation, shifts):
    lesser = padded[0]
    greater = padded[1]

    def energy_view(source, offset):
        return lax.dynamic_slice_in_dim(source, margin + offset, length, axis=source.ndim - 1)

    sigma_less = coupling_row[:, None] * energy_view(lesser, 0)
    sigma_more = coupling_row[:, None] * energy_view(greater, 0)
    for column in range(2):
        strength = optical[column]
        number = occupation[column]
        offset = shifts[column]
        sigma_less = sigma_less + strength * (
            (number + 1.0) * energy_view(lesser, offset) + number * energy_view(lesser, -offset)
        )
        sigma_more = sigma_more + strength * (
            (number + 1.0) * energy_view(greater, -offset) + number * energy_view(greater, offset)
        )
    return jnp.stack([sigma_less, sigma_more])


def _pick(mask, x, axis):
    return jnp.sum(jnp.where(mask, x, 0.0), axis=axis, keepdims=True)


def _weights_from_products(prod):
    size_n = HIST
    row = lax.broadcasted_iota(jnp.int32, prod.shape, 0)
    col = lax.broadcasted_iota(jnp.int32, prod.shape, 1)
    rows, cols = prod.shape
    down = pltpu.roll(prod, rows - 1, 0)
    right = pltpu.roll(prod, cols - 1, 1)
    diag = pltpu.roll(down, cols - 1, 1)
    inside = (row < size_n) & (col < size_n)
    system = jnp.where(inside, prod - right - down + diag, 0.0)
    target = _pick((col == 0) & (row < size_n), prod - down, 1)
    eye = inside & (row == col)
    trace = jnp.sum(jnp.where(eye, system, 0.0), keepdims=True)
    ridge = ridge_share * trace / size_n + 1e-06
    a = system + jnp.where(eye, ridge, 0.0)
    lower = jnp.zeros_like(a)
    upper = jnp.zeros_like(a)
    for j in range(size_n):
        pivot = jnp.sqrt(_pick((row == j) & (col == j), a, None).reshape(1, 1))
        lcol = jnp.where(row[:, :1] >= j, _pick(col == j, a, 1) / pivot, 0.0)
        lrow = jnp.where(col[:1, :] >= j, _pick(row == j, a, 0) / pivot, 0.0)
        lower = lower + jnp.where(col == j, lcol, 0.0)
        upper = upper + jnp.where(row == j, lrow, 0.0)
        a = a - lcol * lrow
    row1 = row[:, :1]
    rest = target
    forward = jnp.zeros_like(target)
    for i in range(size_n):
        lii = _pick((row == i) & (col == i), lower, None).reshape(1, 1)
        yi = _pick(row1 == i, rest, 0) / lii
        forward = forward + jnp.where(row1 == i, yi, 0.0)
        rest = rest - jnp.where(row1 > i, _pick(col == i, lower, 1), 0.0) * yi
    rest = forward
    gamma = jnp.zeros_like(target)
    for i in range(size_n - 1, -1, -1):
        lii = _pick((row == i) & (col == i), lower, None).reshape(1, 1)
        gi = _pick(row1 == i, rest, 0) / lii
        gamma = gamma + jnp.where(row1 == i, gi, 0.0)
        rest = rest - jnp.where(row1 < i, _pick(col == i, upper, 1), 0.0) * gi
    before = pltpu.roll(gamma, 1, 0)
    weights = jnp.where(row1 == 0, 1.0, 0.0) - gamma + before
    return jnp.broadcast_to(weights, prod.shape)


def _allreduce_weights_kernel(nk, ne, entries, p_ref, w_ref, recv1, recv2, acc1, ss1, rs1, ss2, rs2):
    mk = lax.axis_index("kgrp")
    me = lax.axis_index("energy")
    barrier = pltpu.get_barrier_semaphore()
    for s in range(nk - 1):
        pl.semaphore_signal(barrier, 1, device_id=((mk + s + 1) % nk, me), device_id_type=MESH)
    for s in range(ne - 1):
        pl.semaphore_signal(barrier, 1, device_id=(mk, (me + s + 1) % ne), device_id_type=MESH)
    pl.semaphore_wait(barrier, nk - 1 + ne - 1)

    def exchange(src, recv, ssem, rsem, count, peer):
        copies = []
        for s in range(count - 1):
            c = pltpu.make_async_remote_copy(
                src_ref=src,
                dst_ref=recv.at[count - 2 - s],
                send_sem=ssem.at[s],
                recv_sem=rsem.at[count - 2 - s],
                device_id=peer(s),
                device_id_type=MESH,
            )
            c.start()
            copies.append(c)
        for s in range(count - 1):
            copies[s].wait_recv()
        for s in range(count - 1):
            copies[s].wait_send()

    def total(own, recv, mine, count):
        acc = jnp.zeros_like(own)
        for idx in range(count):
            slot = jnp.minimum((idx - mine - 1 + count) % count, count - 2)
            acc = acc + jnp.where(idx == mine, own, recv[slot])
        return acc

    exchange(p_ref, recv1, ss1, rs1, nk, lambda s: ((mk + s + 1) % nk, me))
    acc1[...] = total(p_ref[...], recv1, mk, nk)
    exchange(acc1, recv2, ss2, rs2, ne, lambda s: (mk, (me + s + 1) % ne))
    summed = total(acc1[...], recv2, me, ne)
    w_ref[...] = _weights_from_products(summed / entries)


def allreduce_weights(prod_tile, nk, ne, entries):
    return pl.pallas_call(
        functools.partial(_allreduce_weights_kernel, nk, ne, entries),
        out_shape=jax.ShapeDtypeStruct(prod_tile.shape, jnp.float32),
        in_specs=[pl.BlockSpec(memory_space=pltpu.VMEM)],
        out_specs=pl.BlockSpec(memory_space=pltpu.VMEM),
        scratch_shapes=[
            pltpu.VMEM((nk - 1,) + prod_tile.shape, jnp.float32),
            pltpu.VMEM((ne - 1,) + prod_tile.shape, jnp.float32),
            pltpu.VMEM(prod_tile.shape, jnp.float32),
            pltpu.SemaphoreType.DMA((nk - 1,)),
            pltpu.SemaphoreType.DMA((nk - 1,)),
            pltpu.SemaphoreType.DMA((ne - 1,)),
            pltpu.SemaphoreType.DMA((ne - 1,)),
        ],
        compiler_params=pltpu.CompilerParams(collective_id=0, has_side_effects=True),
    )(prod_tile)


def per_device(
    greens,
    current,
    past_inputs,
    past_residuals,
    slot_order,
    neighbour,
    momentum_class,
    stencil_weight,
    acoustic_coupling,
    optical_coupling,
    occupation,
    phonon_shift,
):
    group_len = greens.shape[3]
    rows_here = current.shape[3]
    group_id = lax.axis_index("kgrp")
    energy_id = lax.axis_index("energy")
    nk = lax.axis_size("kgrp")
    ne = lax.axis_size("energy")
    total_k = group_len * nk
    extended = padded_2(greens, (("kgrp", 3),), group_len, True)
    local_index = (neighbour - group_id * group_len + group_len) % total_k
    smeared = jnp.zeros_like(greens)
    for column in range(5):
        smeared = smeared + stencil_weight[column] * jnp.take(
            extended, local_index[:, column], axis=3
        )
    rows = lax.all_to_all(smeared, "energy", split_axis=3, concat_axis=4, tiled=True)
    classes = acoustic_coupling.shape[0]
    my_class = lax.dynamic_slice_in_dim(momentum_class, energy_id * rows_here, rows_here)
    coupling_row = jnp.sum(
        jnp.where(
            my_class[:, None] == jnp.arange(classes, dtype=jnp.int32)[None, :],
            acoustic_coupling[None, :],
            0.0,
        ),
        axis=1,
    )
    pad = [(0, 0)] * (rows.ndim - 1) + [(SHIFT_MAX, SHIFT_MAX)]
    padded = jnp.pad(rows, pad)
    sigma_new = emit(
        padded, SHIFT_MAX, rows.shape[-1], coupling_row, optical_coupling, occupation, phonon_shift
    )
    residual_now = sigma_new - current
    older_res = jnp.take(past_residuals, slot_order, axis=0)
    older_in = jnp.take(past_inputs, slot_order, axis=0)
    fresh = residual_now.reshape(1, -1)
    stacked = jnp.concatenate([fresh, older_res.reshape(HIST, -1)], axis=0)
    products = jnp.dot(stacked, stacked.T, precision=lax.Precision.HIGHEST)
    prod_tile = jnp.zeros((8, 128), jnp.float32).at[: HIST + 1, : HIST + 1].set(products)
    entries = float(fresh.shape[1] * nk * ne)
    weights = allreduce_weights(prod_tile, nk, ne, entries)[: HIST + 1, 0]
    mixed = weights[0] * (current + mixing_share * residual_now)
    for column in range(HIST):
        mixed = mixed + weights[column + 1] * (
            older_in[column] + mixing_share * older_res[column]
        )
    return mixed


def solution(mesh):
    return jax.shard_map(
        per_device,
        mesh=mesh,
        in_specs=(
            P(None, None, None, "kgrp", "energy"),
            P(None, None, None, ("kgrp", "energy"), None),
            P(None, None, None, None, ("kgrp", "energy"), None),
            P(None, None, None, None, ("kgrp", "energy"), None),
            P(),
            P("kgrp", None),
            P("kgrp"),
            P(),
            P(),
            P(),
            P(),
            P(),
        ),
        out_specs=P(None, None, None, ("kgrp", "energy"), None),
        check_vma=False,
    )
```

```python
import functools

import jax
import jax.numpy as jnp
from jax import lax
from jax.experimental import pallas as pl
from jax.experimental.pallas import tpu as pltpu
from jax.sharding import PartitionSpec as P

SHIFT_MAX = 96
HIST = 5

mixing_share = 0.5
ridge_share = 0.1

MESH = pl.DeviceIdType.MESH


def padded_2(block, sides, width, periodic):
    for axis, dim in sides:
        count = lax.axis_size(axis)
        forward = [(i, i + 1) for i in range(count - 1)]
        if periodic:
            forward.append((count - 1, 0))
        backward = [(target, source) for source, target in forward]
        low = lax.ppermute(
            lax.slice_in_dim(block, block.shape[dim] - width, None, axis=dim), axis, forward
        )
        high = lax.ppermute(lax.slice_in_dim(block, 0, width, axis=dim), axis, backward)
        block = jnp.concatenate([low, block, high], axis=dim)
    return block


def emit(padded, margin, length, coupling_row, optical, occupation, shifts):
    lesser = padded[0]
    greater = padded[1]

    def energy_view(source, offset):
        return lax.dynamic_slice_in_dim(source, margin + offset, length, axis=source.ndim - 1)

    sigma_less = coupling_row[:, None] * energy_view(lesser, 0)
    sigma_more = coupling_row[:, None] * energy_view(greater, 0)
    for column in range(2):
        strength = optical[column]
        number = occupation[column]
        offset = shifts[column]
        sigma_less = sigma_less + strength * (
            (number + 1.0) * energy_view(lesser, offset) + number * energy_view(lesser, -offset)
        )
        sigma_more = sigma_more + strength * (
            (number + 1.0) * energy_view(greater, -offset) + number * energy_view(greater, offset)
        )
    return jnp.stack([sigma_less, sigma_more])


def _pick(mask, x, axis):
    return jnp.sum(jnp.where(mask, x, 0.0), axis=axis, keepdims=True)


def _weights_from_products(prod):
    size_n = HIST
    row = lax.broadcasted_iota(jnp.int32, prod.shape, 0)
    col = lax.broadcasted_iota(jnp.int32, prod.shape, 1)
    rows, cols = prod.shape
    down = pltpu.roll(prod, rows - 1, 0)
    right = pltpu.roll(prod, cols - 1, 1)
    diag = pltpu.roll(down, cols - 1, 1)
    inside = (row < size_n) & (col < size_n)
    system = jnp.where(inside, prod - right - down + diag, 0.0)
    target = _pick((col == 0) & (row < size_n), prod - down, 1)
    eye = inside & (row == col)
    trace = jnp.sum(jnp.where(eye, system, 0.0), keepdims=True)
    ridge = ridge_share * trace / size_n + 1e-06
    a = system + jnp.where(eye, ridge, 0.0)
    lower = jnp.zeros_like(a)
    upper = jnp.zeros_like(a)
    for j in range(size_n):
        pivot = jnp.sqrt(_pick((row == j) & (col == j), a, None).reshape(1, 1))
        lcol = jnp.where(row[:, :1] >= j, _pick(col == j, a, 1) / pivot, 0.0)
        lrow = jnp.where(col[:1, :] >= j, _pick(row == j, a, 0) / pivot, 0.0)
        lower = lower + jnp.where(col == j, lcol, 0.0)
        upper = upper + jnp.where(row == j, lrow, 0.0)
        a = a - lcol * lrow
    row1 = row[:, :1]
    rest = target
    forward = jnp.zeros_like(target)
    for i in range(size_n):
        lii = _pick((row == i) & (col == i), lower, None).reshape(1, 1)
        yi = _pick(row1 == i, rest, 0) / lii
        forward = forward + jnp.where(row1 == i, yi, 0.0)
        rest = rest - jnp.where(row1 > i, _pick(col == i, lower, 1), 0.0) * yi
    rest = forward
    gamma = jnp.zeros_like(target)
    for i in range(size_n - 1, -1, -1):
        lii = _pick((row == i) & (col == i), lower, None).reshape(1, 1)
        gi = _pick(row1 == i, rest, 0) / lii
        gamma = gamma + jnp.where(row1 == i, gi, 0.0)
        rest = rest - jnp.where(row1 < i, _pick(col == i, upper, 1), 0.0) * gi
    before = pltpu.roll(gamma, 1, 0)
    weights = jnp.where(row1 == 0, 1.0, 0.0) - gamma + before
    return jnp.broadcast_to(weights, prod.shape)


def _permute_square(prod, perm):
    row = lax.broadcasted_iota(jnp.int32, prod.shape, 0)
    col = lax.broadcasted_iota(jnp.int32, prod.shape, 1)
    count = len(perm)
    permcol = jnp.zeros((prod.shape[0], 1), jnp.int32)
    permrow = jnp.zeros((1, prod.shape[1]), jnp.int32)
    for i in range(count):
        permcol = jnp.where(row[:, :1] == i, perm[i], permcol)
        permrow = jnp.where(col[:1, :] == i, perm[i], permrow)
    by_rows = jnp.zeros_like(prod)
    for m in range(count):
        by_rows = by_rows + jnp.where(permcol == m, _pick(row == m, prod, 0), 0.0)
    by_rows = jnp.where(row < count, by_rows, 0.0)
    both = jnp.zeros_like(prod)
    for m in range(count):
        both = both + jnp.where(permrow == m, _pick(col == m, by_rows, 1), 0.0)
    return jnp.where(col < count, both, 0.0)


def _allreduce_weights_kernel(nk, ne, entries, slot_ref, p_ref, w_ref, recv1, recv2, acc1, ss1, rs1, ss2, rs2):
    mk = lax.axis_index("kgrp")
    me = lax.axis_index("energy")
    barrier = pltpu.get_barrier_semaphore()
    for s in range(nk - 1):
        pl.semaphore_signal(barrier, 1, device_id=((mk + s + 1) % nk, me), device_id_type=MESH)
    for s in range(ne - 1):
        pl.semaphore_signal(barrier, 1, device_id=(mk, (me + s + 1) % ne), device_id_type=MESH)
    pl.semaphore_wait(barrier, nk - 1 + ne - 1)

    def exchange(src, recv, ssem, rsem, count, peer):
        copies = []
        for s in range(count - 1):
            c = pltpu.make_async_remote_copy(
                src_ref=src,
                dst_ref=recv.at[count - 2 - s],
                send_sem=ssem.at[s],
                recv_sem=rsem.at[count - 2 - s],
                device_id=peer(s),
                device_id_type=MESH,
            )
            c.start()
            copies.append(c)
        for s in range(count - 1):
            copies[s].wait_recv()
        for s in range(count - 1):
            copies[s].wait_send()

    def total(own, recv, mine, count):
        acc = jnp.zeros_like(own)
        for idx in range(count):
            slot = jnp.minimum((idx - mine - 1 + count) % count, count - 2)
            acc = acc + jnp.where(idx == mine, own, recv[slot])
        return acc

    exchange(p_ref, recv1, ss1, rs1, nk, lambda s: ((mk + s + 1) % nk, me))
    acc1[...] = total(p_ref[...], recv1, mk, nk)
    exchange(acc1, recv2, ss2, rs2, ne, lambda s: (mk, (me + s + 1) % ne))
    summed = total(acc1[...], recv2, me, ne)
    perm = [0] + [slot_ref[i] + 1 for i in range(HIST)]
    aged = _permute_square(summed / entries, perm)
    weights = _weights_from_products(aged)[:, :1]
    row1 = lax.broadcasted_iota(jnp.int32, weights.shape, 0)
    by_slot = jnp.zeros_like(weights)
    for i in range(HIST + 1):
        by_slot = by_slot + jnp.where(row1 == perm[i], _pick(row1 == i, weights, 0), 0.0)
    w_ref[...] = jnp.broadcast_to(by_slot, w_ref.shape)


def allreduce_weights(slot_order, prod_tile, nk, ne, entries):
    return pl.pallas_call(
        functools.partial(_allreduce_weights_kernel, nk, ne, entries),
        out_shape=jax.ShapeDtypeStruct(prod_tile.shape, jnp.float32),
        in_specs=[
            pl.BlockSpec(memory_space=pltpu.SMEM),
            pl.BlockSpec(memory_space=pltpu.VMEM),
        ],
        out_specs=pl.BlockSpec(memory_space=pltpu.VMEM),
        scratch_shapes=[
            pltpu.VMEM((nk - 1,) + prod_tile.shape, jnp.float32),
            pltpu.VMEM((ne - 1,) + prod_tile.shape, jnp.float32),
            pltpu.VMEM(prod_tile.shape, jnp.float32),
            pltpu.SemaphoreType.DMA((nk - 1,)),
            pltpu.SemaphoreType.DMA((nk - 1,)),
            pltpu.SemaphoreType.DMA((ne - 1,)),
            pltpu.SemaphoreType.DMA((ne - 1,)),
        ],
        compiler_params=pltpu.CompilerParams(collective_id=0, has_side_effects=True),
    )(slot_order, prod_tile)


def per_device(
    greens,
    current,
    past_inputs,
    past_residuals,
    slot_order,
    neighbour,
    momentum_class,
    stencil_weight,
    acoustic_coupling,
    optical_coupling,
    occupation,
    phonon_shift,
):
    group_len = greens.shape[3]
    rows_here = current.shape[3]
    group_id = lax.axis_index("kgrp")
    energy_id = lax.axis_index("energy")
    nk = lax.axis_size("kgrp")
    ne = lax.axis_size("energy")
    total_k = group_len * nk
    ends = padded_2(greens, (("kgrp", 3),), group_len, True)
    low = ends[:, :, :, :group_len]
    high = ends[:, :, :, 2 * group_len :]
    local_index = (neighbour - group_id * group_len + group_len) % total_k
    stencil = jnp.sum(
        jnp.where(
            local_index[:, :, None] == jnp.arange(3 * group_len, dtype=jnp.int32)[None, None, :],
            stencil_weight[None, :, None],
            0.0,
        ),
        axis=1,
    )
    lead = greens.shape[:3]
    flat = lambda x: x.reshape((-1,) + x.shape[3:])
    smeared = jnp.zeros_like(flat(greens))
    for part, block in enumerate((low, greens, high)):
        smeared = smeared + jnp.einsum(
            "kr,bre->bke",
            stencil[:, part * group_len : (part + 1) * group_len],
            flat(block),
            precision=lax.Precision.HIGHEST,
        )
    smeared = smeared.reshape(lead + smeared.shape[1:])
    rows = lax.all_to_all(smeared, "energy", split_axis=3, concat_axis=4, tiled=True)
    classes = acoustic_coupling.shape[0]
    my_class = lax.dynamic_slice_in_dim(momentum_class, energy_id * rows_here, rows_here)
    coupling_row = jnp.sum(
        jnp.where(
            my_class[:, None] == jnp.arange(classes, dtype=jnp.int32)[None, :],
            acoustic_coupling[None, :],
            0.0,
        ),
        axis=1,
    )
    pad = [(0, 0)] * (rows.ndim - 1) + [(SHIFT_MAX, SHIFT_MAX)]
    padded = jnp.pad(rows, pad)
    sigma_new = emit(
        padded, SHIFT_MAX, rows.shape[-1], coupling_row, optical_coupling, occupation, phonon_shift
    )
    residual_now = sigma_new - current
    data_axes = tuple(range(1, past_residuals.ndim))
    old_gram = jnp.sum(past_residuals[:, None] * past_residuals[None, :], axis=tuple(a + 1 for a in data_axes))
    cross = jnp.sum(residual_now[None] * past_residuals, axis=data_axes)
    self_term = jnp.sum(residual_now * residual_now)
    top = jnp.concatenate([self_term[None], cross])
    products = jnp.concatenate([top[None, :], jnp.concatenate([cross[:, None], old_gram], axis=1)], axis=0)
    prod_tile = jnp.pad(products, ((0, 8 - HIST - 1), (0, 128 - HIST - 1)))
    entries = float(residual_now.size * nk * ne)
    weights = allreduce_weights(slot_order, prod_tile, nk, ne, entries)[: HIST + 1, 0]
    mixed = weights[0] * (current + mixing_share * residual_now)
    for column in range(HIST):
        mixed = mixed + weights[column + 1] * (
            past_inputs[column] + mixing_share * past_residuals[column]
        )
    return mixed


def solution(mesh):
    return jax.shard_map(
        per_device,
        mesh=mesh,
        in_specs=(
            P(None, None, None, "kgrp", "energy"),
            P(None, None, None, ("kgrp", "energy"), None),
            P(None, None, None, None, ("kgrp", "energy"), None),
            P(None, None, None, None, ("kgrp", "energy"), None),
            P(),
            P("kgrp", None),
            P("kgrp"),
            P(),
            P(),
            P(),
            P(),
            P(),
        ),
        out_specs=P(None, None, None, ("kgrp", "energy"), None),
        check_vma=False,
    )
```

```python
import functools

import jax
import jax.numpy as jnp
from jax import lax
from jax.experimental import pallas as pl
from jax.experimental.pallas import tpu as pltpu
from jax.sharding import PartitionSpec as P

SHIFT_MAX = 96
HIST = 5

mixing_share = 0.5
ridge_share = 0.1

MESH = pl.DeviceIdType.MESH


def padded_2(block, sides, width, periodic):
    for axis, dim in sides:
        count = lax.axis_size(axis)
        forward = [(i, i + 1) for i in range(count - 1)]
        if periodic:
            forward.append((count - 1, 0))
        backward = [(target, source) for source, target in forward]
        low = lax.ppermute(
            lax.slice_in_dim(block, block.shape[dim] - width, None, axis=dim), axis, forward
        )
        high = lax.ppermute(lax.slice_in_dim(block, 0, width, axis=dim), axis, backward)
        block = jnp.concatenate([low, block, high], axis=dim)
    return block


def emit(padded, margin, length, coupling_row, optical, occupation, shifts):
    lesser = padded[0]
    greater = padded[1]

    def energy_view(source, offset):
        return lax.dynamic_slice_in_dim(source, margin + offset, length, axis=source.ndim - 1)

    sigma_less = coupling_row[:, None] * energy_view(lesser, 0)
    sigma_more = coupling_row[:, None] * energy_view(greater, 0)
    for column in range(2):
        strength = optical[column]
        number = occupation[column]
        offset = shifts[column]
        sigma_less = sigma_less + strength * (
            (number + 1.0) * energy_view(lesser, offset) + number * energy_view(lesser, -offset)
        )
        sigma_more = sigma_more + strength * (
            (number + 1.0) * energy_view(greater, -offset) + number * energy_view(greater, offset)
        )
    return jnp.stack([sigma_less, sigma_more])


def _pick(mask, x, axis):
    return jnp.sum(jnp.where(mask, x, 0.0), axis=axis, keepdims=True)


def _weights_from_products(prod):
    size_n = HIST
    row = lax.broadcasted_iota(jnp.int32, prod.shape, 0)
    col = lax.broadcasted_iota(jnp.int32, prod.shape, 1)
    rows, cols = prod.shape
    down = pltpu.roll(prod, rows - 1, 0)
    right = pltpu.roll(prod, cols - 1, 1)
    diag = pltpu.roll(down, cols - 1, 1)
    inside = (row < size_n) & (col < size_n)
    system = jnp.where(inside, prod - right - down + diag, 0.0)
    target = _pick((col == 0) & (row < size_n), prod - down, 1)
    eye = inside & (row == col)
    trace = jnp.sum(jnp.where(eye, system, 0.0), keepdims=True)
    ridge = ridge_share * trace / size_n + 1e-06
    a = system + jnp.where(eye, ridge, 0.0)
    lower = jnp.zeros_like(a)
    upper = jnp.zeros_like(a)
    for j in range(size_n):
        pivot = jnp.sqrt(_pick((row == j) & (col == j), a, None).reshape(1, 1))
        lcol = jnp.where(row[:, :1] >= j, _pick(col == j, a, 1) / pivot, 0.0)
        lrow = jnp.where(col[:1, :] >= j, _pick(row == j, a, 0) / pivot, 0.0)
        lower = lower + jnp.where(col == j, lcol, 0.0)
        upper = upper + jnp.where(row == j, lrow, 0.0)
        a = a - lcol * lrow
    row1 = row[:, :1]
    rest = target
    forward = jnp.zeros_like(target)
    for i in range(size_n):
        lii = _pick((row == i) & (col == i), lower, None).reshape(1, 1)
        yi = _pick(row1 == i, rest, 0) / lii
        forward = forward + jnp.where(row1 == i, yi, 0.0)
        rest = rest - jnp.where(row1 > i, _pick(col == i, lower, 1), 0.0) * yi
    rest = forward
    gamma = jnp.zeros_like(target)
    for i in range(size_n - 1, -1, -1):
        lii = _pick((row == i) & (col == i), lower, None).reshape(1, 1)
        gi = _pick(row1 == i, rest, 0) / lii
        gamma = gamma + jnp.where(row1 == i, gi, 0.0)
        rest = rest - jnp.where(row1 < i, _pick(col == i, upper, 1), 0.0) * gi
    before = pltpu.roll(gamma, 1, 0)
    weights = jnp.where(row1 == 0, 1.0, 0.0) - gamma + before
    return jnp.broadcast_to(weights, prod.shape)


def _permute_square(prod, perm):
    row = lax.broadcasted_iota(jnp.int32, prod.shape, 0)
    col = lax.broadcasted_iota(jnp.int32, prod.shape, 1)
    count = len(perm)
    permcol = jnp.zeros((prod.shape[0], 1), jnp.int32)
    permrow = jnp.zeros((1, prod.shape[1]), jnp.int32)
    for i in range(count):
        permcol = jnp.where(row[:, :1] == i, perm[i], permcol)
        permrow = jnp.where(col[:1, :] == i, perm[i], permrow)
    by_rows = jnp.zeros_like(prod)
    for m in range(count):
        by_rows = by_rows + jnp.where(permcol == m, _pick(row == m, prod, 0), 0.0)
    by_rows = jnp.where(row < count, by_rows, 0.0)
    both = jnp.zeros_like(prod)
    for m in range(count):
        both = both + jnp.where(permrow == m, _pick(col == m, by_rows, 1), 0.0)
    return jnp.where(col < count, both, 0.0)


def _allreduce_weights_kernel(nk, ne, entries, slot_ref, p_ref, w_ref, recv1, recv2, acc1, ss1, rs1, ss2, rs2):
    mk = lax.axis_index("kgrp")
    me = lax.axis_index("energy")
    barrier = pltpu.get_barrier_semaphore()
    for s in range(nk - 1):
        pl.semaphore_signal(barrier, 1, device_id=((mk + s + 1) % nk, me), device_id_type=MESH)
    for s in range(ne - 1):
        pl.semaphore_signal(barrier, 1, device_id=(mk, (me + s + 1) % ne), device_id_type=MESH)
    pl.semaphore_wait(barrier, nk - 1 + ne - 1)

    def exchange(src, recv, ssem, rsem, count, peer):
        copies = []
        for s in range(count - 1):
            c = pltpu.make_async_remote_copy(
                src_ref=src,
                dst_ref=recv.at[count - 2 - s],
                send_sem=ssem.at[s],
                recv_sem=rsem.at[count - 2 - s],
                device_id=peer(s),
                device_id_type=MESH,
            )
            c.start()
            copies.append(c)
        for s in range(count - 1):
            copies[s].wait_recv()
        for s in range(count - 1):
            copies[s].wait_send()

    def total(own, recv, mine, count):
        acc = jnp.zeros_like(own)
        for idx in range(count):
            slot = jnp.minimum((idx - mine - 1 + count) % count, count - 2)
            acc = acc + jnp.where(idx == mine, own, recv[slot])
        return acc

    exchange(p_ref, recv1, ss1, rs1, nk, lambda s: ((mk + s + 1) % nk, me))
    acc1[...] = total(p_ref[...], recv1, mk, nk)
    exchange(acc1, recv2, ss2, rs2, ne, lambda s: (mk, (me + s + 1) % ne))
    summed = total(acc1[...], recv2, me, ne)
    perm = [0] + [slot_ref[i] + 1 for i in range(HIST)]
    aged = _permute_square(summed / entries, perm)
    weights = _weights_from_products(aged)[:, :1]
    row1 = lax.broadcasted_iota(jnp.int32, weights.shape, 0)
    by_slot = jnp.zeros_like(weights)
    for i in range(HIST + 1):
        by_slot = by_slot + jnp.where(row1 == perm[i], _pick(row1 == i, weights, 0), 0.0)
    w_ref[...] = jnp.broadcast_to(by_slot, w_ref.shape)


def _transpose_kernel(ne, x_ref, y_ref, ssem, rsem):
    mk = lax.axis_index("kgrp")
    me = lax.axis_index("energy")
    width = x_ref.shape[-1]
    barrier = pltpu.get_barrier_semaphore()
    for s in range(ne - 1):
        pl.semaphore_signal(barrier, 1, device_id=(mk, (me + s + 1) % ne), device_id_type=MESH)
    pl.semaphore_wait(barrier, ne - 1)
    copies = []
    for s in range(ne - 1):
        peer = (me + s + 1) % ne
        c = pltpu.make_async_remote_copy(
            src_ref=x_ref.at[peer],
            dst_ref=y_ref.at[:, pl.ds(pl.multiple_of(me * width, width), width)],
            send_sem=ssem.at[s],
            recv_sem=rsem.at[ne - 2 - s],
            device_id=(mk, peer),
            device_id_type=MESH,
        )
        c.start()
        copies.append(c)
    y_ref[:, pl.ds(pl.multiple_of(me * width, width), width)] = x_ref[me]
    for q in range(ne - 1):
        source = (me + q + 1) % ne
        pltpu.make_async_remote_copy(
            src_ref=x_ref.at[me],
            dst_ref=y_ref.at[:, pl.ds(pl.multiple_of(source * width, width), width)],
            send_sem=ssem.at[q],
            recv_sem=rsem.at[q],
            device_id=(mk, source),
            device_id_type=MESH,
        ).wait_recv()
    for s in range(ne - 1):
        copies[s].wait_send()


def energy_transpose(chunks, ne):
    rows, width = chunks.shape[1:]
    return pl.pallas_call(
        functools.partial(_transpose_kernel, ne),
        out_shape=jax.ShapeDtypeStruct((rows, ne * width), jnp.float32),
        in_specs=[pl.BlockSpec(memory_space=pltpu.VMEM)],
        out_specs=pl.BlockSpec(memory_space=pltpu.VMEM),
        scratch_shapes=[
            pltpu.SemaphoreType.DMA((ne - 1,)),
            pltpu.SemaphoreType.DMA((ne - 1,)),
        ],
        compiler_params=pltpu.CompilerParams(collective_id=1, has_side_effects=True),
    )(chunks)


def allreduce_weights(slot_order, prod_tile, nk, ne, entries):
    return pl.pallas_call(
        functools.partial(_allreduce_weights_kernel, nk, ne, entries),
        out_shape=jax.ShapeDtypeStruct(prod_tile.shape, jnp.float32),
        in_specs=[
            pl.BlockSpec(memory_space=pltpu.SMEM),
            pl.BlockSpec(memory_space=pltpu.VMEM),
        ],
        out_specs=pl.BlockSpec(memory_space=pltpu.VMEM),
        scratch_shapes=[
            pltpu.VMEM((nk - 1,) + prod_tile.shape, jnp.float32),
            pltpu.VMEM((ne - 1,) + prod_tile.shape, jnp.float32),
            pltpu.VMEM(prod_tile.shape, jnp.float32),
            pltpu.SemaphoreType.DMA((nk - 1,)),
            pltpu.SemaphoreType.DMA((nk - 1,)),
            pltpu.SemaphoreType.DMA((ne - 1,)),
            pltpu.SemaphoreType.DMA((ne - 1,)),
        ],
        compiler_params=pltpu.CompilerParams(collective_id=0, has_side_effects=True),
    )(slot_order, prod_tile)


def per_device(
    greens,
    current,
    past_inputs,
    past_residuals,
    slot_order,
    neighbour,
    momentum_class,
    stencil_weight,
    acoustic_coupling,
    optical_coupling,
    occupation,
    phonon_shift,
):
    group_len = greens.shape[3]
    rows_here = current.shape[3]
    group_id = lax.axis_index("kgrp")
    energy_id = lax.axis_index("energy")
    nk = lax.axis_size("kgrp")
    ne = lax.axis_size("energy")
    total_k = group_len * nk
    ends = padded_2(greens, (("kgrp", 3),), group_len, True)
    low = ends[:, :, :, :group_len]
    high = ends[:, :, :, 2 * group_len :]
    local_index = (neighbour - group_id * group_len + group_len) % total_k
    stencil = jnp.sum(
        jnp.where(
            local_index[:, :, None] == jnp.arange(3 * group_len, dtype=jnp.int32)[None, None, :],
            stencil_weight[None, :, None],
            0.0,
        ),
        axis=1,
    )
    lead = greens.shape[:3]
    flat = lambda x: x.reshape((-1,) + x.shape[3:])
    stencil = stencil.reshape(ne, rows_here, 3 * group_len)
    chunks = jnp.zeros((ne, flat(greens).shape[0], rows_here, greens.shape[4]), jnp.float32)
    for part, block in enumerate((low, greens, high)):
        chunks = chunks + jnp.einsum(
            "dkr,bre->dbke",
            stencil[:, :, part * group_len : (part + 1) * group_len],
            flat(block),
            precision=lax.Precision.HIGHEST,
        )
    chunks = chunks.reshape(ne, -1, greens.shape[4])
    rows = energy_transpose(chunks, ne).reshape(lead + (rows_here, -1))
    classes = acoustic_coupling.shape[0]
    my_class = lax.dynamic_slice_in_dim(momentum_class, energy_id * rows_here, rows_here)
    coupling_row = jnp.sum(
        jnp.where(
            my_class[:, None] == jnp.arange(classes, dtype=jnp.int32)[None, :],
            acoustic_coupling[None, :],
            0.0,
        ),
        axis=1,
    )
    pad = [(0, 0)] * (rows.ndim - 1) + [(SHIFT_MAX, SHIFT_MAX)]
    padded = jnp.pad(rows, pad)
    sigma_new = emit(
        padded, SHIFT_MAX, rows.shape[-1], coupling_row, optical_coupling, occupation, phonon_shift
    )
    residual_now = sigma_new - current
    data_axes = tuple(range(1, past_residuals.ndim))
    old_gram = jnp.sum(past_residuals[:, None] * past_residuals[None, :], axis=tuple(a + 1 for a in data_axes))
    cross = jnp.sum(residual_now[None] * past_residuals, axis=data_axes)
    self_term = jnp.sum(residual_now * residual_now)
    top = jnp.concatenate([self_term[None], cross])
    products = jnp.concatenate([top[None, :], jnp.concatenate([cross[:, None], old_gram], axis=1)], axis=0)
    prod_tile = jnp.pad(products, ((0, 8 - HIST - 1), (0, 128 - HIST - 1)))
    entries = float(residual_now.size * nk * ne)
    weights = allreduce_weights(slot_order, prod_tile, nk, ne, entries)[: HIST + 1, 0]
    mixed = weights[0] * (current + mixing_share * residual_now)
    for column in range(HIST):
        mixed = mixed + weights[column + 1] * (
            past_inputs[column] + mixing_share * past_residuals[column]
        )
    return mixed


def solution(mesh):
    return jax.shard_map(
        per_device,
        mesh=mesh,
        in_specs=(
            P(None, None, None, "kgrp", "energy"),
            P(None, None, None, ("kgrp", "energy"), None),
            P(None, None, None, None, ("kgrp", "energy"), None),
            P(None, None, None, None, ("kgrp", "energy"), None),
            P(),
            P("kgrp", None),
            P("kgrp"),
            P(),
            P(),
            P(),
            P(),
            P(),
        ),
        out_specs=P(None, None, None, ("kgrp", "energy"), None),
        check_vma=False,
    )
```

```python
import functools

import jax
import jax.numpy as jnp
from jax import lax
from jax.experimental import pallas as pl
from jax.experimental.pallas import tpu as pltpu
from jax.sharding import PartitionSpec as P

SHIFT_MAX = 96
HIST = 5

mixing_share = 0.5
ridge_share = 0.1

MESH = pl.DeviceIdType.MESH


def padded_2(block, sides, width, periodic):
    for axis, dim in sides:
        count = lax.axis_size(axis)
        forward = [(i, i + 1) for i in range(count - 1)]
        if periodic:
            forward.append((count - 1, 0))
        backward = [(target, source) for source, target in forward]
        low = lax.ppermute(
            lax.slice_in_dim(block, block.shape[dim] - width, None, axis=dim), axis, forward
        )
        high = lax.ppermute(lax.slice_in_dim(block, 0, width, axis=dim), axis, backward)
        block = jnp.concatenate([low, block, high], axis=dim)
    return block


def emit(padded, margin, length, coupling_row, optical, occupation, shifts):
    lesser = padded[0]
    greater = padded[1]

    def energy_view(source, offset):
        return lax.dynamic_slice_in_dim(source, margin + offset, length, axis=source.ndim - 1)

    sigma_less = coupling_row[:, None] * energy_view(lesser, 0)
    sigma_more = coupling_row[:, None] * energy_view(greater, 0)
    for column in range(2):
        strength = optical[column]
        number = occupation[column]
        offset = shifts[column]
        sigma_less = sigma_less + strength * (
            (number + 1.0) * energy_view(lesser, offset) + number * energy_view(lesser, -offset)
        )
        sigma_more = sigma_more + strength * (
            (number + 1.0) * energy_view(greater, -offset) + number * energy_view(greater, offset)
        )
    return jnp.stack([sigma_less, sigma_more])


def _pick(mask, x, axis):
    return jnp.sum(jnp.where(mask, x, 0.0), axis=axis, keepdims=True)


def _weights_from_products(prod):
    size_n = HIST
    row = lax.broadcasted_iota(jnp.int32, prod.shape, 0)
    col = lax.broadcasted_iota(jnp.int32, prod.shape, 1)
    rows, cols = prod.shape
    down = pltpu.roll(prod, rows - 1, 0)
    right = pltpu.roll(prod, cols - 1, 1)
    diag = pltpu.roll(down, cols - 1, 1)
    inside = (row < size_n) & (col < size_n)
    system = jnp.where(inside, prod - right - down + diag, 0.0)
    target = _pick((col == 0) & (row < size_n), prod - down, 1)
    eye = inside & (row == col)
    trace = jnp.sum(jnp.where(eye, system, 0.0), keepdims=True)
    ridge = ridge_share * trace / size_n + 1e-06
    a = system + jnp.where(eye, ridge, 0.0)
    lower = jnp.zeros_like(a)
    upper = jnp.zeros_like(a)
    for j in range(size_n):
        pivot = jnp.sqrt(_pick((row == j) & (col == j), a, None).reshape(1, 1))
        lcol = jnp.where(row[:, :1] >= j, _pick(col == j, a, 1) / pivot, 0.0)
        lrow = jnp.where(col[:1, :] >= j, _pick(row == j, a, 0) / pivot, 0.0)
        lower = lower + jnp.where(col == j, lcol, 0.0)
        upper = upper + jnp.where(row == j, lrow, 0.0)
        a = a - lcol * lrow
    row1 = row[:, :1]
    rest = target
    forward = jnp.zeros_like(target)
    for i in range(size_n):
        lii = _pick((row == i) & (col == i), lower, None).reshape(1, 1)
        yi = _pick(row1 == i, rest, 0) / lii
        forward = forward + jnp.where(row1 == i, yi, 0.0)
        rest = rest - jnp.where(row1 > i, _pick(col == i, lower, 1), 0.0) * yi
    rest = forward
    gamma = jnp.zeros_like(target)
    for i in range(size_n - 1, -1, -1):
        lii = _pick((row == i) & (col == i), lower, None).reshape(1, 1)
        gi = _pick(row1 == i, rest, 0) / lii
        gamma = gamma + jnp.where(row1 == i, gi, 0.0)
        rest = rest - jnp.where(row1 < i, _pick(col == i, upper, 1), 0.0) * gi
    before = pltpu.roll(gamma, 1, 0)
    weights = jnp.where(row1 == 0, 1.0, 0.0) - gamma + before
    return jnp.broadcast_to(weights, prod.shape)


def _permute_square(prod, perm):
    row = lax.broadcasted_iota(jnp.int32, prod.shape, 0)
    col = lax.broadcasted_iota(jnp.int32, prod.shape, 1)
    count = len(perm)
    permcol = jnp.zeros((prod.shape[0], 1), jnp.int32)
    permrow = jnp.zeros((1, prod.shape[1]), jnp.int32)
    for i in range(count):
        permcol = jnp.where(row[:, :1] == i, perm[i], permcol)
        permrow = jnp.where(col[:1, :] == i, perm[i], permrow)
    by_rows = jnp.zeros_like(prod)
    for m in range(count):
        by_rows = by_rows + jnp.where(permcol == m, _pick(row == m, prod, 0), 0.0)
    by_rows = jnp.where(row < count, by_rows, 0.0)
    both = jnp.zeros_like(prod)
    for m in range(count):
        both = both + jnp.where(permrow == m, _pick(col == m, by_rows, 1), 0.0)
    return jnp.where(col < count, both, 0.0)


def _local_products(res, hist):
    shape = (8, 128)
    row = lax.broadcasted_iota(jnp.int32, shape, 0)
    col = lax.broadcasted_iota(jnp.int32, shape, 1)
    vectors = [res] + [hist[m] for m in range(HIST)]
    prod = jnp.zeros(shape, jnp.float32)
    for i in range(HIST + 1):
        for j in range(i, HIST + 1):
            value = jnp.sum(vectors[i] * vectors[j], keepdims=True)
            spot = ((row == i) & (col == j)) | ((row == j) & (col == i))
            prod = jnp.where(spot, value, prod)
    return prod


def _mix_kernel(nk, ne, entries, slot_ref, res_ref, cur_ref, pin_ref, pres_ref, out_ref,
                send1, recv1, recv2, acc1, ss1, rs1, ss2, rs2):
    mk = lax.axis_index("kgrp")
    me = lax.axis_index("energy")
    barrier = pltpu.get_barrier_semaphore()
    for s in range(nk - 1):
        pl.semaphore_signal(barrier, 1, device_id=((mk + s + 1) % nk, me), device_id_type=MESH)
    for s in range(ne - 1):
        pl.semaphore_signal(barrier, 1, device_id=(mk, (me + s + 1) % ne), device_id_type=MESH)
    send1[...] = _local_products(res_ref[...], pres_ref)
    pl.semaphore_wait(barrier, nk - 1 + ne - 1)

    def exchange(src, recv, ssem, rsem, count, peer):
        copies = []
        for s in range(count - 1):
            c = pltpu.make_async_remote_copy(
                src_ref=src,
                dst_ref=recv.at[count - 2 - s],
                send_sem=ssem.at[s],
                recv_sem=rsem.at[count - 2 - s],
                device_id=peer(s),
                device_id_type=MESH,
            )
            c.start()
            copies.append(c)
        for s in range(count - 1):
            copies[s].wait_recv()
        for s in range(count - 1):
            copies[s].wait_send()

    def total(own, recv, mine, count):
        acc = jnp.zeros_like(own)
        for idx in range(count):
            slot = jnp.minimum((idx - mine - 1 + count) % count, count - 2)
            acc = acc + jnp.where(idx == mine, own, recv[slot])
        return acc

    exchange(send1, recv1, ss1, rs1, nk, lambda s: ((mk + s + 1) % nk, me))
    acc1[...] = total(send1[...], recv1, mk, nk)
    exchange(acc1, recv2, ss2, rs2, ne, lambda s: (mk, (me + s + 1) % ne))
    summed = total(acc1[...], recv2, me, ne)
    perm = [0] + [slot_ref[i] + 1 for i in range(HIST)]
    aged = _permute_square(summed / entries, perm)
    weights = _weights_from_products(aged)[:, :1]
    row1 = lax.broadcasted_iota(jnp.int32, weights.shape, 0)
    slot_w = [None] * (HIST + 1)
    for i in range(HIST + 1):
        w_i = _pick(row1 == i, weights, 0)
        for m in range(HIST + 1):
            term = jnp.where(perm[i] == m, w_i, 0.0)
            slot_w[m] = term if slot_w[m] is None else slot_w[m] + term
    mixed = slot_w[0] * (cur_ref[...] + mixing_share * res_ref[...])
    for m in range(HIST):
        mixed = mixed + slot_w[m + 1] * (pin_ref[m] + mixing_share * pres_ref[m])
    out_ref[...] = mixed


def mix_allreduce(slot_order, res, cur, pin, pres, nk, ne, entries):
    tile = (8, 128)
    vmem = pl.BlockSpec(memory_space=pltpu.VMEM)
    return pl.pallas_call(
        functools.partial(_mix_kernel, nk, ne, entries),
        out_shape=jax.ShapeDtypeStruct(cur.shape, jnp.float32),
        in_specs=[pl.BlockSpec(memory_space=pltpu.SMEM), vmem, vmem, vmem, vmem],
        out_specs=vmem,
        scratch_shapes=[
            pltpu.VMEM(tile, jnp.float32),
            pltpu.VMEM((nk - 1,) + tile, jnp.float32),
            pltpu.VMEM((ne - 1,) + tile, jnp.float32),
            pltpu.VMEM(tile, jnp.float32),
            pltpu.SemaphoreType.DMA((nk - 1,)),
            pltpu.SemaphoreType.DMA((nk - 1,)),
            pltpu.SemaphoreType.DMA((ne - 1,)),
            pltpu.SemaphoreType.DMA((ne - 1,)),
        ],
        compiler_params=pltpu.CompilerParams(collective_id=0, has_side_effects=True),
    )(slot_order, res, cur, pin, pres)


def _transpose_kernel(ne, x_ref, y_ref, ssem, rsem):
    mk = lax.axis_index("kgrp")
    me = lax.axis_index("energy")
    width = x_ref.shape[-1]
    barrier = pltpu.get_barrier_semaphore()
    for s in range(ne - 1):
        pl.semaphore_signal(barrier, 1, device_id=(mk, (me + s + 1) % ne), device_id_type=MESH)
    pl.semaphore_wait(barrier, ne - 1)
    copies = []
    for s in range(ne - 1):
        peer = (me + s + 1) % ne
        c = pltpu.make_async_remote_copy(
            src_ref=x_ref.at[peer],
            dst_ref=y_ref.at[:, pl.ds(pl.multiple_of(me * width, width), width)],
            send_sem=ssem.at[s],
            recv_sem=rsem.at[ne - 2 - s],
            device_id=(mk, peer),
            device_id_type=MESH,
        )
        c.start()
        copies.append(c)
    y_ref[:, pl.ds(pl.multiple_of(me * width, width), width)] = x_ref[me]
    for q in range(ne - 1):
        source = (me + q + 1) % ne
        pltpu.make_async_remote_copy(
            src_ref=x_ref.at[me],
            dst_ref=y_ref.at[:, pl.ds(pl.multiple_of(source * width, width), width)],
            send_sem=ssem.at[q],
            recv_sem=rsem.at[q],
            device_id=(mk, source),
            device_id_type=MESH,
        ).wait_recv()
    for s in range(ne - 1):
        copies[s].wait_send()


def energy_transpose(chunks, ne):
    rows, width = chunks.shape[1:]
    return pl.pallas_call(
        functools.partial(_transpose_kernel, ne),
        out_shape=jax.ShapeDtypeStruct((rows, ne * width), jnp.float32),
        in_specs=[pl.BlockSpec(memory_space=pltpu.VMEM)],
        out_specs=pl.BlockSpec(memory_space=pltpu.VMEM),
        scratch_shapes=[
            pltpu.SemaphoreType.DMA((ne - 1,)),
            pltpu.SemaphoreType.DMA((ne - 1,)),
        ],
        compiler_params=pltpu.CompilerParams(collective_id=1, has_side_effects=True),
    )(chunks)


def per_device(
    greens,
    current,
    past_inputs,
    past_residuals,
    slot_order,
    neighbour,
    momentum_class,
    stencil_weight,
    acoustic_coupling,
    optical_coupling,
    occupation,
    phonon_shift,
):
    group_len = greens.shape[3]
    rows_here = current.shape[3]
    group_id = lax.axis_index("kgrp")
    energy_id = lax.axis_index("energy")
    nk = lax.axis_size("kgrp")
    ne = lax.axis_size("energy")
    total_k = group_len * nk
    ends = padded_2(greens, (("kgrp", 3),), group_len, True)
    low = ends[:, :, :, :group_len]
    high = ends[:, :, :, 2 * group_len :]
    local_index = (neighbour - group_id * group_len + group_len) % total_k
    stencil = jnp.sum(
        jnp.where(
            local_index[:, :, None] == jnp.arange(3 * group_len, dtype=jnp.int32)[None, None, :],
            stencil_weight[None, :, None],
            0.0,
        ),
        axis=1,
    )
    lead = greens.shape[:3]
    flat = lambda x: x.reshape((-1,) + x.shape[3:])
    stencil = stencil.reshape(ne, rows_here, 3 * group_len)
    chunks = jnp.zeros((ne, flat(greens).shape[0], rows_here, greens.shape[4]), jnp.float32)
    for part, block in enumerate((low, greens, high)):
        chunks = chunks + jnp.einsum(
            "dkr,bre->dbke",
            stencil[:, :, part * group_len : (part + 1) * group_len],
            flat(block),
            precision=lax.Precision.HIGHEST,
        )
    chunks = chunks.reshape(ne, -1, greens.shape[4])
    rows = energy_transpose(chunks, ne).reshape(lead + (rows_here, -1))
    classes = acoustic_coupling.shape[0]
    my_class = lax.dynamic_slice_in_dim(momentum_class, energy_id * rows_here, rows_here)
    coupling_row = jnp.sum(
        jnp.where(
            my_class[:, None] == jnp.arange(classes, dtype=jnp.int32)[None, :],
            acoustic_coupling[None, :],
            0.0,
        ),
        axis=1,
    )
    pad = [(0, 0)] * (rows.ndim - 1) + [(SHIFT_MAX, SHIFT_MAX)]
    padded = jnp.pad(rows, pad)
    sigma_new = emit(
        padded, SHIFT_MAX, rows.shape[-1], coupling_row, optical_coupling, occupation, phonon_shift
    )
    residual_now = sigma_new - current
    lanes = current.shape[-1]
    entries = float(residual_now.size * nk * ne)
    mixed = mix_allreduce(
        slot_order,
        residual_now.reshape(-1, lanes),
        current.reshape(-1, lanes),
        past_inputs.reshape(HIST, -1, lanes),
        past_residuals.reshape(HIST, -1, lanes),
        nk,
        ne,
        entries,
    ).reshape(current.shape)
    return mixed


def solution(mesh):
    return jax.shard_map(
        per_device,
        mesh=mesh,
        in_specs=(
            P(None, None, None, "kgrp", "energy"),
            P(None, None, None, ("kgrp", "energy"), None),
            P(None, None, None, None, ("kgrp", "energy"), None),
            P(None, None, None, None, ("kgrp", "energy"), None),
            P(),
            P("kgrp", None),
            P("kgrp"),
            P(),
            P(),
            P(),
            P(),
            P(),
        ),
        out_specs=P(None, None, None, ("kgrp", "energy"), None),
        check_vma=False,
    )
```

```python
import functools

import jax
import jax.numpy as jnp
from jax import lax
from jax.experimental import pallas as pl
from jax.experimental.pallas import tpu as pltpu
from jax.sharding import PartitionSpec as P

SHIFT_MAX = 96
HIST = 5

mixing_share = 0.5
ridge_share = 0.1

MESH = pl.DeviceIdType.MESH


def padded_2(block, sides, width, periodic):
    for axis, dim in sides:
        count = lax.axis_size(axis)
        forward = [(i, i + 1) for i in range(count - 1)]
        if periodic:
            forward.append((count - 1, 0))
        backward = [(target, source) for source, target in forward]
        low = lax.ppermute(
            lax.slice_in_dim(block, block.shape[dim] - width, None, axis=dim), axis, forward
        )
        high = lax.ppermute(lax.slice_in_dim(block, 0, width, axis=dim), axis, backward)
        block = jnp.concatenate([low, block, high], axis=dim)
    return block


def emit(padded, margin, length, coupling_row, optical, occupation, shifts):
    lesser = padded[0]
    greater = padded[1]

    def energy_view(source, offset):
        return lax.dynamic_slice_in_dim(source, margin + offset, length, axis=source.ndim - 1)

    sigma_less = coupling_row[:, None] * energy_view(lesser, 0)
    sigma_more = coupling_row[:, None] * energy_view(greater, 0)
    for column in range(2):
        strength = optical[column]
        number = occupation[column]
        offset = shifts[column]
        sigma_less = sigma_less + strength * (
            (number + 1.0) * energy_view(lesser, offset) + number * energy_view(lesser, -offset)
        )
        sigma_more = sigma_more + strength * (
            (number + 1.0) * energy_view(greater, -offset) + number * energy_view(greater, offset)
        )
    return jnp.stack([sigma_less, sigma_more])


def _pick(mask, x, axis):
    return jnp.sum(jnp.where(mask, x, 0.0), axis=axis, keepdims=True)


def _weights_from_products(prod):
    size_n = HIST
    row = lax.broadcasted_iota(jnp.int32, prod.shape, 0)
    col = lax.broadcasted_iota(jnp.int32, prod.shape, 1)
    rows, cols = prod.shape
    down = pltpu.roll(prod, rows - 1, 0)
    right = pltpu.roll(prod, cols - 1, 1)
    diag = pltpu.roll(down, cols - 1, 1)
    inside = (row < size_n) & (col < size_n)
    system = jnp.where(inside, prod - right - down + diag, 0.0)
    target = _pick((col == 0) & (row < size_n), prod - down, 1)
    eye = inside & (row == col)
    trace = jnp.sum(jnp.where(eye, system, 0.0), keepdims=True)
    ridge = ridge_share * trace / size_n + 1e-06
    a = system + jnp.where(eye, ridge, 0.0)
    lower = jnp.zeros_like(a)
    upper = jnp.zeros_like(a)
    for j in range(size_n):
        pivot = jnp.sqrt(_pick((row == j) & (col == j), a, None).reshape(1, 1))
        lcol = jnp.where(row[:, :1] >= j, _pick(col == j, a, 1) / pivot, 0.0)
        lrow = jnp.where(col[:1, :] >= j, _pick(row == j, a, 0) / pivot, 0.0)
        lower = lower + jnp.where(col == j, lcol, 0.0)
        upper = upper + jnp.where(row == j, lrow, 0.0)
        a = a - lcol * lrow
    row1 = row[:, :1]
    rest = target
    forward = jnp.zeros_like(target)
    for i in range(size_n):
        lii = _pick((row == i) & (col == i), lower, None).reshape(1, 1)
        yi = _pick(row1 == i, rest, 0) / lii
        forward = forward + jnp.where(row1 == i, yi, 0.0)
        rest = rest - jnp.where(row1 > i, _pick(col == i, lower, 1), 0.0) * yi
    rest = forward
    gamma = jnp.zeros_like(target)
    for i in range(size_n - 1, -1, -1):
        lii = _pick((row == i) & (col == i), lower, None).reshape(1, 1)
        gi = _pick(row1 == i, rest, 0) / lii
        gamma = gamma + jnp.where(row1 == i, gi, 0.0)
        rest = rest - jnp.where(row1 < i, _pick(col == i, upper, 1), 0.0) * gi
    before = pltpu.roll(gamma, 1, 0)
    weights = jnp.where(row1 == 0, 1.0, 0.0) - gamma + before
    return jnp.broadcast_to(weights, prod.shape)


def _permute_square(prod, perm):
    row = lax.broadcasted_iota(jnp.int32, prod.shape, 0)
    col = lax.broadcasted_iota(jnp.int32, prod.shape, 1)
    count = len(perm)
    permcol = jnp.zeros((prod.shape[0], 1), jnp.int32)
    permrow = jnp.zeros((1, prod.shape[1]), jnp.int32)
    for i in range(count):
        permcol = jnp.where(row[:, :1] == i, perm[i], permcol)
        permrow = jnp.where(col[:1, :] == i, perm[i], permrow)
    by_rows = jnp.zeros_like(prod)
    for m in range(count):
        by_rows = by_rows + jnp.where(permcol == m, _pick(row == m, prod, 0), 0.0)
    by_rows = jnp.where(row < count, by_rows, 0.0)
    both = jnp.zeros_like(prod)
    for m in range(count):
        both = both + jnp.where(permrow == m, _pick(col == m, by_rows, 1), 0.0)
    return jnp.where(col < count, both, 0.0)


def _pair_sums(vectors, pairs):
    shape = (8, 128)
    row = lax.broadcasted_iota(jnp.int32, shape, 0)
    col = lax.broadcasted_iota(jnp.int32, shape, 1)
    prod = jnp.zeros(shape, jnp.float32)
    for i, j in pairs:
        value = jnp.sum(vectors[i] * vectors[j], keepdims=True)
        spot = ((row == i) & (col == j)) | ((row == j) & (col == i))
        prod = jnp.where(spot, value, prod)
    return prod


def _fused_kernel(nk, ne, entries, margin,
                  slot_ref, shift_ref, class_ref, optical_ref, occ_ref, acoustic_ref,
                  chunk_ref, cur_ref, pin_ref, pres_ref, out_ref,
                  ypad, send1, recv1, recv2, acc1, ts, tr, ss1, rs1, ss2, rs2):
    mk = lax.axis_index("kgrp")
    me = lax.axis_index("energy")
    width = chunk_ref.shape[-1]
    rows, padded_len = ypad.shape
    length = padded_len - 2 * margin
    barrier = pltpu.get_barrier_semaphore()
    for s in range(nk - 1):
        pl.semaphore_signal(barrier, 1, device_id=((mk + s + 1) % nk, me), device_id_type=MESH)
    for s in range(ne - 1):
        pl.semaphore_signal(barrier, 1, device_id=(mk, (me + s + 1) % ne), device_id_type=MESH)
    ypad[:, :margin] = jnp.zeros((rows, margin), jnp.float32)
    ypad[:, margin + length :] = jnp.zeros((rows, margin), jnp.float32)
    ypad[:, pl.ds(pl.multiple_of(margin + me * width, width), width)] = chunk_ref[me]
    pl.semaphore_wait(barrier, nk - 1 + ne - 1)

    copies = []
    for s in range(ne - 1):
        peer = (me + s + 1) % ne
        c = pltpu.make_async_remote_copy(
            src_ref=chunk_ref.at[peer],
            dst_ref=ypad.at[:, pl.ds(pl.multiple_of(margin + me * width, width), width)],
            send_sem=ts.at[s],
            recv_sem=tr.at[ne - 2 - s],
            device_id=(mk, peer),
            device_id_type=MESH,
        )
        c.start()
        copies.append(c)
    history = [pres_ref[m] for m in range(HIST)]
    gram = _pair_sums([None] + history, [(i, j) for i in range(1, HIST + 1) for j in range(i, HIST + 1)])
    for q in range(ne - 1):
        source = (me + q + 1) % ne
        pltpu.make_async_remote_copy(
            src_ref=chunk_ref.at[me],
            dst_ref=ypad.at[:, pl.ds(pl.multiple_of(margin + source * width, width), width)],
            send_sem=ts.at[q],
            recv_sem=tr.at[q],
            device_id=(mk, source),
            device_id_type=MESH,
        ).wait_recv()
    for s in range(ne - 1):
        copies[s].wait_send()

    y = ypad[...]
    row = lax.broadcasted_iota(jnp.int32, (rows, 1), 0)
    lesser = row < rows // 2
    per_row = rows // 8
    coupling = jnp.zeros((rows, 1), jnp.float32)
    for r in range(per_row):
        coupling = jnp.where(row % per_row == r, acoustic_ref[class_ref[me * per_row + r]], coupling)
    sigma = coupling * y[:, margin : margin + length]
    for m in range(2):
        shift = shift_ref[m]
        strength = optical_ref[m]
        number = occ_ref[m]
        ahead = pltpu.roll(y, padded_len - shift, 1)[:, margin : margin + length]
        behind = pltpu.roll(y, shift, 1)[:, margin : margin + length]
        up = jnp.where(lesser, number + 1.0, number)
        down = jnp.where(lesser, number, number + 1.0)
        sigma = sigma + strength * (up * ahead + down * behind)
    res = sigma - cur_ref[...]
    fresh = _pair_sums([res] + history, [(0, j) for j in range(HIST + 1)])
    send1[...] = fresh + gram

    def exchange(src, recv, ssem, rsem, count, peer):
        out = []
        for s in range(count - 1):
            c = pltpu.make_async_remote_copy(
                src_ref=src,
                dst_ref=recv.at[count - 2 - s],
                send_sem=ssem.at[s],
                recv_sem=rsem.at[count - 2 - s],
                device_id=peer(s),
                device_id_type=MESH,
            )
            c.start()
            out.append(c)
        for s in range(count - 1):
            out[s].wait_recv()
        for s in range(count - 1):
            out[s].wait_send()

    def total(own, recv, mine, count):
        acc = jnp.zeros_like(own)
        for idx in range(count):
            slot = jnp.minimum((idx - mine - 1 + count) % count, count - 2)
            acc = acc + jnp.where(idx == mine, own, recv[slot])
        return acc

    exchange(send1, recv1, ss1, rs1, nk, lambda s: ((mk + s + 1) % nk, me))
    acc1[...] = total(send1[...], recv1, mk, nk)
    exchange(acc1, recv2, ss2, rs2, ne, lambda s: (mk, (me + s + 1) % ne))
    summed = total(acc1[...], recv2, me, ne)
    perm = [0] + [slot_ref[i] + 1 for i in range(HIST)]
    aged = _permute_square(summed / entries, perm)
    weights = _weights_from_products(aged)[:, :1]
    row1 = lax.broadcasted_iota(jnp.int32, weights.shape, 0)
    slot_w = [None] * (HIST + 1)
    for i in range(HIST + 1):
        w_i = _pick(row1 == i, weights, 0)
        for m in range(HIST + 1):
            term = jnp.where(perm[i] == m, w_i, 0.0)
            slot_w[m] = term if slot_w[m] is None else slot_w[m] + term
    mixed = slot_w[0] * (cur_ref[...] + mixing_share * res)
    for m in range(HIST):
        mixed = mixed + slot_w[m + 1] * (pin_ref[m] + mixing_share * pres_ref[m])
    out_ref[...] = mixed


def fused_tail(scalars, chunks, cur, pin, pres, nk, ne, entries):
    tile = (8, 128)
    margin = 128
    rows = chunks.shape[1]
    smem = pl.BlockSpec(memory_space=pltpu.SMEM)
    vmem = pl.BlockSpec(memory_space=pltpu.VMEM)
    return pl.pallas_call(
        functools.partial(_fused_kernel, nk, ne, entries, margin),
        out_shape=jax.ShapeDtypeStruct(cur.shape, jnp.float32),
        in_specs=[smem] * len(scalars) + [vmem] * 4,
        out_specs=vmem,
        scratch_shapes=[
            pltpu.VMEM((rows, cur.shape[1] + 2 * margin), jnp.float32),
            pltpu.VMEM(tile, jnp.float32),
            pltpu.VMEM((nk - 1,) + tile, jnp.float32),
            pltpu.VMEM((ne - 1,) + tile, jnp.float32),
            pltpu.VMEM(tile, jnp.float32),
            pltpu.SemaphoreType.DMA((ne - 1,)),
            pltpu.SemaphoreType.DMA((ne - 1,)),
            pltpu.SemaphoreType.DMA((nk - 1,)),
            pltpu.SemaphoreType.DMA((nk - 1,)),
            pltpu.SemaphoreType.DMA((ne - 1,)),
            pltpu.SemaphoreType.DMA((ne - 1,)),
        ],
        compiler_params=pltpu.CompilerParams(collective_id=0, has_side_effects=True),
    )(*scalars, chunks, cur, pin, pres)


def per_device(
    greens,
    current,
    past_inputs,
    past_residuals,
    slot_order,
    neighbour,
    momentum_class,
    stencil_weight,
    acoustic_coupling,
    optical_coupling,
    occupation,
    phonon_shift,
):
    group_len = greens.shape[3]
    rows_here = current.shape[3]
    group_id = lax.axis_index("kgrp")
    energy_id = lax.axis_index("energy")
    nk = lax.axis_size("kgrp")
    ne = lax.axis_size("energy")
    total_k = group_len * nk
    ends = padded_2(greens, (("kgrp", 3),), group_len, True)
    low = ends[:, :, :, :group_len]
    high = ends[:, :, :, 2 * group_len :]
    local_index = (neighbour - group_id * group_len + group_len) % total_k
    stencil = jnp.sum(
        jnp.where(
            local_index[:, :, None] == jnp.arange(3 * group_len, dtype=jnp.int32)[None, None, :],
            stencil_weight[None, :, None],
            0.0,
        ),
        axis=1,
    )
    lead = greens.shape[:3]
    flat = lambda x: x.reshape((-1,) + x.shape[3:])
    stencil = stencil.reshape(ne, rows_here, 3 * group_len)
    chunks = jnp.zeros((ne, flat(greens).shape[0], rows_here, greens.shape[4]), jnp.float32)
    for part, block in enumerate((low, greens, high)):
        chunks = chunks + jnp.einsum(
            "dkr,bre->dbke",
            stencil[:, :, part * group_len : (part + 1) * group_len],
            flat(block),
            precision=lax.Precision.HIGHEST,
        )
    chunks = chunks.reshape(ne, -1, greens.shape[4])
    lanes = current.shape[-1]
    entries = float(current.size * nk * ne)
    scalars = (slot_order, phonon_shift, momentum_class, optical_coupling, occupation, acoustic_coupling)
    mixed = fused_tail(
        scalars,
        chunks,
        current.reshape(-1, lanes),
        past_inputs.reshape(HIST, -1, lanes),
        past_residuals.reshape(HIST, -1, lanes),
        nk,
        ne,
        entries,
    ).reshape(current.shape)
    return mixed


def solution(mesh):
    return jax.shard_map(
        per_device,
        mesh=mesh,
        in_specs=(
            P(None, None, None, "kgrp", "energy"),
            P(None, None, None, ("kgrp", "energy"), None),
            P(None, None, None, None, ("kgrp", "energy"), None),
            P(None, None, None, None, ("kgrp", "energy"), None),
            P(),
            P("kgrp", None),
            P("kgrp"),
            P(),
            P(),
            P(),
            P(),
            P(),
        ),
        out_specs=P(None, None, None, ("kgrp", "energy"), None),
        check_vma=False,
    )
```

```python
import functools

import jax
import jax.numpy as jnp
from jax import lax
from jax.experimental import pallas as pl
from jax.experimental.pallas import tpu as pltpu
from jax.sharding import PartitionSpec as P

SHIFT_MAX = 96
HIST = 5

mixing_share = 0.5
ridge_share = 0.1

MESH = pl.DeviceIdType.MESH


def padded_2(block, sides, width, periodic):
    for axis, dim in sides:
        count = lax.axis_size(axis)
        forward = [(i, i + 1) for i in range(count - 1)]
        if periodic:
            forward.append((count - 1, 0))
        backward = [(target, source) for source, target in forward]
        low = lax.ppermute(
            lax.slice_in_dim(block, block.shape[dim] - width, None, axis=dim), axis, forward
        )
        high = lax.ppermute(lax.slice_in_dim(block, 0, width, axis=dim), axis, backward)
        block = jnp.concatenate([low, block, high], axis=dim)
    return block


def emit(padded, margin, length, coupling_row, optical, occupation, shifts):
    lesser = padded[0]
    greater = padded[1]

    def energy_view(source, offset):
        return lax.dynamic_slice_in_dim(source, margin + offset, length, axis=source.ndim - 1)

    sigma_less = coupling_row[:, None] * energy_view(lesser, 0)
    sigma_more = coupling_row[:, None] * energy_view(greater, 0)
    for column in range(2):
        strength = optical[column]
        number = occupation[column]
        offset = shifts[column]
        sigma_less = sigma_less + strength * (
            (number + 1.0) * energy_view(lesser, offset) + number * energy_view(lesser, -offset)
        )
        sigma_more = sigma_more + strength * (
            (number + 1.0) * energy_view(greater, -offset) + number * energy_view(greater, offset)
        )
    return jnp.stack([sigma_less, sigma_more])


def _pick(mask, x, axis):
    return jnp.sum(jnp.where(mask, x, 0.0), axis=axis, keepdims=True)


def _weights_from_products(prod):
    size_n = HIST
    row = lax.broadcasted_iota(jnp.int32, prod.shape, 0)
    col = lax.broadcasted_iota(jnp.int32, prod.shape, 1)
    rows, cols = prod.shape
    down = pltpu.roll(prod, rows - 1, 0)
    right = pltpu.roll(prod, cols - 1, 1)
    diag = pltpu.roll(down, cols - 1, 1)
    inside = (row < size_n) & (col < size_n)
    system = jnp.where(inside, prod - right - down + diag, 0.0)
    target = _pick((col == 0) & (row < size_n), prod - down, 1)
    eye = inside & (row == col)
    trace = jnp.sum(jnp.where(eye, system, 0.0), keepdims=True)
    ridge = ridge_share * trace / size_n + 1e-06
    a = system + jnp.where(eye, ridge, 0.0)
    lower = jnp.zeros_like(a)
    upper = jnp.zeros_like(a)
    for j in range(size_n):
        pivot = jnp.sqrt(_pick((row == j) & (col == j), a, None).reshape(1, 1))
        lcol = jnp.where(row[:, :1] >= j, _pick(col == j, a, 1) / pivot, 0.0)
        lrow = jnp.where(col[:1, :] >= j, _pick(row == j, a, 0) / pivot, 0.0)
        lower = lower + jnp.where(col == j, lcol, 0.0)
        upper = upper + jnp.where(row == j, lrow, 0.0)
        a = a - lcol * lrow
    row1 = row[:, :1]
    rest = target
    forward = jnp.zeros_like(target)
    for i in range(size_n):
        lii = _pick((row == i) & (col == i), lower, None).reshape(1, 1)
        yi = _pick(row1 == i, rest, 0) / lii
        forward = forward + jnp.where(row1 == i, yi, 0.0)
        rest = rest - jnp.where(row1 > i, _pick(col == i, lower, 1), 0.0) * yi
    rest = forward
    gamma = jnp.zeros_like(target)
    for i in range(size_n - 1, -1, -1):
        lii = _pick((row == i) & (col == i), lower, None).reshape(1, 1)
        gi = _pick(row1 == i, rest, 0) / lii
        gamma = gamma + jnp.where(row1 == i, gi, 0.0)
        rest = rest - jnp.where(row1 < i, _pick(col == i, upper, 1), 0.0) * gi
    before = pltpu.roll(gamma, 1, 0)
    weights = jnp.where(row1 == 0, 1.0, 0.0) - gamma + before
    return jnp.broadcast_to(weights, prod.shape)


def _permute_square(prod, perm):
    row = lax.broadcasted_iota(jnp.int32, prod.shape, 0)
    col = lax.broadcasted_iota(jnp.int32, prod.shape, 1)
    count = len(perm)
    permcol = jnp.zeros((prod.shape[0], 1), jnp.int32)
    permrow = jnp.zeros((1, prod.shape[1]), jnp.int32)
    for i in range(count):
        permcol = jnp.where(row[:, :1] == i, perm[i], permcol)
        permrow = jnp.where(col[:1, :] == i, perm[i], permrow)
    by_rows = jnp.zeros_like(prod)
    for m in range(count):
        by_rows = by_rows + jnp.where(permcol == m, _pick(row == m, prod, 0), 0.0)
    by_rows = jnp.where(row < count, by_rows, 0.0)
    both = jnp.zeros_like(prod)
    for m in range(count):
        both = both + jnp.where(permrow == m, _pick(col == m, by_rows, 1), 0.0)
    return jnp.where(col < count, both, 0.0)


def _pair_sums(vectors, pairs):
    shape = (8, 128)
    row = lax.broadcasted_iota(jnp.int32, shape, 0)
    col = lax.broadcasted_iota(jnp.int32, shape, 1)
    prod = jnp.zeros(shape, jnp.float32)
    for i, j in pairs:
        value = jnp.sum(vectors[i] * vectors[j]).reshape(1, 1)
        spot = ((row == i) & (col == j)) | ((row == j) & (col == i))
        prod = jnp.where(spot, value, prod)
    return prod


def _fused_kernel(nk, ne, entries, margin,
                  slot_ref, shift_ref, class_ref, optical_ref, occ_ref, acoustic_ref,
                  chunk_ref, cur_ref, pin_ref, pres_ref, out_ref,
                  ypad, send1, recv1, recv2, acc1, ts, tr, ss1, rs1, ss2, rs2):
    mk = lax.axis_index("kgrp")
    me = lax.axis_index("energy")
    width = chunk_ref.shape[-1]
    lead, per_row, padded_len = ypad.shape
    length = padded_len - 2 * margin
    barrier = pltpu.get_barrier_semaphore()
    for s in range(nk - 1):
        pl.semaphore_signal(barrier, 1, device_id=((mk + s + 1) % nk, me), device_id_type=MESH)
    for s in range(ne - 1):
        pl.semaphore_signal(barrier, 1, device_id=(mk, (me + s + 1) % ne), device_id_type=MESH)
    ypad[:, :, :margin] = jnp.zeros((lead, per_row, margin), jnp.float32)
    ypad[:, :, margin + length :] = jnp.zeros((lead, per_row, margin), jnp.float32)
    ypad[:, :, pl.ds(pl.multiple_of(margin + me * width, width), width)] = chunk_ref[me]
    pl.semaphore_wait(barrier, nk - 1 + ne - 1)

    copies = []
    for s in range(ne - 1):
        peer = (me + s + 1) % ne
        c = pltpu.make_async_remote_copy(
            src_ref=chunk_ref.at[peer],
            dst_ref=ypad.at[:, :, pl.ds(pl.multiple_of(margin + me * width, width), width)],
            send_sem=ts.at[s],
            recv_sem=tr.at[ne - 2 - s],
            device_id=(mk, peer),
            device_id_type=MESH,
        )
        c.start()
        copies.append(c)
    history = [pres_ref[m * lead : (m + 1) * lead] for m in range(HIST)]
    gram = _pair_sums([None] + history, [(i, j) for i in range(1, HIST + 1) for j in range(i, HIST + 1)])
    for q in range(ne - 1):
        source = (me + q + 1) % ne
        pltpu.make_async_remote_copy(
            src_ref=chunk_ref.at[me],
            dst_ref=ypad.at[:, :, pl.ds(pl.multiple_of(margin + source * width, width), width)],
            send_sem=ts.at[q],
            recv_sem=tr.at[q],
            device_id=(mk, source),
            device_id_type=MESH,
        ).wait_recv()
    for s in range(ne - 1):
        copies[s].wait_send()

    y = ypad[...]
    lesser = lax.broadcasted_iota(jnp.int32, (lead, 1, 1), 0) < lead // 2
    row = lax.broadcasted_iota(jnp.int32, (1, per_row, 1), 1)
    coupling = jnp.zeros((1, per_row, 1), jnp.float32)
    for r in range(per_row):
        coupling = jnp.where(row == r, acoustic_ref[class_ref[me * per_row + r]], coupling)
    sigma = coupling * y[:, :, margin : margin + length]
    for m in range(2):
        shift = shift_ref[m]
        strength = optical_ref[m]
        number = occ_ref[m]
        ahead = pltpu.roll(y, padded_len - shift, 2)[:, :, margin : margin + length]
        behind = pltpu.roll(y, shift, 2)[:, :, margin : margin + length]
        up = jnp.where(lesser, number + 1.0, number)
        down = jnp.where(lesser, number, number + 1.0)
        sigma = sigma + strength * (up * ahead + down * behind)
    res = sigma - cur_ref[...]
    fresh = _pair_sums([res] + history, [(0, j) for j in range(HIST + 1)])
    send1[...] = fresh + gram

    def exchange(src, recv, ssem, rsem, count, peer):
        out = []
        for s in range(count - 1):
            c = pltpu.make_async_remote_copy(
                src_ref=src,
                dst_ref=recv.at[count - 2 - s],
                send_sem=ssem.at[s],
                recv_sem=rsem.at[count - 2 - s],
                device_id=peer(s),
                device_id_type=MESH,
            )
            c.start()
            out.append(c)
        for s in range(count - 1):
            out[s].wait_recv()
        for s in range(count - 1):
            out[s].wait_send()

    def total(own, recv, mine, count):
        acc = jnp.zeros_like(own)
        for idx in range(count):
            slot = jnp.minimum((idx - mine - 1 + count) % count, count - 2)
            acc = acc + jnp.where(idx == mine, own, recv[slot])
        return acc

    exchange(send1, recv1, ss1, rs1, nk, lambda s: ((mk + s + 1) % nk, me))
    acc1[...] = total(send1[...], recv1, mk, nk)
    exchange(acc1, recv2, ss2, rs2, ne, lambda s: (mk, (me + s + 1) % ne))
    summed = total(acc1[...], recv2, me, ne)
    perm = [0] + [slot_ref[i] + 1 for i in range(HIST)]
    aged = _permute_square(summed / entries, perm)
    weights = _weights_from_products(aged)[:, :1]
    row1 = lax.broadcasted_iota(jnp.int32, weights.shape, 0)
    slot_w = [None] * (HIST + 1)
    row1 = lax.broadcasted_iota(jnp.int32, weights.shape, 0)
    for i in range(HIST + 1):
        w_i = _pick(row1 == i, weights, 0)
        for m in range(HIST + 1):
            term = jnp.where(perm[i] == m, w_i, 0.0)
            slot_w[m] = term if slot_w[m] is None else slot_w[m] + term
    slot_w = [w.reshape(1, 1, 1) for w in slot_w]
    mixed = slot_w[0] * (cur_ref[...] + mixing_share * res)
    for m in range(HIST):
        mixed = mixed + slot_w[m + 1] * (
            pin_ref[m * lead : (m + 1) * lead] + mixing_share * history[m]
        )
    out_ref[...] = mixed


def fused_tail(scalars, chunks, cur, pin, pres, nk, ne, entries):
    tile = (8, 128)
    margin = 128
    lead, per_row = chunks.shape[1:3]
    smem = pl.BlockSpec(memory_space=pltpu.SMEM)
    vmem = pl.BlockSpec(memory_space=pltpu.VMEM)
    return pl.pallas_call(
        functools.partial(_fused_kernel, nk, ne, entries, margin),
        out_shape=jax.ShapeDtypeStruct(cur.shape, jnp.float32),
        in_specs=[smem] * len(scalars) + [vmem] * 4,
        out_specs=vmem,
        scratch_shapes=[
            pltpu.VMEM((lead, per_row, cur.shape[-1] + 2 * margin), jnp.float32),
            pltpu.VMEM(tile, jnp.float32),
            pltpu.VMEM((nk - 1,) + tile, jnp.float32),
            pltpu.VMEM((ne - 1,) + tile, jnp.float32),
            pltpu.VMEM(tile, jnp.float32),
            pltpu.SemaphoreType.DMA((ne - 1,)),
            pltpu.SemaphoreType.DMA((ne - 1,)),
            pltpu.SemaphoreType.DMA((nk - 1,)),
            pltpu.SemaphoreType.DMA((nk - 1,)),
            pltpu.SemaphoreType.DMA((ne - 1,)),
            pltpu.SemaphoreType.DMA((ne - 1,)),
        ],
        compiler_params=pltpu.CompilerParams(collective_id=0, has_side_effects=True),
    )(*scalars, chunks, cur, pin, pres)


def per_device(
    greens,
    current,
    past_inputs,
    past_residuals,
    slot_order,
    neighbour,
    momentum_class,
    stencil_weight,
    acoustic_coupling,
    optical_coupling,
    occupation,
    phonon_shift,
):
    group_len = greens.shape[3]
    rows_here = current.shape[3]
    group_id = lax.axis_index("kgrp")
    energy_id = lax.axis_index("energy")
    nk = lax.axis_size("kgrp")
    ne = lax.axis_size("energy")
    total_k = group_len * nk
    ends = padded_2(greens, (("kgrp", 3),), group_len, True)
    low = ends[:, :, :, :group_len]
    high = ends[:, :, :, 2 * group_len :]
    local_index = (neighbour - group_id * group_len + group_len) % total_k
    stencil = jnp.sum(
        jnp.where(
            local_index[:, :, None] == jnp.arange(3 * group_len, dtype=jnp.int32)[None, None, :],
            stencil_weight[None, :, None],
            0.0,
        ),
        axis=1,
    )
    lead = greens.shape[:3]
    flat = lambda x: x.reshape((-1,) + x.shape[3:])
    stencil = stencil.reshape(ne, rows_here, 3 * group_len)
    chunks = jnp.zeros((ne, flat(greens).shape[0], rows_here, greens.shape[4]), jnp.float32)
    for part, block in enumerate((low, greens, high)):
        chunks = chunks + jnp.einsum(
            "dkr,bre->dbke",
            stencil[:, :, part * group_len : (part + 1) * group_len],
            flat(block),
            precision=lax.Precision.HIGHEST,
        )
    lanes = current.shape[-1]
    entries = float(current.size * nk * ne)
    scalars = (slot_order, phonon_shift, momentum_class, optical_coupling, occupation, acoustic_coupling)
    mixed = fused_tail(
        scalars,
        chunks,
        current.reshape(-1, rows_here, lanes),
        past_inputs.reshape(-1, rows_here, lanes),
        past_residuals.reshape(-1, rows_here, lanes),
        nk,
        ne,
        entries,
    ).reshape(current.shape)
    return mixed


def solution(mesh):
    return jax.shard_map(
        per_device,
        mesh=mesh,
        in_specs=(
            P(None, None, None, "kgrp", "energy"),
            P(None, None, None, ("kgrp", "energy"), None),
            P(None, None, None, None, ("kgrp", "energy"), None),
            P(None, None, None, None, ("kgrp", "energy"), None),
            P(),
            P("kgrp", None),
            P("kgrp"),
            P(),
            P(),
            P(),
            P(),
            P(),
        ),
        out_specs=P(None, None, None, ("kgrp", "energy"), None),
        check_vma=False,
    )
```

```python
import functools

import jax
import jax.numpy as jnp
from jax import lax
from jax.experimental import pallas as pl
from jax.experimental.pallas import tpu as pltpu
from jax.sharding import PartitionSpec as P

SHIFT_MAX = 96
HIST = 5

mixing_share = 0.5
ridge_share = 0.1

MESH = pl.DeviceIdType.MESH


def padded_2(block, sides, width, periodic):
    for axis, dim in sides:
        count = lax.axis_size(axis)
        forward = [(i, i + 1) for i in range(count - 1)]
        if periodic:
            forward.append((count - 1, 0))
        backward = [(target, source) for source, target in forward]
        low = lax.ppermute(
            lax.slice_in_dim(block, block.shape[dim] - width, None, axis=dim), axis, forward
        )
        high = lax.ppermute(lax.slice_in_dim(block, 0, width, axis=dim), axis, backward)
        block = jnp.concatenate([low, block, high], axis=dim)
    return block


def emit(padded, margin, length, coupling_row, optical, occupation, shifts):
    lesser = padded[0]
    greater = padded[1]

    def energy_view(source, offset):
        return lax.dynamic_slice_in_dim(source, margin + offset, length, axis=source.ndim - 1)

    sigma_less = coupling_row[:, None] * energy_view(lesser, 0)
    sigma_more = coupling_row[:, None] * energy_view(greater, 0)
    for column in range(2):
        strength = optical[column]
        number = occupation[column]
        offset = shifts[column]
        sigma_less = sigma_less + strength * (
            (number + 1.0) * energy_view(lesser, offset) + number * energy_view(lesser, -offset)
        )
        sigma_more = sigma_more + strength * (
            (number + 1.0) * energy_view(greater, -offset) + number * energy_view(greater, offset)
        )
    return jnp.stack([sigma_less, sigma_more])


def _pick(mask, x, axis):
    return jnp.sum(jnp.where(mask, x, 0.0), axis=axis, keepdims=True)


def _weights_from_products(prod):
    size_n = HIST
    row = lax.broadcasted_iota(jnp.int32, prod.shape, 0)
    col = lax.broadcasted_iota(jnp.int32, prod.shape, 1)
    rows, cols = prod.shape
    down = pltpu.roll(prod, rows - 1, 0)
    right = pltpu.roll(prod, cols - 1, 1)
    diag = pltpu.roll(down, cols - 1, 1)
    inside = (row < size_n) & (col < size_n)
    system = jnp.where(inside, prod - right - down + diag, 0.0)
    target = _pick((col == 0) & (row < size_n), prod - down, 1)
    eye = inside & (row == col)
    trace = jnp.sum(jnp.where(eye, system, 0.0), keepdims=True)
    ridge = ridge_share * trace / size_n + 1e-06
    a = system + jnp.where(eye, ridge, 0.0)
    lower = jnp.zeros_like(a)
    upper = jnp.zeros_like(a)
    for j in range(size_n):
        pivot = jnp.sqrt(_pick((row == j) & (col == j), a, None).reshape(1, 1))
        lcol = jnp.where(row[:, :1] >= j, _pick(col == j, a, 1) / pivot, 0.0)
        lrow = jnp.where(col[:1, :] >= j, _pick(row == j, a, 0) / pivot, 0.0)
        lower = lower + jnp.where(col == j, lcol, 0.0)
        upper = upper + jnp.where(row == j, lrow, 0.0)
        a = a - lcol * lrow
    row1 = row[:, :1]
    rest = target
    forward = jnp.zeros_like(target)
    for i in range(size_n):
        lii = _pick((row == i) & (col == i), lower, None).reshape(1, 1)
        yi = _pick(row1 == i, rest, 0) / lii
        forward = forward + jnp.where(row1 == i, yi, 0.0)
        rest = rest - jnp.where(row1 > i, _pick(col == i, lower, 1), 0.0) * yi
    rest = forward
    gamma = jnp.zeros_like(target)
    for i in range(size_n - 1, -1, -1):
        lii = _pick((row == i) & (col == i), lower, None).reshape(1, 1)
        gi = _pick(row1 == i, rest, 0) / lii
        gamma = gamma + jnp.where(row1 == i, gi, 0.0)
        rest = rest - jnp.where(row1 < i, _pick(col == i, upper, 1), 0.0) * gi
    before = pltpu.roll(gamma, 1, 0)
    weights = jnp.where(row1 == 0, 1.0, 0.0) - gamma + before
    return jnp.broadcast_to(weights, prod.shape)


def _permute_square(prod, perm):
    row = lax.broadcasted_iota(jnp.int32, prod.shape, 0)
    col = lax.broadcasted_iota(jnp.int32, prod.shape, 1)
    count = len(perm)
    permcol = jnp.zeros((prod.shape[0], 1), jnp.int32)
    permrow = jnp.zeros((1, prod.shape[1]), jnp.int32)
    for i in range(count):
        permcol = jnp.where(row[:, :1] == i, perm[i], permcol)
        permrow = jnp.where(col[:1, :] == i, perm[i], permrow)
    by_rows = jnp.zeros_like(prod)
    for m in range(count):
        by_rows = by_rows + jnp.where(permcol == m, _pick(row == m, prod, 0), 0.0)
    by_rows = jnp.where(row < count, by_rows, 0.0)
    both = jnp.zeros_like(prod)
    for m in range(count):
        both = both + jnp.where(permrow == m, _pick(col == m, by_rows, 1), 0.0)
    return jnp.where(col < count, both, 0.0)


def _pair_sums(vectors, pairs):
    shape = (8, 128)
    row = lax.broadcasted_iota(jnp.int32, shape, 0)
    col = lax.broadcasted_iota(jnp.int32, shape, 1)
    prod = jnp.zeros(shape, jnp.float32)
    for i, j in pairs:
        value = jnp.sum(vectors[i] * vectors[j]).reshape(1, 1)
        spot = ((row == i) & (col == j)) | ((row == j) & (col == i))
        prod = jnp.where(spot, value, prod)
    return prod


def _fused_kernel(nk, ne, entries, margin,
                  slot_ref, shift_ref, class_ref, optical_ref, occ_ref, acoustic_ref,
                  chunk_ref, cur_ref, pin_ref, pres_ref, out_ref,
                  ypad, bases, send1, recv1, recv2, acc1, ts, tr, ss1, rs1, ss2, rs2):
    mk = lax.axis_index("kgrp")
    me = lax.axis_index("energy")
    width = chunk_ref.shape[-1]
    lead, per_row, padded_len = ypad.shape
    length = padded_len - 2 * margin
    barrier = pltpu.get_barrier_semaphore()
    for s in range(nk - 1):
        pl.semaphore_signal(barrier, 1, device_id=((mk + s + 1) % nk, me), device_id_type=MESH)
    for s in range(ne - 1):
        pl.semaphore_signal(barrier, 1, device_id=(mk, (me + s + 1) % ne), device_id_type=MESH)
    ypad[:, :, :margin] = jnp.zeros((lead, per_row, margin), jnp.float32)
    ypad[:, :, margin + length :] = jnp.zeros((lead, per_row, margin), jnp.float32)
    ypad[:, :, pl.ds(pl.multiple_of(margin + me * width, width), width)] = chunk_ref[me]
    pl.semaphore_wait(barrier, nk - 1 + ne - 1)

    copies = []
    for s in range(ne - 1):
        peer = (me + s + 1) % ne
        c = pltpu.make_async_remote_copy(
            src_ref=chunk_ref.at[peer],
            dst_ref=ypad.at[:, :, pl.ds(pl.multiple_of(margin + me * width, width), width)],
            send_sem=ts.at[s],
            recv_sem=tr.at[ne - 2 - s],
            device_id=(mk, peer),
            device_id_type=MESH,
        )
        c.start()
        copies.append(c)
    history = [pres_ref[m * lead : (m + 1) * lead] for m in range(HIST)]
    gram = _pair_sums([None] + history, [(i, j) for i in range(1, HIST + 1) for j in range(i, HIST + 1)])
    for q in range(ne - 1):
        source = (me + q + 1) % ne
        pltpu.make_async_remote_copy(
            src_ref=chunk_ref.at[me],
            dst_ref=ypad.at[:, :, pl.ds(pl.multiple_of(margin + source * width, width), width)],
            send_sem=ts.at[q],
            recv_sem=tr.at[q],
            device_id=(mk, source),
            device_id_type=MESH,
        ).wait_recv()
    for s in range(ne - 1):
        copies[s].wait_send()

    y = ypad[...]
    lesser = lax.broadcasted_iota(jnp.int32, (lead, 1, 1), 0) < lead // 2
    row = lax.broadcasted_iota(jnp.int32, (1, per_row, 1), 1)
    coupling = jnp.zeros((1, per_row, 1), jnp.float32)
    for r in range(per_row):
        coupling = jnp.where(row == r, acoustic_ref[class_ref[me * per_row + r]], coupling)
    sigma = coupling * y[:, :, margin : margin + length]
    for m in range(2):
        shift = shift_ref[m]
        strength = optical_ref[m]
        number = occ_ref[m]
        ahead = pltpu.roll(y, padded_len - shift, 2)[:, :, margin : margin + length]
        behind = pltpu.roll(y, shift, 2)[:, :, margin : margin + length]
        up = jnp.where(lesser, number + 1.0, number)
        down = jnp.where(lesser, number, number + 1.0)
        sigma = sigma + strength * (up * ahead + down * behind)
    res = sigma - cur_ref[...]
    fresh = _pair_sums([res] + history, [(0, j) for j in range(HIST + 1)])
    send1[...] = fresh + gram

    def exchange(src, recv, ssem, rsem, count, peer):
        out = []
        for s in range(count - 1):
            c = pltpu.make_async_remote_copy(
                src_ref=src,
                dst_ref=recv.at[count - 2 - s],
                send_sem=ssem.at[s],
                recv_sem=rsem.at[count - 2 - s],
                device_id=peer(s),
                device_id_type=MESH,
            )
            c.start()
            out.append(c)
        return out

    def finish(out):
        for c in out:
            c.wait_recv()
        for c in out:
            c.wait_send()

    def total(own, recv, mine, count):
        acc = jnp.zeros_like(own)
        for idx in range(count):
            slot = jnp.minimum((idx - mine - 1 + count) % count, count - 2)
            acc = acc + jnp.where(idx == mine, own, recv[slot])
        return acc

    pending = exchange(send1, recv1, ss1, rs1, nk, lambda s: ((mk + s + 1) % nk, me))
    for m in range(HIST):
        bases[m + 1] = pin_ref[m * lead : (m + 1) * lead] + mixing_share * history[m]
    finish(pending)
    acc1[...] = total(send1[...], recv1, mk, nk)
    pending = exchange(acc1, recv2, ss2, rs2, ne, lambda s: (mk, (me + s + 1) % ne))
    bases[0] = cur_ref[...] + mixing_share * res
    finish(pending)
    summed = total(acc1[...], recv2, me, ne)
    perm = [0] + [slot_ref[i] + 1 for i in range(HIST)]
    aged = _permute_square(summed / entries, perm)
    weights = _weights_from_products(aged)[:, :1]
    row1 = lax.broadcasted_iota(jnp.int32, weights.shape, 0)
    slot_w = [None] * (HIST + 1)
    row1 = lax.broadcasted_iota(jnp.int32, weights.shape, 0)
    for i in range(HIST + 1):
        w_i = _pick(row1 == i, weights, 0)
        for m in range(HIST + 1):
            term = jnp.where(perm[i] == m, w_i, 0.0)
            slot_w[m] = term if slot_w[m] is None else slot_w[m] + term
    slot_w = [w.reshape(1, 1, 1) for w in slot_w]
    mixed = slot_w[0] * bases[0]
    for m in range(HIST):
        mixed = mixed + slot_w[m + 1] * bases[m + 1]
    out_ref[...] = mixed


def fused_tail(scalars, chunks, cur, pin, pres, nk, ne, entries):
    tile = (8, 128)
    margin = 128
    lead, per_row = chunks.shape[1:3]
    smem = pl.BlockSpec(memory_space=pltpu.SMEM)
    vmem = pl.BlockSpec(memory_space=pltpu.VMEM)
    return pl.pallas_call(
        functools.partial(_fused_kernel, nk, ne, entries, margin),
        out_shape=jax.ShapeDtypeStruct(cur.shape, jnp.float32),
        in_specs=[smem] * len(scalars) + [vmem] * 4,
        out_specs=vmem,
        scratch_shapes=[
            pltpu.VMEM((lead, per_row, cur.shape[-1] + 2 * margin), jnp.float32),
            pltpu.VMEM((HIST + 1,) + cur.shape, jnp.float32),
            pltpu.VMEM(tile, jnp.float32),
            pltpu.VMEM((nk - 1,) + tile, jnp.float32),
            pltpu.VMEM((ne - 1,) + tile, jnp.float32),
            pltpu.VMEM(tile, jnp.float32),
            pltpu.SemaphoreType.DMA((ne - 1,)),
            pltpu.SemaphoreType.DMA((ne - 1,)),
            pltpu.SemaphoreType.DMA((nk - 1,)),
            pltpu.SemaphoreType.DMA((nk - 1,)),
            pltpu.SemaphoreType.DMA((ne - 1,)),
            pltpu.SemaphoreType.DMA((ne - 1,)),
        ],
        compiler_params=pltpu.CompilerParams(collective_id=0, has_side_effects=True),
    )(*scalars, chunks, cur, pin, pres)


def per_device(
    greens,
    current,
    past_inputs,
    past_residuals,
    slot_order,
    neighbour,
    momentum_class,
    stencil_weight,
    acoustic_coupling,
    optical_coupling,
    occupation,
    phonon_shift,
):
    group_len = greens.shape[3]
    rows_here = current.shape[3]
    group_id = lax.axis_index("kgrp")
    energy_id = lax.axis_index("energy")
    nk = lax.axis_size("kgrp")
    ne = lax.axis_size("energy")
    total_k = group_len * nk
    ends = padded_2(greens, (("kgrp", 3),), group_len, True)
    low = ends[:, :, :, :group_len]
    high = ends[:, :, :, 2 * group_len :]
    local_index = (neighbour - group_id * group_len + group_len) % total_k
    stencil = jnp.sum(
        jnp.where(
            local_index[:, :, None] == jnp.arange(3 * group_len, dtype=jnp.int32)[None, None, :],
            stencil_weight[None, :, None],
            0.0,
        ),
        axis=1,
    )
    lead = greens.shape[:3]
    flat = lambda x: x.reshape((-1,) + x.shape[3:])
    stencil = stencil.reshape(ne, rows_here, 3 * group_len)
    chunks = jnp.zeros((ne, flat(greens).shape[0], rows_here, greens.shape[4]), jnp.float32)
    for part, block in enumerate((low, greens, high)):
        chunks = chunks + jnp.einsum(
            "dkr,bre->dbke",
            stencil[:, :, part * group_len : (part + 1) * group_len],
            flat(block),
            precision=lax.Precision.HIGHEST,
        )
    lanes = current.shape[-1]
    entries = float(current.size * nk * ne)
    scalars = (slot_order, phonon_shift, momentum_class, optical_coupling, occupation, acoustic_coupling)
    mixed = fused_tail(
        scalars,
        chunks,
        current.reshape(-1, rows_here, lanes),
        past_inputs.reshape(-1, rows_here, lanes),
        past_residuals.reshape(-1, rows_here, lanes),
        nk,
        ne,
        entries,
    ).reshape(current.shape)
    return mixed


def solution(mesh):
    return jax.shard_map(
        per_device,
        mesh=mesh,
        in_specs=(
            P(None, None, None, "kgrp", "energy"),
            P(None, None, None, ("kgrp", "energy"), None),
            P(None, None, None, None, ("kgrp", "energy"), None),
            P(None, None, None, None, ("kgrp", "energy"), None),
            P(),
            P("kgrp", None),
            P("kgrp"),
            P(),
            P(),
            P(),
            P(),
            P(),
        ),
        out_specs=P(None, None, None, ("kgrp", "energy"), None),
        check_vma=False,
    )
```

```python
import functools

import jax
import jax.numpy as jnp
from jax import lax
from jax.experimental import pallas as pl
from jax.experimental.pallas import tpu as pltpu
from jax.sharding import PartitionSpec as P

SHIFT_MAX = 96
HIST = 5

mixing_share = 0.5
ridge_share = 0.1

MESH = pl.DeviceIdType.MESH


def padded_2(block, sides, width, periodic):
    for axis, dim in sides:
        count = lax.axis_size(axis)
        forward = [(i, i + 1) for i in range(count - 1)]
        if periodic:
            forward.append((count - 1, 0))
        backward = [(target, source) for source, target in forward]
        low = lax.ppermute(
            lax.slice_in_dim(block, block.shape[dim] - width, None, axis=dim), axis, forward
        )
        high = lax.ppermute(lax.slice_in_dim(block, 0, width, axis=dim), axis, backward)
        block = jnp.concatenate([low, block, high], axis=dim)
    return block


def emit(padded, margin, length, coupling_row, optical, occupation, shifts):
    lesser = padded[0]
    greater = padded[1]

    def energy_view(source, offset):
        return lax.dynamic_slice_in_dim(source, margin + offset, length, axis=source.ndim - 1)

    sigma_less = coupling_row[:, None] * energy_view(lesser, 0)
    sigma_more = coupling_row[:, None] * energy_view(greater, 0)
    for column in range(2):
        strength = optical[column]
        number = occupation[column]
        offset = shifts[column]
        sigma_less = sigma_less + strength * (
            (number + 1.0) * energy_view(lesser, offset) + number * energy_view(lesser, -offset)
        )
        sigma_more = sigma_more + strength * (
            (number + 1.0) * energy_view(greater, -offset) + number * energy_view(greater, offset)
        )
    return jnp.stack([sigma_less, sigma_more])


def _pick(mask, x, axis):
    return jnp.sum(jnp.where(mask, x, 0.0), axis=axis, keepdims=True)


def _weights_from_products(prod):
    size_n = HIST
    row = lax.broadcasted_iota(jnp.int32, prod.shape, 0)
    col = lax.broadcasted_iota(jnp.int32, prod.shape, 1)
    rows, cols = prod.shape
    down = pltpu.roll(prod, rows - 1, 0)
    right = pltpu.roll(prod, cols - 1, 1)
    diag = pltpu.roll(down, cols - 1, 1)
    inside = (row < size_n) & (col < size_n)
    system = jnp.where(inside, prod - right - down + diag, 0.0)
    target = _pick((col == 0) & (row < size_n), prod - down, 1)
    eye = inside & (row == col)
    trace = jnp.sum(jnp.where(eye, system, 0.0), keepdims=True)
    ridge = ridge_share * trace / size_n + 1e-06
    a = system + jnp.where(eye, ridge, 0.0)
    lower = jnp.zeros_like(a)
    upper = jnp.zeros_like(a)
    for j in range(size_n):
        pivot = jnp.sqrt(_pick((row == j) & (col == j), a, None).reshape(1, 1))
        lcol = jnp.where(row[:, :1] >= j, _pick(col == j, a, 1) / pivot, 0.0)
        lrow = jnp.where(col[:1, :] >= j, _pick(row == j, a, 0) / pivot, 0.0)
        lower = lower + jnp.where(col == j, lcol, 0.0)
        upper = upper + jnp.where(row == j, lrow, 0.0)
        a = a - lcol * lrow
    row1 = row[:, :1]
    rest = target
    forward = jnp.zeros_like(target)
    for i in range(size_n):
        lii = _pick((row == i) & (col == i), lower, None).reshape(1, 1)
        yi = _pick(row1 == i, rest, 0) / lii
        forward = forward + jnp.where(row1 == i, yi, 0.0)
        rest = rest - jnp.where(row1 > i, _pick(col == i, lower, 1), 0.0) * yi
    rest = forward
    gamma = jnp.zeros_like(target)
    for i in range(size_n - 1, -1, -1):
        lii = _pick((row == i) & (col == i), lower, None).reshape(1, 1)
        gi = _pick(row1 == i, rest, 0) / lii
        gamma = gamma + jnp.where(row1 == i, gi, 0.0)
        rest = rest - jnp.where(row1 < i, _pick(col == i, upper, 1), 0.0) * gi
    before = pltpu.roll(gamma, 1, 0)
    weights = jnp.where(row1 == 0, 1.0, 0.0) - gamma + before
    return jnp.broadcast_to(weights, prod.shape)


def _permute_square(prod, perm):
    row = lax.broadcasted_iota(jnp.int32, prod.shape, 0)
    col = lax.broadcasted_iota(jnp.int32, prod.shape, 1)
    count = len(perm)
    permcol = jnp.zeros((prod.shape[0], 1), jnp.int32)
    permrow = jnp.zeros((1, prod.shape[1]), jnp.int32)
    for i in range(count):
        permcol = jnp.where(row[:, :1] == i, perm[i], permcol)
        permrow = jnp.where(col[:1, :] == i, perm[i], permrow)
    by_rows = jnp.zeros_like(prod)
    for m in range(count):
        by_rows = by_rows + jnp.where(permcol == m, _pick(row == m, prod, 0), 0.0)
    by_rows = jnp.where(row < count, by_rows, 0.0)
    both = jnp.zeros_like(prod)
    for m in range(count):
        both = both + jnp.where(permrow == m, _pick(col == m, by_rows, 1), 0.0)
    return jnp.where(col < count, both, 0.0)


def _pair_sums(vectors, pairs):
    shape = (8, 128)
    row = lax.broadcasted_iota(jnp.int32, shape, 0)
    col = lax.broadcasted_iota(jnp.int32, shape, 1)
    prod = jnp.zeros(shape, jnp.float32)
    for i, j in pairs:
        value = jnp.sum(vectors[i] * vectors[j]).reshape(1, 1)
        spot = ((row == i) & (col == j)) | ((row == j) & (col == i))
        prod = jnp.where(spot, value, prod)
    return prod


def _fused_kernel(nk, ne, entries, margin,
                  slot_ref, shift_ref, class_ref, optical_ref, occ_ref, acoustic_ref,
                  chunk_ref, cur_ref, pin_ref, pres_ref, out_ref,
                  ypad, cur16, hist16, bases, send1, recv1, recv2, acc1, ts, tr, ss1, rs1, ss2, rs2):
    mk = lax.axis_index("kgrp")
    me = lax.axis_index("energy")
    width = chunk_ref.shape[-1]
    rows, padded_len = ypad.shape
    lead = cur_ref.shape[0]
    per_row = rows // lead
    length = padded_len - 2 * margin
    barrier = pltpu.get_barrier_semaphore()
    for s in range(nk - 1):
        pl.semaphore_signal(barrier, 1, device_id=((mk + s + 1) % nk, me), device_id_type=MESH)
    for s in range(ne - 1):
        pl.semaphore_signal(barrier, 1, device_id=(mk, (me + s + 1) % ne), device_id_type=MESH)
    ypad[:, :margin] = jnp.zeros((rows, margin), jnp.float32)
    ypad[:, margin + length :] = jnp.zeros((rows, margin), jnp.float32)
    ypad[:, pl.ds(pl.multiple_of(margin + me * width, width), width)] = chunk_ref[me]
    pl.semaphore_wait(barrier, nk - 1 + ne - 1)

    copies = []
    for s in range(ne - 1):
        peer = (me + s + 1) % ne
        c = pltpu.make_async_remote_copy(
            src_ref=chunk_ref.at[peer],
            dst_ref=ypad.at[:, pl.ds(pl.multiple_of(margin + me * width, width), width)],
            send_sem=ts.at[s],
            recv_sem=tr.at[ne - 2 - s],
            device_id=(mk, peer),
            device_id_type=MESH,
        )
        c.start()
        copies.append(c)
    history = [pres_ref[m * lead : (m + 1) * lead] for m in range(HIST)]
    cur16[...] = cur_ref[...].reshape(rows, length)
    for m in range(HIST):
        hist16[m] = history[m].reshape(rows, length)
    flat_hist = [hist16[m] for m in range(HIST)]
    gram = _pair_sums([None] + flat_hist, [(i, j) for i in range(1, HIST + 1) for j in range(i, HIST + 1)])
    for q in range(ne - 1):
        source = (me + q + 1) % ne
        pltpu.make_async_remote_copy(
            src_ref=chunk_ref.at[me],
            dst_ref=ypad.at[:, pl.ds(pl.multiple_of(margin + source * width, width), width)],
            send_sem=ts.at[q],
            recv_sem=tr.at[q],
            device_id=(mk, source),
            device_id_type=MESH,
        ).wait_recv()
    for s in range(ne - 1):
        copies[s].wait_send()

    y = ypad[...]
    row = lax.broadcasted_iota(jnp.int32, (rows, 1), 0)
    lesser = row < rows // 2
    coupling = jnp.zeros((rows, 1), jnp.float32)
    for r in range(per_row):
        coupling = jnp.where(row % per_row == r, acoustic_ref[class_ref[me * per_row + r]], coupling)
    sigma = coupling * y[:, margin : margin + length]
    for m in range(2):
        shift = shift_ref[m]
        strength = optical_ref[m]
        number = occ_ref[m]
        ahead = pltpu.roll(y, padded_len - shift, 1)[:, margin : margin + length]
        behind = pltpu.roll(y, shift, 1)[:, margin : margin + length]
        up = jnp.where(lesser, number + 1.0, number)
        down = jnp.where(lesser, number, number + 1.0)
        sigma = sigma + strength * (up * ahead + down * behind)
    res = sigma - cur16[...]
    fresh = _pair_sums([res] + [hist16[m] for m in range(HIST)], [(0, j) for j in range(HIST + 1)])
    send1[...] = fresh + gram

    def exchange(src, recv, ssem, rsem, count, peer):
        out = []
        for s in range(count - 1):
            c = pltpu.make_async_remote_copy(
                src_ref=src,
                dst_ref=recv.at[count - 2 - s],
                send_sem=ssem.at[s],
                recv_sem=rsem.at[count - 2 - s],
                device_id=peer(s),
                device_id_type=MESH,
            )
            c.start()
            out.append(c)
        return out

    def finish(out):
        for c in out:
            c.wait_recv()
        for c in out:
            c.wait_send()

    def total(own, recv, mine, count):
        acc = jnp.zeros_like(own)
        for idx in range(count):
            slot = jnp.minimum((idx - mine - 1 + count) % count, count - 2)
            acc = acc + jnp.where(idx == mine, own, recv[slot])
        return acc

    pending = exchange(send1, recv1, ss1, rs1, nk, lambda s: ((mk + s + 1) % nk, me))
    for m in range(HIST):
        bases[m + 1] = pin_ref[m * lead : (m + 1) * lead] + mixing_share * history[m]
    finish(pending)
    acc1[...] = total(send1[...], recv1, mk, nk)
    pending = exchange(acc1, recv2, ss2, rs2, ne, lambda s: (mk, (me + s + 1) % ne))
    bases[0] = (cur16[...] + mixing_share * res).reshape(cur_ref.shape)
    finish(pending)
    summed = total(acc1[...], recv2, me, ne)
    perm = [0] + [slot_ref[i] + 1 for i in range(HIST)]
    aged = _permute_square(summed / entries, perm)
    weights = _weights_from_products(aged)[:, :1]
    row1 = lax.broadcasted_iota(jnp.int32, weights.shape, 0)
    slot_w = [None] * (HIST + 1)
    row1 = lax.broadcasted_iota(jnp.int32, weights.shape, 0)
    for i in range(HIST + 1):
        w_i = _pick(row1 == i, weights, 0)
        for m in range(HIST + 1):
            term = jnp.where(perm[i] == m, w_i, 0.0)
            slot_w[m] = term if slot_w[m] is None else slot_w[m] + term
    slot_w = [w.reshape(1, 1, 1) for w in slot_w]
    mixed = slot_w[0] * bases[0]
    for m in range(HIST):
        mixed = mixed + slot_w[m + 1] * bases[m + 1]
    out_ref[...] = mixed


def fused_tail(scalars, chunks, cur, pin, pres, nk, ne, entries):
    tile = (8, 128)
    margin = 128
    rows = chunks.shape[1]
    smem = pl.BlockSpec(memory_space=pltpu.SMEM)
    vmem = pl.BlockSpec(memory_space=pltpu.VMEM)
    return pl.pallas_call(
        functools.partial(_fused_kernel, nk, ne, entries, margin),
        out_shape=jax.ShapeDtypeStruct(cur.shape, jnp.float32),
        in_specs=[smem] * len(scalars) + [vmem] * 4,
        out_specs=vmem,
        scratch_shapes=[
            pltpu.VMEM((rows, cur.shape[-1] + 2 * margin), jnp.float32),
            pltpu.VMEM((rows, cur.shape[-1]), jnp.float32),
            pltpu.VMEM((HIST, rows, cur.shape[-1]), jnp.float32),
            pltpu.VMEM((HIST + 1,) + cur.shape, jnp.float32),
            pltpu.VMEM(tile, jnp.float32),
            pltpu.VMEM((nk - 1,) + tile, jnp.float32),
            pltpu.VMEM((ne - 1,) + tile, jnp.float32),
            pltpu.VMEM(tile, jnp.float32),
            pltpu.SemaphoreType.DMA((ne - 1,)),
            pltpu.SemaphoreType.DMA((ne - 1,)),
            pltpu.SemaphoreType.DMA((nk - 1,)),
            pltpu.SemaphoreType.DMA((nk - 1,)),
            pltpu.SemaphoreType.DMA((ne - 1,)),
            pltpu.SemaphoreType.DMA((ne - 1,)),
        ],
        compiler_params=pltpu.CompilerParams(collective_id=0, has_side_effects=True),
    )(*scalars, chunks, cur, pin, pres)


def per_device(
    greens,
    current,
    past_inputs,
    past_residuals,
    slot_order,
    neighbour,
    momentum_class,
    stencil_weight,
    acoustic_coupling,
    optical_coupling,
    occupation,
    phonon_shift,
):
    group_len = greens.shape[3]
    rows_here = current.shape[3]
    group_id = lax.axis_index("kgrp")
    energy_id = lax.axis_index("energy")
    nk = lax.axis_size("kgrp")
    ne = lax.axis_size("energy")
    total_k = group_len * nk
    ends = padded_2(greens, (("kgrp", 3),), group_len, True)
    low = ends[:, :, :, :group_len]
    high = ends[:, :, :, 2 * group_len :]
    local_index = (neighbour - group_id * group_len + group_len) % total_k
    stencil = jnp.sum(
        jnp.where(
            local_index[:, :, None] == jnp.arange(3 * group_len, dtype=jnp.int32)[None, None, :],
            stencil_weight[None, :, None],
            0.0,
        ),
        axis=1,
    )
    lead = greens.shape[:3]
    flat = lambda x: x.reshape((-1,) + x.shape[3:])
    stencil = stencil.reshape(ne, rows_here, 3 * group_len)
    chunks = jnp.zeros((ne, flat(greens).shape[0], rows_here, greens.shape[4]), jnp.float32)
    for part, block in enumerate((low, greens, high)):
        chunks = chunks + jnp.einsum(
            "dkr,bre->dbke",
            stencil[:, :, part * group_len : (part + 1) * group_len],
            flat(block),
            precision=lax.Precision.HIGHEST,
        )
    chunks = chunks.reshape(ne, -1, greens.shape[4])
    lanes = current.shape[-1]
    entries = float(current.size * nk * ne)
    scalars = (slot_order, phonon_shift, momentum_class, optical_coupling, occupation, acoustic_coupling)
    mixed = fused_tail(
        scalars,
        chunks,
        current.reshape(-1, rows_here, lanes),
        past_inputs.reshape(-1, rows_here, lanes),
        past_residuals.reshape(-1, rows_here, lanes),
        nk,
        ne,
        entries,
    ).reshape(current.shape)
    return mixed


def solution(mesh):
    return jax.shard_map(
        per_device,
        mesh=mesh,
        in_specs=(
            P(None, None, None, "kgrp", "energy"),
            P(None, None, None, ("kgrp", "energy"), None),
            P(None, None, None, None, ("kgrp", "energy"), None),
            P(None, None, None, None, ("kgrp", "energy"), None),
            P(),
            P("kgrp", None),
            P("kgrp"),
            P(),
            P(),
            P(),
            P(),
            P(),
        ),
        out_specs=P(None, None, None, ("kgrp", "energy"), None),
        check_vma=False,
    )
```

```python
import functools

import jax
import jax.numpy as jnp
from jax import lax
from jax.experimental import pallas as pl
from jax.experimental.pallas import tpu as pltpu
from jax.sharding import PartitionSpec as P

SHIFT_MAX = 96
HIST = 5

mixing_share = 0.5
ridge_share = 0.1

MESH = pl.DeviceIdType.MESH


def padded_2(block, sides, width, periodic):
    for axis, dim in sides:
        count = lax.axis_size(axis)
        forward = [(i, i + 1) for i in range(count - 1)]
        if periodic:
            forward.append((count - 1, 0))
        backward = [(target, source) for source, target in forward]
        low = lax.ppermute(
            lax.slice_in_dim(block, block.shape[dim] - width, None, axis=dim), axis, forward
        )
        high = lax.ppermute(lax.slice_in_dim(block, 0, width, axis=dim), axis, backward)
        block = jnp.concatenate([low, block, high], axis=dim)
    return block


def emit(padded, margin, length, coupling_row, optical, occupation, shifts):
    lesser = padded[0]
    greater = padded[1]

    def energy_view(source, offset):
        return lax.dynamic_slice_in_dim(source, margin + offset, length, axis=source.ndim - 1)

    sigma_less = coupling_row[:, None] * energy_view(lesser, 0)
    sigma_more = coupling_row[:, None] * energy_view(greater, 0)
    for column in range(2):
        strength = optical[column]
        number = occupation[column]
        offset = shifts[column]
        sigma_less = sigma_less + strength * (
            (number + 1.0) * energy_view(lesser, offset) + number * energy_view(lesser, -offset)
        )
        sigma_more = sigma_more + strength * (
            (number + 1.0) * energy_view(greater, -offset) + number * energy_view(greater, offset)
        )
    return jnp.stack([sigma_less, sigma_more])


def _pick(mask, x, axis):
    return jnp.sum(jnp.where(mask, x, 0.0), axis=axis, keepdims=True)


def _weights_from_products(prod):
    size_n = HIST
    row = lax.broadcasted_iota(jnp.int32, prod.shape, 0)
    col = lax.broadcasted_iota(jnp.int32, prod.shape, 1)
    rows, cols = prod.shape
    down = pltpu.roll(prod, rows - 1, 0)
    right = pltpu.roll(prod, cols - 1, 1)
    diag = pltpu.roll(down, cols - 1, 1)
    inside = (row < size_n) & (col < size_n)
    system = jnp.where(inside, prod - right - down + diag, 0.0)
    target = _pick((col == 0) & (row < size_n), prod - down, 1)
    eye = inside & (row == col)
    trace = jnp.sum(jnp.where(eye, system, 0.0), keepdims=True)
    ridge = ridge_share * trace / size_n + 1e-06
    a = system + jnp.where(eye, ridge, 0.0)
    lower = jnp.zeros_like(a)
    upper = jnp.zeros_like(a)
    for j in range(size_n):
        pivot = jnp.sqrt(_pick((row == j) & (col == j), a, None).reshape(1, 1))
        lcol = jnp.where(row[:, :1] >= j, _pick(col == j, a, 1) / pivot, 0.0)
        lrow = jnp.where(col[:1, :] >= j, _pick(row == j, a, 0) / pivot, 0.0)
        lower = lower + jnp.where(col == j, lcol, 0.0)
        upper = upper + jnp.where(row == j, lrow, 0.0)
        a = a - lcol * lrow
    row1 = row[:, :1]
    rest = target
    forward = jnp.zeros_like(target)
    for i in range(size_n):
        lii = _pick((row == i) & (col == i), lower, None).reshape(1, 1)
        yi = _pick(row1 == i, rest, 0) / lii
        forward = forward + jnp.where(row1 == i, yi, 0.0)
        rest = rest - jnp.where(row1 > i, _pick(col == i, lower, 1), 0.0) * yi
    rest = forward
    gamma = jnp.zeros_like(target)
    for i in range(size_n - 1, -1, -1):
        lii = _pick((row == i) & (col == i), lower, None).reshape(1, 1)
        gi = _pick(row1 == i, rest, 0) / lii
        gamma = gamma + jnp.where(row1 == i, gi, 0.0)
        rest = rest - jnp.where(row1 < i, _pick(col == i, upper, 1), 0.0) * gi
    before = pltpu.roll(gamma, 1, 0)
    weights = jnp.where(row1 == 0, 1.0, 0.0) - gamma + before
    return jnp.broadcast_to(weights, prod.shape)


def _permute_square(prod, perm):
    row = lax.broadcasted_iota(jnp.int32, prod.shape, 0)
    col = lax.broadcasted_iota(jnp.int32, prod.shape, 1)
    count = len(perm)
    permcol = jnp.zeros((prod.shape[0], 1), jnp.int32)
    permrow = jnp.zeros((1, prod.shape[1]), jnp.int32)
    for i in range(count):
        permcol = jnp.where(row[:, :1] == i, perm[i], permcol)
        permrow = jnp.where(col[:1, :] == i, perm[i], permrow)
    by_rows = jnp.zeros_like(prod)
    for m in range(count):
        by_rows = by_rows + jnp.where(permcol == m, _pick(row == m, prod, 0), 0.0)
    by_rows = jnp.where(row < count, by_rows, 0.0)
    both = jnp.zeros_like(prod)
    for m in range(count):
        both = both + jnp.where(permrow == m, _pick(col == m, by_rows, 1), 0.0)
    return jnp.where(col < count, both, 0.0)


def _pair_sums(vectors, pairs):
    shape = (8, 128)
    row = lax.broadcasted_iota(jnp.int32, shape, 0)
    col = lax.broadcasted_iota(jnp.int32, shape, 1)
    prod = jnp.zeros(shape, jnp.float32)
    for i, j in pairs:
        value = jnp.sum(vectors[i] * vectors[j]).reshape(1, 1)
        spot = ((row == i) & (col == j)) | ((row == j) & (col == i))
        prod = jnp.where(spot, value, prod)
    return prod


def _halo_kernel(nk, x_ref, low_ref, high_ref, ssem, rsem):
    mk = lax.axis_index("kgrp")
    me = lax.axis_index("energy")
    before = (mk + nk - 1) % nk
    after = (mk + 1) % nk
    barrier = pltpu.get_barrier_semaphore()
    pl.semaphore_signal(barrier, 1, device_id=(before, me), device_id_type=MESH)
    pl.semaphore_signal(barrier, 1, device_id=(after, me), device_id_type=MESH)
    pl.semaphore_wait(barrier, 2)
    to_before = pltpu.make_async_remote_copy(
        src_ref=x_ref, dst_ref=high_ref, send_sem=ssem.at[0], recv_sem=rsem.at[1],
        device_id=(before, me), device_id_type=MESH,
    )
    to_after = pltpu.make_async_remote_copy(
        src_ref=x_ref, dst_ref=low_ref, send_sem=ssem.at[1], recv_sem=rsem.at[0],
        device_id=(after, me), device_id_type=MESH,
    )
    to_before.start()
    to_after.start()
    to_after.wait_recv()
    to_before.wait_recv()
    to_before.wait_send()
    to_after.wait_send()


def halo(block, nk):
    vmem = pl.BlockSpec(memory_space=pltpu.VMEM)
    shape = jax.ShapeDtypeStruct(block.shape, jnp.float32)
    return pl.pallas_call(
        functools.partial(_halo_kernel, nk),
        out_shape=(shape, shape),
        in_specs=[vmem],
        out_specs=(vmem, vmem),
        scratch_shapes=[pltpu.SemaphoreType.DMA((2,)), pltpu.SemaphoreType.DMA((2,))],
        compiler_params=pltpu.CompilerParams(collective_id=1, has_side_effects=True),
    )(block)


def _fused_kernel(nk, ne, entries, margin,
                  slot_ref, shift_ref, class_ref, optical_ref, occ_ref, acoustic_ref,
                  chunk_ref, cur_ref, pin_ref, pres_ref, out_ref,
                  ypad, cur16, hist16, bases, send1, recv1, recv2, acc1, ts, tr, ss1, rs1, ss2, rs2):
    mk = lax.axis_index("kgrp")
    me = lax.axis_index("energy")
    width = chunk_ref.shape[-1]
    rows, padded_len = ypad.shape
    lead = cur_ref.shape[0]
    per_row = rows // lead
    length = padded_len - 2 * margin
    barrier = pltpu.get_barrier_semaphore()
    for s in range(nk - 1):
        pl.semaphore_signal(barrier, 1, device_id=((mk + s + 1) % nk, me), device_id_type=MESH)
    for s in range(ne - 1):
        pl.semaphore_signal(barrier, 1, device_id=(mk, (me + s + 1) % ne), device_id_type=MESH)
    ypad[:, :margin] = jnp.zeros((rows, margin), jnp.float32)
    ypad[:, margin + length :] = jnp.zeros((rows, margin), jnp.float32)
    ypad[:, pl.ds(pl.multiple_of(margin + me * width, width), width)] = chunk_ref[me]
    pl.semaphore_wait(barrier, nk - 1 + ne - 1)

    copies = []
    for s in range(ne - 1):
        peer = (me + s + 1) % ne
        c = pltpu.make_async_remote_copy(
            src_ref=chunk_ref.at[peer],
            dst_ref=ypad.at[:, pl.ds(pl.multiple_of(margin + me * width, width), width)],
            send_sem=ts.at[s],
            recv_sem=tr.at[ne - 2 - s],
            device_id=(mk, peer),
            device_id_type=MESH,
        )
        c.start()
        copies.append(c)
    history = [pres_ref[m * lead : (m + 1) * lead] for m in range(HIST)]
    cur16[...] = cur_ref[...].reshape(rows, length)
    for m in range(HIST):
        hist16[m] = history[m].reshape(rows, length)
    flat_hist = [hist16[m] for m in range(HIST)]
    gram = _pair_sums([None] + flat_hist, [(i, j) for i in range(1, HIST + 1) for j in range(i, HIST + 1)])
    for q in range(ne - 1):
        source = (me + q + 1) % ne
        pltpu.make_async_remote_copy(
            src_ref=chunk_ref.at[me],
            dst_ref=ypad.at[:, pl.ds(pl.multiple_of(margin + source * width, width), width)],
            send_sem=ts.at[q],
            recv_sem=tr.at[q],
            device_id=(mk, source),
            device_id_type=MESH,
        ).wait_recv()
    for s in range(ne - 1):
        copies[s].wait_send()

    y = ypad[...]
    row = lax.broadcasted_iota(jnp.int32, (rows, 1), 0)
    lesser = row < rows // 2
    coupling = jnp.zeros((rows, 1), jnp.float32)
    for r in range(per_row):
        coupling = jnp.where(row % per_row == r, acoustic_ref[class_ref[me * per_row + r]], coupling)
    sigma = coupling * y[:, margin : margin + length]
    for m in range(2):
        shift = shift_ref[m]
        strength = optical_ref[m]
        number = occ_ref[m]
        ahead = pltpu.roll(y, padded_len - shift, 1)[:, margin : margin + length]
        behind = pltpu.roll(y, shift, 1)[:, margin : margin + length]
        up = jnp.where(lesser, number + 1.0, number)
        down = jnp.where(lesser, number, number + 1.0)
        sigma = sigma + strength * (up * ahead + down * behind)
    res = sigma - cur16[...]
    fresh = _pair_sums([res] + [hist16[m] for m in range(HIST)], [(0, j) for j in range(HIST + 1)])
    send1[...] = fresh + gram

    def exchange(src, recv, ssem, rsem, count, peer):
        out = []
        for s in range(count - 1):
            c = pltpu.make_async_remote_copy(
                src_ref=src,
                dst_ref=recv.at[count - 2 - s],
                send_sem=ssem.at[s],
                recv_sem=rsem.at[count - 2 - s],
                device_id=peer(s),
                device_id_type=MESH,
            )
            c.start()
            out.append(c)
        return out

    def finish(out):
        for c in out:
            c.wait_recv()
        for c in out:
            c.wait_send()

    def total(own, recv, mine, count):
        acc = jnp.zeros_like(own)
        for idx in range(count):
            slot = jnp.minimum((idx - mine - 1 + count) % count, count - 2)
            acc = acc + jnp.where(idx == mine, own, recv[slot])
        return acc

    pending = exchange(send1, recv1, ss1, rs1, nk, lambda s: ((mk + s + 1) % nk, me))
    for m in range(HIST):
        bases[m + 1] = pin_ref[m * lead : (m + 1) * lead] + mixing_share * history[m]
    finish(pending)
    acc1[...] = total(send1[...], recv1, mk, nk)
    pending = exchange(acc1, recv2, ss2, rs2, ne, lambda s: (mk, (me + s + 1) % ne))
    bases[0] = (cur16[...] + mixing_share * res).reshape(cur_ref.shape)
    finish(pending)
    summed = total(acc1[...], recv2, me, ne)
    perm = [0] + [slot_ref[i] + 1 for i in range(HIST)]
    aged = _permute_square(summed / entries, perm)
    weights = _weights_from_products(aged)[:, :1]
    row1 = lax.broadcasted_iota(jnp.int32, weights.shape, 0)
    slot_w = [None] * (HIST + 1)
    row1 = lax.broadcasted_iota(jnp.int32, weights.shape, 0)
    for i in range(HIST + 1):
        w_i = _pick(row1 == i, weights, 0)
        for m in range(HIST + 1):
            term = jnp.where(perm[i] == m, w_i, 0.0)
            slot_w[m] = term if slot_w[m] is None else slot_w[m] + term
    slot_w = [w.reshape(1, 1, 1) for w in slot_w]
    mixed = slot_w[0] * bases[0]
    for m in range(HIST):
        mixed = mixed + slot_w[m + 1] * bases[m + 1]
    out_ref[...] = mixed


def fused_tail(scalars, chunks, cur, pin, pres, nk, ne, entries):
    tile = (8, 128)
    margin = 128
    rows = chunks.shape[1]
    smem = pl.BlockSpec(memory_space=pltpu.SMEM)
    vmem = pl.BlockSpec(memory_space=pltpu.VMEM)
    return pl.pallas_call(
        functools.partial(_fused_kernel, nk, ne, entries, margin),
        out_shape=jax.ShapeDtypeStruct(cur.shape, jnp.float32),
        in_specs=[smem] * len(scalars) + [vmem] * 4,
        out_specs=vmem,
        scratch_shapes=[
            pltpu.VMEM((rows, cur.shape[-1] + 2 * margin), jnp.float32),
            pltpu.VMEM((rows, cur.shape[-1]), jnp.float32),
            pltpu.VMEM((HIST, rows, cur.shape[-1]), jnp.float32),
            pltpu.VMEM((HIST + 1,) + cur.shape, jnp.float32),
            pltpu.VMEM(tile, jnp.float32),
            pltpu.VMEM((nk - 1,) + tile, jnp.float32),
            pltpu.VMEM((ne - 1,) + tile, jnp.float32),
            pltpu.VMEM(tile, jnp.float32),
            pltpu.SemaphoreType.DMA((ne - 1,)),
            pltpu.SemaphoreType.DMA((ne - 1,)),
            pltpu.SemaphoreType.DMA((nk - 1,)),
            pltpu.SemaphoreType.DMA((nk - 1,)),
            pltpu.SemaphoreType.DMA((ne - 1,)),
            pltpu.SemaphoreType.DMA((ne - 1,)),
        ],
        compiler_params=pltpu.CompilerParams(collective_id=0, has_side_effects=True),
    )(*scalars, chunks, cur, pin, pres)


def per_device(
    greens,
    current,
    past_inputs,
    past_residuals,
    slot_order,
    neighbour,
    momentum_class,
    stencil_weight,
    acoustic_coupling,
    optical_coupling,
    occupation,
    phonon_shift,
):
    group_len = greens.shape[3]
    rows_here = current.shape[3]
    group_id = lax.axis_index("kgrp")
    energy_id = lax.axis_index("energy")
    nk = lax.axis_size("kgrp")
    ne = lax.axis_size("energy")
    total_k = group_len * nk
    low, high = halo(greens.reshape((-1,) + greens.shape[3:]), nk)
    local_index = (neighbour - group_id * group_len + group_len) % total_k
    stencil = jnp.sum(
        jnp.where(
            local_index[:, :, None] == jnp.arange(3 * group_len, dtype=jnp.int32)[None, None, :],
            stencil_weight[None, :, None],
            0.0,
        ),
        axis=1,
    )
    lead = greens.shape[:3]
    flat = lambda x: x.reshape((-1,) + x.shape[3:])
    stencil = stencil.reshape(ne, rows_here, 3 * group_len)
    chunks = jnp.zeros((ne, flat(greens).shape[0], rows_here, greens.shape[4]), jnp.float32)
    for part, block in enumerate((low.reshape(greens.shape), greens, high.reshape(greens.shape))):
        chunks = chunks + jnp.einsum(
            "dkr,bre->dbke",
            stencil[:, :, part * group_len : (part + 1) * group_len],
            flat(block),
            precision=lax.Precision.HIGHEST,
        )
    chunks = chunks.reshape(ne, -1, greens.shape[4])
    lanes = current.shape[-1]
    entries = float(current.size * nk * ne)
    scalars = (slot_order, phonon_shift, momentum_class, optical_coupling, occupation, acoustic_coupling)
    mixed = fused_tail(
        scalars,
        chunks,
        current.reshape(-1, rows_here, lanes),
        past_inputs.reshape(-1, rows_here, lanes),
        past_residuals.reshape(-1, rows_here, lanes),
        nk,
        ne,
        entries,
    ).reshape(current.shape)
    return mixed


def solution(mesh):
    return jax.shard_map(
        per_device,
        mesh=mesh,
        in_specs=(
            P(None, None, None, "kgrp", "energy"),
            P(None, None, None, ("kgrp", "energy"), None),
            P(None, None, None, None, ("kgrp", "energy"), None),
            P(None, None, None, None, ("kgrp", "energy"), None),
            P(),
            P("kgrp", None),
            P("kgrp"),
            P(),
            P(),
            P(),
            P(),
            P(),
        ),
        out_specs=P(None, None, None, ("kgrp", "energy"), None),
        check_vma=False,
    )
```

```python
import functools

import jax
import jax.numpy as jnp
from jax import lax
from jax.experimental import pallas as pl
from jax.experimental.pallas import tpu as pltpu
from jax.sharding import PartitionSpec as P

SHIFT_MAX = 96
HIST = 5

mixing_share = 0.5
ridge_share = 0.1

MESH = pl.DeviceIdType.MESH


def padded_2(block, sides, width, periodic):
    for axis, dim in sides:
        count = lax.axis_size(axis)
        forward = [(i, i + 1) for i in range(count - 1)]
        if periodic:
            forward.append((count - 1, 0))
        backward = [(target, source) for source, target in forward]
        low = lax.ppermute(
            lax.slice_in_dim(block, block.shape[dim] - width, None, axis=dim), axis, forward
        )
        high = lax.ppermute(lax.slice_in_dim(block, 0, width, axis=dim), axis, backward)
        block = jnp.concatenate([low, block, high], axis=dim)
    return block


def emit(padded, margin, length, coupling_row, optical, occupation, shifts):
    lesser = padded[0]
    greater = padded[1]

    def energy_view(source, offset):
        return lax.dynamic_slice_in_dim(source, margin + offset, length, axis=source.ndim - 1)

    sigma_less = coupling_row[:, None] * energy_view(lesser, 0)
    sigma_more = coupling_row[:, None] * energy_view(greater, 0)
    for column in range(2):
        strength = optical[column]
        number = occupation[column]
        offset = shifts[column]
        sigma_less = sigma_less + strength * (
            (number + 1.0) * energy_view(lesser, offset) + number * energy_view(lesser, -offset)
        )
        sigma_more = sigma_more + strength * (
            (number + 1.0) * energy_view(greater, -offset) + number * energy_view(greater, offset)
        )
    return jnp.stack([sigma_less, sigma_more])


def _pick(mask, x, axis):
    return jnp.sum(jnp.where(mask, x, 0.0), axis=axis, keepdims=True)


def _weights_from_products(prod):
    size_n = HIST
    row = lax.broadcasted_iota(jnp.int32, prod.shape, 0)
    col = lax.broadcasted_iota(jnp.int32, prod.shape, 1)
    rows, cols = prod.shape
    down = pltpu.roll(prod, rows - 1, 0)
    right = pltpu.roll(prod, cols - 1, 1)
    diag = pltpu.roll(down, cols - 1, 1)
    inside = (row < size_n) & (col < size_n)
    system = jnp.where(inside, prod - right - down + diag, 0.0)
    target = _pick((col == 0) & (row < size_n), prod - down, 1)
    eye = inside & (row == col)
    trace = jnp.sum(jnp.where(eye, system, 0.0), keepdims=True)
    ridge = ridge_share * trace / size_n + 1e-06
    a = system + jnp.where(eye, ridge, 0.0)
    lower = jnp.zeros_like(a)
    upper = jnp.zeros_like(a)
    for j in range(size_n):
        pivot = jnp.sqrt(_pick((row == j) & (col == j), a, None).reshape(1, 1))
        lcol = jnp.where(row[:, :1] >= j, _pick(col == j, a, 1) / pivot, 0.0)
        lrow = jnp.where(col[:1, :] >= j, _pick(row == j, a, 0) / pivot, 0.0)
        lower = lower + jnp.where(col == j, lcol, 0.0)
        upper = upper + jnp.where(row == j, lrow, 0.0)
        a = a - lcol * lrow
    row1 = row[:, :1]
    rest = target
    forward = jnp.zeros_like(target)
    for i in range(size_n):
        lii = _pick((row == i) & (col == i), lower, None).reshape(1, 1)
        yi = _pick(row1 == i, rest, 0) / lii
        forward = forward + jnp.where(row1 == i, yi, 0.0)
        rest = rest - jnp.where(row1 > i, _pick(col == i, lower, 1), 0.0) * yi
    rest = forward
    gamma = jnp.zeros_like(target)
    for i in range(size_n - 1, -1, -1):
        lii = _pick((row == i) & (col == i), lower, None).reshape(1, 1)
        gi = _pick(row1 == i, rest, 0) / lii
        gamma = gamma + jnp.where(row1 == i, gi, 0.0)
        rest = rest - jnp.where(row1 < i, _pick(col == i, upper, 1), 0.0) * gi
    before = pltpu.roll(gamma, 1, 0)
    weights = jnp.where(row1 == 0, 1.0, 0.0) - gamma + before
    return jnp.broadcast_to(weights, prod.shape)


def _permute_square(prod, perm):
    row = lax.broadcasted_iota(jnp.int32, prod.shape, 0)
    col = lax.broadcasted_iota(jnp.int32, prod.shape, 1)
    count = len(perm)
    permcol = jnp.zeros((prod.shape[0], 1), jnp.int32)
    permrow = jnp.zeros((1, prod.shape[1]), jnp.int32)
    for i in range(count):
        permcol = jnp.where(row[:, :1] == i, perm[i], permcol)
        permrow = jnp.where(col[:1, :] == i, perm[i], permrow)
    by_rows = jnp.zeros_like(prod)
    for m in range(count):
        by_rows = by_rows + jnp.where(permcol == m, _pick(row == m, prod, 0), 0.0)
    by_rows = jnp.where(row < count, by_rows, 0.0)
    both = jnp.zeros_like(prod)
    for m in range(count):
        both = both + jnp.where(permrow == m, _pick(col == m, by_rows, 1), 0.0)
    return jnp.where(col < count, both, 0.0)


def _pair_sums(vectors, pairs):
    shape = (8, 128)
    row = lax.broadcasted_iota(jnp.int32, shape, 0)
    col = lax.broadcasted_iota(jnp.int32, shape, 1)
    prod = jnp.zeros(shape, jnp.float32)
    for i, j in pairs:
        value = jnp.sum(vectors[i] * vectors[j], keepdims=True)
        spot = ((row == i) & (col == j)) | ((row == j) & (col == i))
        prod = jnp.where(spot, value, prod)
    return prod


def _pack_rows(prod):
    row = lax.broadcasted_iota(jnp.int32, prod.shape, 0)
    packed = jnp.zeros((1, prod.shape[1]), jnp.float32)
    for i in range(HIST + 1):
        packed = packed + pltpu.roll(_pick(row == i, prod, 0), 8 * i, 1)
    return packed


def _unpack_rows(packed):
    shape = (8, packed.shape[1])
    row = lax.broadcasted_iota(jnp.int32, shape, 0)
    col = lax.broadcasted_iota(jnp.int32, shape, 1)
    prod = jnp.zeros(shape, jnp.float32)
    for i in range(HIST + 1):
        line = pltpu.roll(packed, (shape[1] - 8 * i) % shape[1], 1)
        prod = jnp.where((row == i) & (col <= HIST), line, prod)
    return prod


def _fused_kernel(nk, ne, entries, margin,
                  slot_ref, shift_ref, class_ref, optical_ref, occ_ref, acoustic_ref,
                  chunk_ref, cur_ref, pin_ref, pres_ref, out_ref,
                  ypad, send1, recv1, recv2, acc1, ts, tr, ss1, rs1, ss2, rs2):
    mk = lax.axis_index("kgrp")
    me = lax.axis_index("energy")
    width = chunk_ref.shape[-1]
    rows, padded_len = ypad.shape
    length = padded_len - 2 * margin
    barrier = pltpu.get_barrier_semaphore()
    for s in range(nk - 1):
        pl.semaphore_signal(barrier, 1, device_id=((mk + s + 1) % nk, me), device_id_type=MESH)
    for s in range(ne - 1):
        pl.semaphore_signal(barrier, 1, device_id=(mk, (me + s + 1) % ne), device_id_type=MESH)
    ypad[:, :margin] = jnp.zeros((rows, margin), jnp.float32)
    ypad[:, margin + length :] = jnp.zeros((rows, margin), jnp.float32)
    ypad[:, pl.ds(pl.multiple_of(margin + me * width, width), width)] = chunk_ref[me]
    pl.semaphore_wait(barrier, nk - 1 + ne - 1)

    copies = []
    for s in range(ne - 1):
        peer = (me + s + 1) % ne
        c = pltpu.make_async_remote_copy(
            src_ref=chunk_ref.at[peer],
            dst_ref=ypad.at[:, pl.ds(pl.multiple_of(margin + me * width, width), width)],
            send_sem=ts.at[s],
            recv_sem=tr.at[ne - 2 - s],
            device_id=(mk, peer),
            device_id_type=MESH,
        )
        c.start()
        copies.append(c)
    history = [pres_ref[m] for m in range(HIST)]
    gram = _pair_sums([None] + history, [(i, j) for i in range(1, HIST + 1) for j in range(i, HIST + 1)])
    for q in range(ne - 1):
        source = (me + q + 1) % ne
        pltpu.make_async_remote_copy(
            src_ref=chunk_ref.at[me],
            dst_ref=ypad.at[:, pl.ds(pl.multiple_of(margin + source * width, width), width)],
            send_sem=ts.at[q],
            recv_sem=tr.at[q],
            device_id=(mk, source),
            device_id_type=MESH,
        ).wait_recv()
    for s in range(ne - 1):
        copies[s].wait_send()

    y = ypad[...]
    row = lax.broadcasted_iota(jnp.int32, (rows, 1), 0)
    lesser = row < rows // 2
    per_row = rows // 8
    coupling = jnp.zeros((rows, 1), jnp.float32)
    for r in range(per_row):
        coupling = jnp.where(row % per_row == r, acoustic_ref[class_ref[me * per_row + r]], coupling)
    sigma = coupling * y[:, margin : margin + length]
    for m in range(2):
        shift = shift_ref[m]
        strength = optical_ref[m]
        number = occ_ref[m]
        ahead = pltpu.roll(y, padded_len - shift, 1)[:, margin : margin + length]
        behind = pltpu.roll(y, shift, 1)[:, margin : margin + length]
        up = jnp.where(lesser, number + 1.0, number)
        down = jnp.where(lesser, number, number + 1.0)
        sigma = sigma + strength * (up * ahead + down * behind)
    res = sigma - cur_ref[...]
    fresh = _pair_sums([res] + history, [(0, j) for j in range(HIST + 1)])
    send1[...] = _pack_rows(fresh + gram)

    def exchange(src, recv, ssem, rsem, count, peer):
        out = []
        for s in range(count - 1):
            c = pltpu.make_async_remote_copy(
                src_ref=src,
                dst_ref=recv.at[count - 2 - s],
                send_sem=ssem.at[s],
                recv_sem=rsem.at[count - 2 - s],
                device_id=peer(s),
                device_id_type=MESH,
            )
            c.start()
            out.append(c)
        for s in range(count - 1):
            out[s].wait_recv()
        for s in range(count - 1):
            out[s].wait_send()

    def total(own, recv, mine, count):
        acc = jnp.zeros_like(own)
        for idx in range(count):
            slot = jnp.minimum((idx - mine - 1 + count) % count, count - 2)
            acc = acc + jnp.where(idx == mine, own, recv[slot])
        return acc

    exchange(send1, recv1, ss1, rs1, nk, lambda s: ((mk + s + 1) % nk, me))
    acc1[...] = total(send1[...], recv1, mk, nk)
    exchange(acc1, recv2, ss2, rs2, ne, lambda s: (mk, (me + s + 1) % ne))
    summed = _unpack_rows(total(acc1[...], recv2, me, ne))
    perm = [0] + [slot_ref[i] + 1 for i in range(HIST)]
    aged = _permute_square(summed / entries, perm)
    weights = _weights_from_products(aged)[:, :1]
    row1 = lax.broadcasted_iota(jnp.int32, weights.shape, 0)
    slot_w = [None] * (HIST + 1)
    for i in range(HIST + 1):
        w_i = _pick(row1 == i, weights, 0)
        for m in range(HIST + 1):
            term = jnp.where(perm[i] == m, w_i, 0.0)
            slot_w[m] = term if slot_w[m] is None else slot_w[m] + term
    mixed = slot_w[0] * (cur_ref[...] + mixing_share * res)
    for m in range(HIST):
        mixed = mixed + slot_w[m + 1] * (pin_ref[m] + mixing_share * pres_ref[m])
    out_ref[...] = mixed


def fused_tail(scalars, chunks, cur, pin, pres, nk, ne, entries):
    tile = (1, 128)
    margin = 128
    rows = chunks.shape[1]
    smem = pl.BlockSpec(memory_space=pltpu.SMEM)
    vmem = pl.BlockSpec(memory_space=pltpu.VMEM)
    return pl.pallas_call(
        functools.partial(_fused_kernel, nk, ne, entries, margin),
        out_shape=jax.ShapeDtypeStruct(cur.shape, jnp.float32),
        in_specs=[smem] * len(scalars) + [vmem] * 4,
        out_specs=vmem,
        scratch_shapes=[
            pltpu.VMEM((rows, cur.shape[1] + 2 * margin), jnp.float32),
            pltpu.VMEM(tile, jnp.float32),
            pltpu.VMEM((nk - 1,) + tile, jnp.float32),
            pltpu.VMEM((ne - 1,) + tile, jnp.float32),
            pltpu.VMEM(tile, jnp.float32),
            pltpu.SemaphoreType.DMA((ne - 1,)),
            pltpu.SemaphoreType.DMA((ne - 1,)),
            pltpu.SemaphoreType.DMA((nk - 1,)),
            pltpu.SemaphoreType.DMA((nk - 1,)),
            pltpu.SemaphoreType.DMA((ne - 1,)),
            pltpu.SemaphoreType.DMA((ne - 1,)),
        ],
        compiler_params=pltpu.CompilerParams(collective_id=0, has_side_effects=True),
    )(*scalars, chunks, cur, pin, pres)


def per_device(
    greens,
    current,
    past_inputs,
    past_residuals,
    slot_order,
    neighbour,
    momentum_class,
    stencil_weight,
    acoustic_coupling,
    optical_coupling,
    occupation,
    phonon_shift,
):
    group_len = greens.shape[3]
    rows_here = current.shape[3]
    group_id = lax.axis_index("kgrp")
    energy_id = lax.axis_index("energy")
    nk = lax.axis_size("kgrp")
    ne = lax.axis_size("energy")
    total_k = group_len * nk
    ends = padded_2(greens, (("kgrp", 3),), group_len, True)
    low = ends[:, :, :, :group_len]
    high = ends[:, :, :, 2 * group_len :]
    local_index = (neighbour - group_id * group_len + group_len) % total_k
    stencil = jnp.sum(
        jnp.where(
            local_index[:, :, None] == jnp.arange(3 * group_len, dtype=jnp.int32)[None, None, :],
            stencil_weight[None, :, None],
            0.0,
        ),
        axis=1,
    )
    lead = greens.shape[:3]
    flat = lambda x: x.reshape((-1,) + x.shape[3:])
    stencil = stencil.reshape(ne, rows_here, 3 * group_len)
    chunks = jnp.zeros((ne, flat(greens).shape[0], rows_here, greens.shape[4]), jnp.float32)
    for part, block in enumerate((low, greens, high)):
        chunks = chunks + jnp.einsum(
            "dkr,bre->dbke",
            stencil[:, :, part * group_len : (part + 1) * group_len],
            flat(block),
            precision=lax.Precision.HIGHEST,
        )
    chunks = chunks.reshape(ne, -1, greens.shape[4])
    lanes = current.shape[-1]
    entries = float(current.size * nk * ne)
    scalars = (slot_order, phonon_shift, momentum_class, optical_coupling, occupation, acoustic_coupling)
    mixed = fused_tail(
        scalars,
        chunks,
        current.reshape(-1, lanes),
        past_inputs.reshape(HIST, -1, lanes),
        past_residuals.reshape(HIST, -1, lanes),
        nk,
        ne,
        entries,
    ).reshape(current.shape)
    return mixed


def solution(mesh):
    return jax.shard_map(
        per_device,
        mesh=mesh,
        in_specs=(
            P(None, None, None, "kgrp", "energy"),
            P(None, None, None, ("kgrp", "energy"), None),
            P(None, None, None, None, ("kgrp", "energy"), None),
            P(None, None, None, None, ("kgrp", "energy"), None),
            P(),
            P("kgrp", None),
            P("kgrp"),
            P(),
            P(),
            P(),
            P(),
            P(),
        ),
        out_specs=P(None, None, None, ("kgrp", "energy"), None),
        check_vma=False,
    )
```

```python
import functools

import jax
import jax.numpy as jnp
from jax import lax
from jax.experimental import pallas as pl
from jax.experimental.pallas import tpu as pltpu
from jax.sharding import PartitionSpec as P

SHIFT_MAX = 96
HIST = 5

mixing_share = 0.5
ridge_share = 0.1

MESH = pl.DeviceIdType.MESH


def padded_2(block, sides, width, periodic):
    for axis, dim in sides:
        count = lax.axis_size(axis)
        forward = [(i, i + 1) for i in range(count - 1)]
        if periodic:
            forward.append((count - 1, 0))
        backward = [(target, source) for source, target in forward]
        low = lax.ppermute(
            lax.slice_in_dim(block, block.shape[dim] - width, None, axis=dim), axis, forward
        )
        high = lax.ppermute(lax.slice_in_dim(block, 0, width, axis=dim), axis, backward)
        block = jnp.concatenate([low, block, high], axis=dim)
    return block


def emit(padded, margin, length, coupling_row, optical, occupation, shifts):
    lesser = padded[0]
    greater = padded[1]

    def energy_view(source, offset):
        return lax.dynamic_slice_in_dim(source, margin + offset, length, axis=source.ndim - 1)

    sigma_less = coupling_row[:, None] * energy_view(lesser, 0)
    sigma_more = coupling_row[:, None] * energy_view(greater, 0)
    for column in range(2):
        strength = optical[column]
        number = occupation[column]
        offset = shifts[column]
        sigma_less = sigma_less + strength * (
            (number + 1.0) * energy_view(lesser, offset) + number * energy_view(lesser, -offset)
        )
        sigma_more = sigma_more + strength * (
            (number + 1.0) * energy_view(greater, -offset) + number * energy_view(greater, offset)
        )
    return jnp.stack([sigma_less, sigma_more])


def _pick(mask, x, axis):
    return jnp.sum(jnp.where(mask, x, 0.0), axis=axis, keepdims=True)


def _weights_from_products(prod):
    size_n = HIST
    row = lax.broadcasted_iota(jnp.int32, prod.shape, 0)
    col = lax.broadcasted_iota(jnp.int32, prod.shape, 1)
    rows, cols = prod.shape
    down = pltpu.roll(prod, rows - 1, 0)
    right = pltpu.roll(prod, cols - 1, 1)
    diag = pltpu.roll(down, cols - 1, 1)
    inside = (row < size_n) & (col < size_n)
    system = jnp.where(inside, prod - right - down + diag, 0.0)
    target = _pick((col == 0) & (row < size_n), prod - down, 1)
    eye = inside & (row == col)
    trace = jnp.sum(jnp.where(eye, system, 0.0), keepdims=True)
    ridge = ridge_share * trace / size_n + 1e-06
    a = system + jnp.where(eye, ridge, 0.0)
    lower = jnp.zeros_like(a)
    upper = jnp.zeros_like(a)
    for j in range(size_n):
        pivot = jnp.sqrt(_pick((row == j) & (col == j), a, None).reshape(1, 1))
        lcol = jnp.where(row[:, :1] >= j, _pick(col == j, a, 1) / pivot, 0.0)
        lrow = jnp.where(col[:1, :] >= j, _pick(row == j, a, 0) / pivot, 0.0)
        lower = lower + jnp.where(col == j, lcol, 0.0)
        upper = upper + jnp.where(row == j, lrow, 0.0)
        a = a - lcol * lrow
    row1 = row[:, :1]
    rest = target
    forward = jnp.zeros_like(target)
    for i in range(size_n):
        lii = _pick((row == i) & (col == i), lower, None).reshape(1, 1)
        yi = _pick(row1 == i, rest, 0) / lii
        forward = forward + jnp.where(row1 == i, yi, 0.0)
        rest = rest - jnp.where(row1 > i, _pick(col == i, lower, 1), 0.0) * yi
    rest = forward
    gamma = jnp.zeros_like(target)
    for i in range(size_n - 1, -1, -1):
        lii = _pick((row == i) & (col == i), lower, None).reshape(1, 1)
        gi = _pick(row1 == i, rest, 0) / lii
        gamma = gamma + jnp.where(row1 == i, gi, 0.0)
        rest = rest - jnp.where(row1 < i, _pick(col == i, upper, 1), 0.0) * gi
    before = pltpu.roll(gamma, 1, 0)
    weights = jnp.where(row1 == 0, 1.0, 0.0) - gamma + before
    return jnp.broadcast_to(weights, prod.shape)


def _permute_square(prod, perm):
    row = lax.broadcasted_iota(jnp.int32, prod.shape, 0)
    col = lax.broadcasted_iota(jnp.int32, prod.shape, 1)
    count = len(perm)
    permcol = jnp.zeros((prod.shape[0], 1), jnp.int32)
    permrow = jnp.zeros((1, prod.shape[1]), jnp.int32)
    for i in range(count):
        permcol = jnp.where(row[:, :1] == i, perm[i], permcol)
        permrow = jnp.where(col[:1, :] == i, perm[i], permrow)
    by_rows = jnp.zeros_like(prod)
    for m in range(count):
        by_rows = by_rows + jnp.where(permcol == m, _pick(row == m, prod, 0), 0.0)
    by_rows = jnp.where(row < count, by_rows, 0.0)
    both = jnp.zeros_like(prod)
    for m in range(count):
        both = both + jnp.where(permrow == m, _pick(col == m, by_rows, 1), 0.0)
    return jnp.where(col < count, both, 0.0)


def _pair_sums(vectors, pairs):
    shape = (8, 128)
    row = lax.broadcasted_iota(jnp.int32, shape, 0)
    col = lax.broadcasted_iota(jnp.int32, shape, 1)
    prod = jnp.zeros(shape, jnp.float32)
    for i, j in pairs:
        value = jnp.sum(vectors[i] * vectors[j], keepdims=True)
        spot = ((row == i) & (col == j)) | ((row == j) & (col == i))
        prod = jnp.where(spot, value, prod)
    return prod


def _pack_rows(prod):
    row = lax.broadcasted_iota(jnp.int32, prod.shape, 0)
    packed = jnp.zeros((1, prod.shape[1]), jnp.float32)
    for i in range(HIST + 1):
        packed = packed + pltpu.roll(_pick(row == i, prod, 0), 8 * i, 1)
    return packed


def _unpack_rows(packed):
    shape = (8, packed.shape[1])
    row = lax.broadcasted_iota(jnp.int32, shape, 0)
    col = lax.broadcasted_iota(jnp.int32, shape, 1)
    prod = jnp.zeros(shape, jnp.float32)
    for i in range(HIST + 1):
        line = pltpu.roll(packed, (shape[1] - 8 * i) % shape[1], 1)
        prod = jnp.where((row == i) & (col <= HIST), line, prod)
    return prod


def _fused_kernel(nk, ne, entries, margin,
                  slot_ref, shift_ref, class_ref, optical_ref, occ_ref, acoustic_ref,
                  chunk_ref, cur_ref, pin_ref, pres_ref, out_ref,
                  ypad, bases, send1, recv1, recv2, acc1, ts, tr, ss1, rs1, ss2, rs2):
    mk = lax.axis_index("kgrp")
    me = lax.axis_index("energy")
    width = chunk_ref.shape[-1]
    rows, padded_len = ypad.shape
    length = padded_len - 2 * margin
    barrier = pltpu.get_barrier_semaphore()
    for s in range(nk - 1):
        pl.semaphore_signal(barrier, 1, device_id=((mk + s + 1) % nk, me), device_id_type=MESH)
    for s in range(ne - 1):
        pl.semaphore_signal(barrier, 1, device_id=(mk, (me + s + 1) % ne), device_id_type=MESH)
    ypad[:, :margin] = jnp.zeros((rows, margin), jnp.float32)
    ypad[:, margin + length :] = jnp.zeros((rows, margin), jnp.float32)
    ypad[:, pl.ds(pl.multiple_of(margin + me * width, width), width)] = chunk_ref[me]
    pl.semaphore_wait(barrier, nk - 1 + ne - 1)

    copies = []
    for s in range(ne - 1):
        peer = (me + s + 1) % ne
        c = pltpu.make_async_remote_copy(
            src_ref=chunk_ref.at[peer],
            dst_ref=ypad.at[:, pl.ds(pl.multiple_of(margin + me * width, width), width)],
            send_sem=ts.at[s],
            recv_sem=tr.at[ne - 2 - s],
            device_id=(mk, peer),
            device_id_type=MESH,
        )
        c.start()
        copies.append(c)
    history = [pres_ref[m] for m in range(HIST)]
    gram = _pair_sums([None] + history, [(i, j) for i in range(1, HIST + 1) for j in range(i, HIST + 1)])
    for q in range(ne - 1):
        source = (me + q + 1) % ne
        pltpu.make_async_remote_copy(
            src_ref=chunk_ref.at[me],
            dst_ref=ypad.at[:, pl.ds(pl.multiple_of(margin + source * width, width), width)],
            send_sem=ts.at[q],
            recv_sem=tr.at[q],
            device_id=(mk, source),
            device_id_type=MESH,
        ).wait_recv()
    for s in range(ne - 1):
        copies[s].wait_send()

    y = ypad[...]
    row = lax.broadcasted_iota(jnp.int32, (rows, 1), 0)
    lesser = row < rows // 2
    per_row = rows // 8
    coupling = jnp.zeros((rows, 1), jnp.float32)
    for r in range(per_row):
        coupling = jnp.where(row % per_row == r, acoustic_ref[class_ref[me * per_row + r]], coupling)
    sigma = coupling * y[:, margin : margin + length]
    for m in range(2):
        shift = shift_ref[m]
        strength = optical_ref[m]
        number = occ_ref[m]
        ahead = pltpu.roll(y, padded_len - shift, 1)[:, margin : margin + length]
        behind = pltpu.roll(y, shift, 1)[:, margin : margin + length]
        up = jnp.where(lesser, number + 1.0, number)
        down = jnp.where(lesser, number, number + 1.0)
        sigma = sigma + strength * (up * ahead + down * behind)
    res = sigma - cur_ref[...]
    fresh = _pair_sums([res] + history, [(0, j) for j in range(HIST + 1)])
    send1[...] = _pack_rows(fresh + gram)

    def exchange(src, recv, ssem, rsem, count, peer):
        out = []
        for s in range(count - 1):
            c = pltpu.make_async_remote_copy(
                src_ref=src,
                dst_ref=recv.at[count - 2 - s],
                send_sem=ssem.at[s],
                recv_sem=rsem.at[count - 2 - s],
                device_id=peer(s),
                device_id_type=MESH,
            )
            c.start()
            out.append(c)
        return out

    def finish(out):
        for c in out:
            c.wait_recv()
        for c in out:
            c.wait_send()

    def total(own, recv, mine, count):
        acc = jnp.zeros_like(own)
        for idx in range(count):
            slot = jnp.minimum((idx - mine - 1 + count) % count, count - 2)
            acc = acc + jnp.where(idx == mine, own, recv[slot])
        return acc

    pending = exchange(send1, recv1, ss1, rs1, nk, lambda s: ((mk + s + 1) % nk, me))
    lead = pin_ref.shape[0] // HIST
    for m in range(HIST):
        bases[m] = pin_ref[m * lead : (m + 1) * lead].reshape(rows, length) + mixing_share * history[m]
    finish(pending)
    acc1[...] = total(send1[...], recv1, mk, nk)
    finish(exchange(acc1, recv2, ss2, rs2, ne, lambda s: (mk, (me + s + 1) % ne)))
    summed = _unpack_rows(total(acc1[...], recv2, me, ne))
    perm = [0] + [slot_ref[i] + 1 for i in range(HIST)]
    aged = _permute_square(summed / entries, perm)
    weights = _weights_from_products(aged)[:, :1]
    row1 = lax.broadcasted_iota(jnp.int32, weights.shape, 0)
    slot_w = [None] * (HIST + 1)
    for i in range(HIST + 1):
        w_i = _pick(row1 == i, weights, 0)
        for m in range(HIST + 1):
            term = jnp.where(perm[i] == m, w_i, 0.0)
            slot_w[m] = term if slot_w[m] is None else slot_w[m] + term
    mixed = slot_w[0] * (cur_ref[...] + mixing_share * res)
    for m in range(HIST):
        mixed = mixed + slot_w[m + 1] * bases[m]
    out_ref[...] = mixed


def fused_tail(scalars, chunks, cur, pin, pres, nk, ne, entries):
    tile = (1, 128)
    margin = 128
    rows = chunks.shape[1]
    smem = pl.BlockSpec(memory_space=pltpu.SMEM)
    vmem = pl.BlockSpec(memory_space=pltpu.VMEM)
    return pl.pallas_call(
        functools.partial(_fused_kernel, nk, ne, entries, margin),
        out_shape=jax.ShapeDtypeStruct(cur.shape, jnp.float32),
        in_specs=[smem] * len(scalars) + [vmem] * 4,
        out_specs=vmem,
        scratch_shapes=[
            pltpu.VMEM((rows, cur.shape[1] + 2 * margin), jnp.float32),
            pltpu.VMEM((HIST,) + cur.shape, jnp.float32),
            pltpu.VMEM(tile, jnp.float32),
            pltpu.VMEM((nk - 1,) + tile, jnp.float32),
            pltpu.VMEM((ne - 1,) + tile, jnp.float32),
            pltpu.VMEM(tile, jnp.float32),
            pltpu.SemaphoreType.DMA((ne - 1,)),
            pltpu.SemaphoreType.DMA((ne - 1,)),
            pltpu.SemaphoreType.DMA((nk - 1,)),
            pltpu.SemaphoreType.DMA((nk - 1,)),
            pltpu.SemaphoreType.DMA((ne - 1,)),
            pltpu.SemaphoreType.DMA((ne - 1,)),
        ],
        compiler_params=pltpu.CompilerParams(collective_id=0, has_side_effects=True),
    )(*scalars, chunks, cur, pin, pres)


def per_device(
    greens,
    current,
    past_inputs,
    past_residuals,
    slot_order,
    neighbour,
    momentum_class,
    stencil_weight,
    acoustic_coupling,
    optical_coupling,
    occupation,
    phonon_shift,
):
    group_len = greens.shape[3]
    rows_here = current.shape[3]
    group_id = lax.axis_index("kgrp")
    energy_id = lax.axis_index("energy")
    nk = lax.axis_size("kgrp")
    ne = lax.axis_size("energy")
    total_k = group_len * nk
    ends = padded_2(greens, (("kgrp", 3),), group_len, True)
    low = ends[:, :, :, :group_len]
    high = ends[:, :, :, 2 * group_len :]
    local_index = (neighbour - group_id * group_len + group_len) % total_k
    stencil = jnp.sum(
        jnp.where(
            local_index[:, :, None] == jnp.arange(3 * group_len, dtype=jnp.int32)[None, None, :],
            stencil_weight[None, :, None],
            0.0,
        ),
        axis=1,
    )
    lead = greens.shape[:3]
    flat = lambda x: x.reshape((-1,) + x.shape[3:])
    stencil = stencil.reshape(ne, rows_here, 3 * group_len)
    chunks = jnp.zeros((ne, flat(greens).shape[0], rows_here, greens.shape[4]), jnp.float32)
    for part, block in enumerate((low, greens, high)):
        chunks = chunks + jnp.einsum(
            "dkr,bre->dbke",
            stencil[:, :, part * group_len : (part + 1) * group_len],
            flat(block),
            precision=lax.Precision.HIGHEST,
        )
    chunks = chunks.reshape(ne, -1, greens.shape[4])
    lanes = current.shape[-1]
    entries = float(current.size * nk * ne)
    scalars = (slot_order, phonon_shift, momentum_class, optical_coupling, occupation, acoustic_coupling)
    mixed = fused_tail(
        scalars,
        chunks,
        current.reshape(-1, lanes),
        past_inputs.reshape(-1, rows_here, lanes),
        past_residuals.reshape(HIST, -1, lanes),
        nk,
        ne,
        entries,
    ).reshape(current.shape)
    return mixed


def solution(mesh):
    return jax.shard_map(
        per_device,
        mesh=mesh,
        in_specs=(
            P(None, None, None, "kgrp", "energy"),
            P(None, None, None, ("kgrp", "energy"), None),
            P(None, None, None, None, ("kgrp", "energy"), None),
            P(None, None, None, None, ("kgrp", "energy"), None),
            P(),
            P("kgrp", None),
            P("kgrp"),
            P(),
            P(),
            P(),
            P(),
            P(),
        ),
        out_specs=P(None, None, None, ("kgrp", "energy"), None),
        check_vma=False,
    )
```

```python
import functools

import jax
import jax.numpy as jnp
from jax import lax
from jax.experimental import pallas as pl
from jax.experimental.pallas import tpu as pltpu
from jax.sharding import PartitionSpec as P

SHIFT_MAX = 96
HIST = 5

mixing_share = 0.5
ridge_share = 0.1

MESH = pl.DeviceIdType.MESH


def padded_2(block, sides, width, periodic):
    for axis, dim in sides:
        count = lax.axis_size(axis)
        forward = [(i, i + 1) for i in range(count - 1)]
        if periodic:
            forward.append((count - 1, 0))
        backward = [(target, source) for source, target in forward]
        low = lax.ppermute(
            lax.slice_in_dim(block, block.shape[dim] - width, None, axis=dim), axis, forward
        )
        high = lax.ppermute(lax.slice_in_dim(block, 0, width, axis=dim), axis, backward)
        block = jnp.concatenate([low, block, high], axis=dim)
    return block


def emit(padded, margin, length, coupling_row, optical, occupation, shifts):
    lesser = padded[0]
    greater = padded[1]

    def energy_view(source, offset):
        return lax.dynamic_slice_in_dim(source, margin + offset, length, axis=source.ndim - 1)

    sigma_less = coupling_row[:, None] * energy_view(lesser, 0)
    sigma_more = coupling_row[:, None] * energy_view(greater, 0)
    for column in range(2):
        strength = optical[column]
        number = occupation[column]
        offset = shifts[column]
        sigma_less = sigma_less + strength * (
            (number + 1.0) * energy_view(lesser, offset) + number * energy_view(lesser, -offset)
        )
        sigma_more = sigma_more + strength * (
            (number + 1.0) * energy_view(greater, -offset) + number * energy_view(greater, offset)
        )
    return jnp.stack([sigma_less, sigma_more])


def _pick(mask, x, axis):
    return jnp.sum(jnp.where(mask, x, 0.0), axis=axis, keepdims=True)


def _weights_from_products(prod):
    size_n = HIST
    row = lax.broadcasted_iota(jnp.int32, prod.shape, 0)
    col = lax.broadcasted_iota(jnp.int32, prod.shape, 1)
    rows, cols = prod.shape
    down = pltpu.roll(prod, rows - 1, 0)
    right = pltpu.roll(prod, cols - 1, 1)
    diag = pltpu.roll(down, cols - 1, 1)
    inside = (row < size_n) & (col < size_n)
    system = jnp.where(inside, prod - right - down + diag, 0.0)
    target = _pick((col == 0) & (row < size_n), prod - down, 1)
    eye = inside & (row == col)
    trace = jnp.sum(jnp.where(eye, system, 0.0), keepdims=True)
    ridge = ridge_share * trace / size_n + 1e-06
    a = system + jnp.where(eye, ridge, 0.0)
    lower = jnp.zeros_like(a)
    upper = jnp.zeros_like(a)
    diagonal = []
    for j in range(size_n):
        head = _pick((row == j) & (col == j), a, None).reshape(1, 1)
        pivot = jnp.sqrt(head)
        diagonal.append(head / pivot)
        lcol = jnp.where(row[:, :1] >= j, _pick(col == j, a, 1) / pivot, 0.0)
        lrow = jnp.where(col[:1, :] >= j, _pick(row == j, a, 0) / pivot, 0.0)
        lower = lower + jnp.where(col == j, lcol, 0.0)
        upper = upper + jnp.where(row == j, lrow, 0.0)
        a = a - lcol * lrow
    row1 = row[:, :1]
    rest = target
    forward = jnp.zeros_like(target)
    for i in range(size_n):
        lii = diagonal[i]
        yi = _pick(row1 == i, rest, 0) / lii
        forward = forward + jnp.where(row1 == i, yi, 0.0)
        rest = rest - jnp.where(row1 > i, _pick(col == i, lower, 1), 0.0) * yi
    rest = forward
    gamma = jnp.zeros_like(target)
    for i in range(size_n - 1, -1, -1):
        lii = diagonal[i]
        gi = _pick(row1 == i, rest, 0) / lii
        gamma = gamma + jnp.where(row1 == i, gi, 0.0)
        rest = rest - jnp.where(row1 < i, _pick(col == i, upper, 1), 0.0) * gi
    before = pltpu.roll(gamma, 1, 0)
    weights = jnp.where(row1 == 0, 1.0, 0.0) - gamma + before
    return jnp.broadcast_to(weights, prod.shape)


def _permute_square(prod, perm):
    row = lax.broadcasted_iota(jnp.int32, prod.shape, 0)
    col = lax.broadcasted_iota(jnp.int32, prod.shape, 1)
    count = len(perm)
    permcol = jnp.zeros((prod.shape[0], 1), jnp.int32)
    permrow = jnp.zeros((1, prod.shape[1]), jnp.int32)
    for i in range(count):
        permcol = jnp.where(row[:, :1] == i, perm[i], permcol)
        permrow = jnp.where(col[:1, :] == i, perm[i], permrow)
    by_rows = jnp.zeros_like(prod)
    for m in range(count):
        by_rows = by_rows + jnp.where(permcol == m, _pick(row == m, prod, 0), 0.0)
    by_rows = jnp.where(row < count, by_rows, 0.0)
    both = jnp.zeros_like(prod)
    for m in range(count):
        both = both + jnp.where(permrow == m, _pick(col == m, by_rows, 1), 0.0)
    return jnp.where(col < count, both, 0.0)


def _pair_sums(vectors, pairs):
    shape = (8, 128)
    row = lax.broadcasted_iota(jnp.int32, shape, 0)
    col = lax.broadcasted_iota(jnp.int32, shape, 1)
    prod = jnp.zeros(shape, jnp.float32)
    for i, j in pairs:
        value = jnp.sum(vectors[i] * vectors[j], keepdims=True)
        spot = ((row == i) & (col == j)) | ((row == j) & (col == i))
        prod = jnp.where(spot, value, prod)
    return prod


def _pack_rows(prod):
    row = lax.broadcasted_iota(jnp.int32, prod.shape, 0)
    packed = jnp.zeros((1, prod.shape[1]), jnp.float32)
    for i in range(HIST + 1):
        packed = packed + pltpu.roll(_pick(row == i, prod, 0), 8 * i, 1)
    return packed


def _unpack_rows(packed):
    shape = (8, packed.shape[1])
    row = lax.broadcasted_iota(jnp.int32, shape, 0)
    col = lax.broadcasted_iota(jnp.int32, shape, 1)
    prod = jnp.zeros(shape, jnp.float32)
    for i in range(HIST + 1):
        line = pltpu.roll(packed, (shape[1] - 8 * i) % shape[1], 1)
        prod = jnp.where((row == i) & (col <= HIST), line, prod)
    return prod


def _fused_kernel(nk, ne, entries, margin,
                  slot_ref, shift_ref, class_ref, optical_ref, occ_ref, acoustic_ref,
                  chunk_ref, cur_ref, pin_ref, pres_ref, out_ref,
                  ypad, bases, send1, recv1, recv2, acc1, ts, tr, ss1, rs1, ss2, rs2):
    mk = lax.axis_index("kgrp")
    me = lax.axis_index("energy")
    width = chunk_ref.shape[-1]
    rows, padded_len = ypad.shape
    length = padded_len - 2 * margin
    barrier = pltpu.get_barrier_semaphore()
    for s in range(nk - 1):
        pl.semaphore_signal(barrier, 1, device_id=((mk + s + 1) % nk, me), device_id_type=MESH)
    for s in range(ne - 1):
        pl.semaphore_signal(barrier, 1, device_id=(mk, (me + s + 1) % ne), device_id_type=MESH)
    ypad[:, :margin] = jnp.zeros((rows, margin), jnp.float32)
    ypad[:, margin + length :] = jnp.zeros((rows, margin), jnp.float32)
    ypad[:, pl.ds(pl.multiple_of(margin + me * width, width), width)] = chunk_ref[:, me, :]
    pl.semaphore_wait(barrier, nk - 1 + ne - 1)

    copies = []
    for s in range(ne - 1):
        peer = (me + s + 1) % ne
        c = pltpu.make_async_remote_copy(
            src_ref=chunk_ref.at[:, peer, :],
            dst_ref=ypad.at[:, pl.ds(pl.multiple_of(margin + me * width, width), width)],
            send_sem=ts.at[s],
            recv_sem=tr.at[ne - 2 - s],
            device_id=(mk, peer),
            device_id_type=MESH,
        )
        c.start()
        copies.append(c)
    history = [pres_ref[m] for m in range(HIST)]
    gram = _pair_sums([None] + history, [(i, j) for i in range(1, HIST + 1) for j in range(i, HIST + 1)])
    for q in range(ne - 1):
        source = (me + q + 1) % ne
        pltpu.make_async_remote_copy(
            src_ref=chunk_ref.at[:, me, :],
            dst_ref=ypad.at[:, pl.ds(pl.multiple_of(margin + source * width, width), width)],
            send_sem=ts.at[q],
            recv_sem=tr.at[q],
            device_id=(mk, source),
            device_id_type=MESH,
        ).wait_recv()
    for s in range(ne - 1):
        copies[s].wait_send()

    y = ypad[...]
    row = lax.broadcasted_iota(jnp.int32, (rows, 1), 0)
    lead = 8
    lesser = row % lead < lead // 2
    per_row = rows // 8
    coupling = jnp.zeros((rows, 1), jnp.float32)
    for r in range(per_row):
        coupling = jnp.where(row // lead == r, acoustic_ref[class_ref[me * per_row + r]], coupling)
    sigma = coupling * y[:, margin : margin + length]
    for m in range(2):
        shift = shift_ref[m]
        strength = optical_ref[m]
        number = occ_ref[m]
        ahead = pltpu.roll(y, padded_len - shift, 1)[:, margin : margin + length]
        behind = pltpu.roll(y, shift, 1)[:, margin : margin + length]
        up = jnp.where(lesser, number + 1.0, number)
        down = jnp.where(lesser, number, number + 1.0)
        sigma = sigma + strength * (up * ahead + down * behind)
    res = sigma - cur_ref[...]
    fresh = _pair_sums([res] + history, [(0, j) for j in range(HIST + 1)])
    send1[...] = _pack_rows(fresh + gram)

    def exchange(src, recv, ssem, rsem, count, peer):
        out = []
        for s in range(count - 1):
            c = pltpu.make_async_remote_copy(
                src_ref=src,
                dst_ref=recv.at[count - 2 - s],
                send_sem=ssem.at[s],
                recv_sem=rsem.at[count - 2 - s],
                device_id=peer(s),
                device_id_type=MESH,
            )
            c.start()
            out.append(c)
        return out

    def finish(out):
        for c in out:
            c.wait_recv()
        for c in out:
            c.wait_send()

    def total(own, recv, mine, count):
        acc = jnp.zeros_like(own)
        for idx in range(count):
            slot = jnp.minimum((idx - mine - 1 + count) % count, count - 2)
            acc = acc + jnp.where(idx == mine, own, recv[slot])
        return acc

    pending = exchange(send1, recv1, ss1, rs1, nk, lambda s: ((mk + s + 1) % nk, me))
    for m in range(HIST):
        bases[m] = pin_ref[m] + mixing_share * history[m]
    finish(pending)
    acc1[...] = total(send1[...], recv1, mk, nk)
    finish(exchange(acc1, recv2, ss2, rs2, ne, lambda s: (mk, (me + s + 1) % ne)))
    summed = _unpack_rows(total(acc1[...], recv2, me, ne))
    perm = [0] + [slot_ref[i] + 1 for i in range(HIST)]
    aged = _permute_square(summed / entries, perm)
    weights = _weights_from_products(aged)[:, :1]
    row1 = lax.broadcasted_iota(jnp.int32, weights.shape, 0)
    slot_w = [None] * (HIST + 1)
    for i in range(HIST + 1):
        w_i = _pick(row1 == i, weights, 0)
        for m in range(HIST + 1):
            term = jnp.where(perm[i] == m, w_i, 0.0)
            slot_w[m] = term if slot_w[m] is None else slot_w[m] + term
    mixed = slot_w[0] * (cur_ref[...] + mixing_share * res)
    for m in range(HIST):
        mixed = mixed + slot_w[m + 1] * bases[m]
    out_ref[...] = mixed


def fused_tail(scalars, chunks, cur, pin, pres, nk, ne, entries):
    tile = (1, 128)
    margin = 128
    rows = chunks.shape[0]
    smem = pl.BlockSpec(memory_space=pltpu.SMEM)
    vmem = pl.BlockSpec(memory_space=pltpu.VMEM)
    return pl.pallas_call(
        functools.partial(_fused_kernel, nk, ne, entries, margin),
        out_shape=jax.ShapeDtypeStruct(cur.shape, jnp.float32),
        in_specs=[smem] * len(scalars) + [vmem] * 4,
        out_specs=vmem,
        scratch_shapes=[
            pltpu.VMEM((rows, cur.shape[1] + 2 * margin), jnp.float32),
            pltpu.VMEM((HIST,) + cur.shape, jnp.float32),
            pltpu.VMEM(tile, jnp.float32),
            pltpu.VMEM((nk - 1,) + tile, jnp.float32),
            pltpu.VMEM((ne - 1,) + tile, jnp.float32),
            pltpu.VMEM(tile, jnp.float32),
            pltpu.SemaphoreType.DMA((ne - 1,)),
            pltpu.SemaphoreType.DMA((ne - 1,)),
            pltpu.SemaphoreType.DMA((nk - 1,)),
            pltpu.SemaphoreType.DMA((nk - 1,)),
            pltpu.SemaphoreType.DMA((ne - 1,)),
            pltpu.SemaphoreType.DMA((ne - 1,)),
        ],
        compiler_params=pltpu.CompilerParams(collective_id=0, has_side_effects=True),
    )(*scalars, chunks, cur, pin, pres)


def per_device(
    greens,
    current,
    past_inputs,
    past_residuals,
    slot_order,
    neighbour,
    momentum_class,
    stencil_weight,
    acoustic_coupling,
    optical_coupling,
    occupation,
    phonon_shift,
):
    group_len = greens.shape[3]
    rows_here = current.shape[3]
    group_id = lax.axis_index("kgrp")
    energy_id = lax.axis_index("energy")
    nk = lax.axis_size("kgrp")
    ne = lax.axis_size("energy")
    total_k = group_len * nk
    ends = padded_2(greens, (("kgrp", 3),), group_len, True)
    low = ends[:, :, :, :group_len]
    high = ends[:, :, :, 2 * group_len :]
    local_index = (neighbour - group_id * group_len + group_len) % total_k
    stencil = jnp.sum(
        jnp.where(
            local_index[:, :, None] == jnp.arange(3 * group_len, dtype=jnp.int32)[None, None, :],
            stencil_weight[None, :, None],
            0.0,
        ),
        axis=1,
    )
    lead = greens.shape[:3]
    flat = lambda x: x.reshape((-1,) + x.shape[3:])
    stencil = stencil.reshape(ne, rows_here, 3 * group_len)
    chunks = jnp.zeros((rows_here, flat(greens).shape[0], ne, greens.shape[4]), jnp.float32)
    for part, block in enumerate((low, greens, high)):
        chunks = chunks + jnp.einsum(
            "dkr,bre->kbde",
            stencil[:, :, part * group_len : (part + 1) * group_len],
            flat(block),
            precision=lax.Precision.HIGHEST,
        )
    chunks = chunks.reshape(-1, ne, greens.shape[4])
    lanes = current.shape[-1]
    entries = float(current.size * nk * ne)
    scalars = (slot_order, phonon_shift, momentum_class, optical_coupling, occupation, acoustic_coupling)
    def to_rows(x):
        x = x.reshape((-1, flat(greens).shape[0], rows_here, lanes))
        return jnp.swapaxes(x, 1, 2).reshape((-1, rows_here * flat(greens).shape[0], lanes))

    mixed = fused_tail(
        scalars,
        chunks,
        to_rows(current)[0],
        to_rows(past_inputs),
        to_rows(past_residuals),
        nk,
        ne,
        entries,
    )
    mixed = jnp.swapaxes(mixed.reshape(rows_here, -1, lanes), 0, 1).reshape(current.shape)
    return mixed


def solution(mesh):
    return jax.shard_map(
        per_device,
        mesh=mesh,
        in_specs=(
            P(None, None, None, "kgrp", "energy"),
            P(None, None, None, ("kgrp", "energy"), None),
            P(None, None, None, None, ("kgrp", "energy"), None),
            P(None, None, None, None, ("kgrp", "energy"), None),
            P(),
            P("kgrp", None),
            P("kgrp"),
            P(),
            P(),
            P(),
            P(),
            P(),
        ),
        out_specs=P(None, None, None, ("kgrp", "energy"), None),
        check_vma=False,
    )
```

```python
import functools

import jax
import jax.numpy as jnp
from jax import lax
from jax.experimental import pallas as pl
from jax.experimental.pallas import tpu as pltpu
from jax.sharding import PartitionSpec as P

SHIFT_MAX = 96
HIST = 5

mixing_share = 0.5
ridge_share = 0.1

MESH = pl.DeviceIdType.MESH


def padded_2(block, sides, width, periodic):
    for axis, dim in sides:
        count = lax.axis_size(axis)
        forward = [(i, i + 1) for i in range(count - 1)]
        if periodic:
            forward.append((count - 1, 0))
        backward = [(target, source) for source, target in forward]
        low = lax.ppermute(
            lax.slice_in_dim(block, block.shape[dim] - width, None, axis=dim), axis, forward
        )
        high = lax.ppermute(lax.slice_in_dim(block, 0, width, axis=dim), axis, backward)
        block = jnp.concatenate([low, block, high], axis=dim)
    return block


def emit(padded, margin, length, coupling_row, optical, occupation, shifts):
    lesser = padded[0]
    greater = padded[1]

    def energy_view(source, offset):
        return lax.dynamic_slice_in_dim(source, margin + offset, length, axis=source.ndim - 1)

    sigma_less = coupling_row[:, None] * energy_view(lesser, 0)
    sigma_more = coupling_row[:, None] * energy_view(greater, 0)
    for column in range(2):
        strength = optical[column]
        number = occupation[column]
        offset = shifts[column]
        sigma_less = sigma_less + strength * (
            (number + 1.0) * energy_view(lesser, offset) + number * energy_view(lesser, -offset)
        )
        sigma_more = sigma_more + strength * (
            (number + 1.0) * energy_view(greater, -offset) + number * energy_view(greater, offset)
        )
    return jnp.stack([sigma_less, sigma_more])


def _pick(mask, x, axis):
    return jnp.sum(jnp.where(mask, x, 0.0), axis=axis, keepdims=True)


def _weights_from_products(prod):
    size_n = HIST
    row = lax.broadcasted_iota(jnp.int32, prod.shape, 0)
    col = lax.broadcasted_iota(jnp.int32, prod.shape, 1)
    rows, cols = prod.shape
    down = pltpu.roll(prod, rows - 1, 0)
    right = pltpu.roll(prod, cols - 1, 1)
    diag = pltpu.roll(down, cols - 1, 1)
    inside = (row < size_n) & (col < size_n)
    system = jnp.where(inside, prod - right - down + diag, 0.0)
    target = _pick((col == 0) & (row < size_n), prod - down, 1)
    eye = inside & (row == col)
    trace = jnp.sum(jnp.where(eye, system, 0.0), keepdims=True)
    ridge = ridge_share * trace / size_n + 1e-06
    a = system + jnp.where(eye, ridge, 0.0)
    lower = jnp.zeros_like(a)
    upper = jnp.zeros_like(a)
    diagonal = []
    for j in range(size_n):
        head = _pick((row == j) & (col == j), a, None).reshape(1, 1)
        pivot = jnp.sqrt(head)
        diagonal.append(head / pivot)
        lcol = jnp.where(row[:, :1] >= j, _pick(col == j, a, 1) / pivot, 0.0)
        lrow = jnp.where(col[:1, :] >= j, _pick(row == j, a, 0) / pivot, 0.0)
        lower = lower + jnp.where(col == j, lcol, 0.0)
        upper = upper + jnp.where(row == j, lrow, 0.0)
        a = a - lcol * lrow
    row1 = row[:, :1]
    rest = target
    forward = jnp.zeros_like(target)
    for i in range(size_n):
        lii = diagonal[i]
        yi = _pick(row1 == i, rest, 0) / lii
        forward = forward + jnp.where(row1 == i, yi, 0.0)
        rest = rest - jnp.where(row1 > i, _pick(col == i, lower, 1), 0.0) * yi
    rest = forward
    gamma = jnp.zeros_like(target)
    for i in range(size_n - 1, -1, -1):
        lii = diagonal[i]
        gi = _pick(row1 == i, rest, 0) / lii
        gamma = gamma + jnp.where(row1 == i, gi, 0.0)
        rest = rest - jnp.where(row1 < i, _pick(col == i, upper, 1), 0.0) * gi
    before = pltpu.roll(gamma, 1, 0)
    weights = jnp.where(row1 == 0, 1.0, 0.0) - gamma + before
    return jnp.broadcast_to(weights, prod.shape)


def _permute_square(prod, perm):
    row = lax.broadcasted_iota(jnp.int32, prod.shape, 0)
    col = lax.broadcasted_iota(jnp.int32, prod.shape, 1)
    count = len(perm)
    permcol = jnp.zeros((prod.shape[0], 1), jnp.int32)
    permrow = jnp.zeros((1, prod.shape[1]), jnp.int32)
    for i in range(count):
        permcol = jnp.where(row[:, :1] == i, perm[i], permcol)
        permrow = jnp.where(col[:1, :] == i, perm[i], permrow)
    by_rows = jnp.zeros_like(prod)
    for m in range(count):
        by_rows = by_rows + jnp.where(permcol == m, _pick(row == m, prod, 0), 0.0)
    by_rows = jnp.where(row < count, by_rows, 0.0)
    both = jnp.zeros_like(prod)
    for m in range(count):
        both = both + jnp.where(permrow == m, _pick(col == m, by_rows, 1), 0.0)
    return jnp.where(col < count, both, 0.0)


def _pair_sums(vectors, pairs):
    shape = (8, 128)
    row = lax.broadcasted_iota(jnp.int32, shape, 0)
    col = lax.broadcasted_iota(jnp.int32, shape, 1)
    prod = jnp.zeros(shape, jnp.float32)
    for i, j in pairs:
        value = jnp.sum(vectors[i] * vectors[j], keepdims=True)
        spot = ((row == i) & (col == j)) | ((row == j) & (col == i))
        prod = jnp.where(spot, value, prod)
    return prod


def _pack_rows(prod):
    row = lax.broadcasted_iota(jnp.int32, prod.shape, 0)
    packed = jnp.zeros((1, prod.shape[1]), jnp.float32)
    for i in range(HIST + 1):
        packed = packed + pltpu.roll(_pick(row == i, prod, 0), 8 * i, 1)
    return packed


def _unpack_rows(packed):
    shape = (8, packed.shape[1])
    row = lax.broadcasted_iota(jnp.int32, shape, 0)
    col = lax.broadcasted_iota(jnp.int32, shape, 1)
    prod = jnp.zeros(shape, jnp.float32)
    for i in range(HIST + 1):
        line = pltpu.roll(packed, (shape[1] - 8 * i) % shape[1], 1)
        prod = jnp.where((row == i) & (col <= HIST), line, prod)
    return prod


def _fused_kernel(nk, ne, entries, margin,
                  slot_ref, shift_ref, class_ref, optical_ref, occ_ref, acoustic_ref,
                  low_ref, mid_ref, high_ref, cur_ref, pin_ref, pres_ref, out_ref,
                  chunk_ref, ypad, bases, send1, recv1, recv2, acc1, ts, tr, ss1, rs1, ss2, rs2):
    mk = lax.axis_index("kgrp")
    me = lax.axis_index("energy")
    width = chunk_ref.shape[-1]
    rows, padded_len = ypad.shape
    length = padded_len - 2 * margin
    barrier = pltpu.get_barrier_semaphore()
    for s in range(nk - 1):
        pl.semaphore_signal(barrier, 1, device_id=((mk + s + 1) % nk, me), device_id_type=MESH)
    for s in range(ne - 1):
        pl.semaphore_signal(barrier, 1, device_id=(mk, (me + s + 1) % ne), device_id_type=MESH)
    chunk_ref[...] = low_ref[...] + mid_ref[...] + high_ref[...]
    ypad[:, :margin] = jnp.zeros((rows, margin), jnp.float32)
    ypad[:, margin + length :] = jnp.zeros((rows, margin), jnp.float32)
    ypad[:, pl.ds(pl.multiple_of(margin + me * width, width), width)] = chunk_ref[:, me, :]
    pl.semaphore_wait(barrier, nk - 1 + ne - 1)

    copies = []
    for s in range(ne - 1):
        peer = (me + s + 1) % ne
        c = pltpu.make_async_remote_copy(
            src_ref=chunk_ref.at[:, peer, :],
            dst_ref=ypad.at[:, pl.ds(pl.multiple_of(margin + me * width, width), width)],
            send_sem=ts.at[s],
            recv_sem=tr.at[ne - 2 - s],
            device_id=(mk, peer),
            device_id_type=MESH,
        )
        c.start()
        copies.append(c)
    history = [pres_ref[m] for m in range(HIST)]
    gram = _pair_sums([None] + history, [(i, j) for i in range(1, HIST + 1) for j in range(i, HIST + 1)])
    for q in range(ne - 1):
        source = (me + q + 1) % ne
        pltpu.make_async_remote_copy(
            src_ref=chunk_ref.at[:, me, :],
            dst_ref=ypad.at[:, pl.ds(pl.multiple_of(margin + source * width, width), width)],
            send_sem=ts.at[q],
            recv_sem=tr.at[q],
            device_id=(mk, source),
            device_id_type=MESH,
        ).wait_recv()
    for s in range(ne - 1):
        copies[s].wait_send()

    y = ypad[...]
    row = lax.broadcasted_iota(jnp.int32, (rows, 1), 0)
    lead = 8
    lesser = row % lead < lead // 2
    per_row = rows // 8
    coupling = jnp.zeros((rows, 1), jnp.float32)
    for r in range(per_row):
        coupling = jnp.where(row // lead == r, acoustic_ref[class_ref[me * per_row + r]], coupling)
    sigma = coupling * y[:, margin : margin + length]
    for m in range(2):
        shift = shift_ref[m]
        strength = optical_ref[m]
        number = occ_ref[m]
        ahead = pltpu.roll(y, padded_len - shift, 1)[:, margin : margin + length]
        behind = pltpu.roll(y, shift, 1)[:, margin : margin + length]
        up = jnp.where(lesser, number + 1.0, number)
        down = jnp.where(lesser, number, number + 1.0)
        sigma = sigma + strength * (up * ahead + down * behind)
    res = sigma - cur_ref[...]
    fresh = _pair_sums([res] + history, [(0, j) for j in range(HIST + 1)])
    send1[...] = _pack_rows(fresh + gram)

    def exchange(src, recv, ssem, rsem, count, peer):
        out = []
        for s in range(count - 1):
            c = pltpu.make_async_remote_copy(
                src_ref=src,
                dst_ref=recv.at[count - 2 - s],
                send_sem=ssem.at[s],
                recv_sem=rsem.at[count - 2 - s],
                device_id=peer(s),
                device_id_type=MESH,
            )
            c.start()
            out.append(c)
        return out

    def finish(out):
        for c in out:
            c.wait_recv()
        for c in out:
            c.wait_send()

    def total(own, recv, mine, count):
        acc = jnp.zeros_like(own)
        for idx in range(count):
            slot = jnp.minimum((idx - mine - 1 + count) % count, count - 2)
            acc = acc + jnp.where(idx == mine, own, recv[slot])
        return acc

    pending = exchange(send1, recv1, ss1, rs1, nk, lambda s: ((mk + s + 1) % nk, me))
    for m in range(HIST):
        bases[m] = pin_ref[m] + mixing_share * history[m]
    finish(pending)
    acc1[...] = total(send1[...], recv1, mk, nk)
    finish(exchange(acc1, recv2, ss2, rs2, ne, lambda s: (mk, (me + s + 1) % ne)))
    summed = _unpack_rows(total(acc1[...], recv2, me, ne))
    perm = [0] + [slot_ref[i] + 1 for i in range(HIST)]
    aged = _permute_square(summed / entries, perm)
    weights = _weights_from_products(aged)[:, :1]
    row1 = lax.broadcasted_iota(jnp.int32, weights.shape, 0)
    slot_w = [None] * (HIST + 1)
    for i in range(HIST + 1):
        w_i = _pick(row1 == i, weights, 0)
        for m in range(HIST + 1):
            term = jnp.where(perm[i] == m, w_i, 0.0)
            slot_w[m] = term if slot_w[m] is None else slot_w[m] + term
    mixed = slot_w[0] * (cur_ref[...] + mixing_share * res)
    for m in range(HIST):
        mixed = mixed + slot_w[m + 1] * bases[m]
    out_ref[...] = mixed


def fused_tail(scalars, parts, cur, pin, pres, nk, ne, entries):
    chunks = parts[0]
    tile = (1, 128)
    margin = 128
    rows = chunks.shape[0]
    smem = pl.BlockSpec(memory_space=pltpu.SMEM)
    vmem = pl.BlockSpec(memory_space=pltpu.VMEM)
    return pl.pallas_call(
        functools.partial(_fused_kernel, nk, ne, entries, margin),
        out_shape=jax.ShapeDtypeStruct(cur.shape, jnp.float32),
        in_specs=[smem] * len(scalars) + [vmem] * 6,
        out_specs=vmem,
        scratch_shapes=[
            pltpu.VMEM(chunks.shape, jnp.float32),
            pltpu.VMEM((rows, cur.shape[1] + 2 * margin), jnp.float32),
            pltpu.VMEM((HIST,) + cur.shape, jnp.float32),
            pltpu.VMEM(tile, jnp.float32),
            pltpu.VMEM((nk - 1,) + tile, jnp.float32),
            pltpu.VMEM((ne - 1,) + tile, jnp.float32),
            pltpu.VMEM(tile, jnp.float32),
            pltpu.SemaphoreType.DMA((ne - 1,)),
            pltpu.SemaphoreType.DMA((ne - 1,)),
            pltpu.SemaphoreType.DMA((nk - 1,)),
            pltpu.SemaphoreType.DMA((nk - 1,)),
            pltpu.SemaphoreType.DMA((ne - 1,)),
            pltpu.SemaphoreType.DMA((ne - 1,)),
        ],
        compiler_params=pltpu.CompilerParams(collective_id=0, has_side_effects=True),
    )(*scalars, *parts, cur, pin, pres)


def per_device(
    greens,
    current,
    past_inputs,
    past_residuals,
    slot_order,
    neighbour,
    momentum_class,
    stencil_weight,
    acoustic_coupling,
    optical_coupling,
    occupation,
    phonon_shift,
):
    group_len = greens.shape[3]
    rows_here = current.shape[3]
    group_id = lax.axis_index("kgrp")
    energy_id = lax.axis_index("energy")
    nk = lax.axis_size("kgrp")
    ne = lax.axis_size("energy")
    total_k = group_len * nk
    ends = padded_2(greens, (("kgrp", 3),), group_len, True)
    low = ends[:, :, :, :group_len]
    high = ends[:, :, :, 2 * group_len :]
    local_index = (neighbour - group_id * group_len + group_len) % total_k
    stencil = jnp.sum(
        jnp.where(
            local_index[:, :, None] == jnp.arange(3 * group_len, dtype=jnp.int32)[None, None, :],
            stencil_weight[None, :, None],
            0.0,
        ),
        axis=1,
    )
    lead = greens.shape[:3]
    flat = lambda x: x.reshape((-1,) + x.shape[3:])
    stencil = stencil.reshape(ne, rows_here, 3 * group_len)
    parts = []
    for part, block in enumerate((low.reshape(greens.shape), greens, high.reshape(greens.shape))):
        parts.append(
            jnp.einsum(
                "dkr,bre->kbde",
                stencil[:, :, part * group_len : (part + 1) * group_len],
                flat(block),
                precision=lax.Precision.HIGHEST,
            ).reshape(-1, ne, greens.shape[4])
        )
    lanes = current.shape[-1]
    entries = float(current.size * nk * ne)
    scalars = (slot_order, phonon_shift, momentum_class, optical_coupling, occupation, acoustic_coupling)
    def to_rows(x):
        x = x.reshape((-1, flat(greens).shape[0], rows_here, lanes))
        return jnp.swapaxes(x, 1, 2).reshape((-1, rows_here * flat(greens).shape[0], lanes))

    mixed = fused_tail(
        scalars,
        parts,
        to_rows(current)[0],
        to_rows(past_inputs),
        to_rows(past_residuals),
        nk,
        ne,
        entries,
    )
    mixed = jnp.swapaxes(mixed.reshape(rows_here, -1, lanes), 0, 1).reshape(current.shape)
    return mixed


def solution(mesh):
    return jax.shard_map(
        per_device,
        mesh=mesh,
        in_specs=(
            P(None, None, None, "kgrp", "energy"),
            P(None, None, None, ("kgrp", "energy"), None),
            P(None, None, None, None, ("kgrp", "energy"), None),
            P(None, None, None, None, ("kgrp", "energy"), None),
            P(),
            P("kgrp", None),
            P("kgrp"),
            P(),
            P(),
            P(),
            P(),
            P(),
        ),
        out_specs=P(None, None, None, ("kgrp", "energy"), None),
        check_vma=False,
    )
```

```python
import functools

import jax
import jax.numpy as jnp
from jax import lax
from jax.experimental import pallas as pl
from jax.experimental.pallas import tpu as pltpu
from jax.sharding import PartitionSpec as P

SHIFT_MAX = 96
HIST = 5

mixing_share = 0.5
ridge_share = 0.1

MESH = pl.DeviceIdType.MESH


def padded_2(block, sides, width, periodic):
    for axis, dim in sides:
        count = lax.axis_size(axis)
        forward = [(i, i + 1) for i in range(count - 1)]
        if periodic:
            forward.append((count - 1, 0))
        backward = [(target, source) for source, target in forward]
        low = lax.ppermute(
            lax.slice_in_dim(block, block.shape[dim] - width, None, axis=dim), axis, forward
        )
        high = lax.ppermute(lax.slice_in_dim(block, 0, width, axis=dim), axis, backward)
        block = jnp.concatenate([low, block, high], axis=dim)
    return block


def emit(padded, margin, length, coupling_row, optical, occupation, shifts):
    lesser = padded[0]
    greater = padded[1]

    def energy_view(source, offset):
        return lax.dynamic_slice_in_dim(source, margin + offset, length, axis=source.ndim - 1)

    sigma_less = coupling_row[:, None] * energy_view(lesser, 0)
    sigma_more = coupling_row[:, None] * energy_view(greater, 0)
    for column in range(2):
        strength = optical[column]
        number = occupation[column]
        offset = shifts[column]
        sigma_less = sigma_less + strength * (
            (number + 1.0) * energy_view(lesser, offset) + number * energy_view(lesser, -offset)
        )
        sigma_more = sigma_more + strength * (
            (number + 1.0) * energy_view(greater, -offset) + number * energy_view(greater, offset)
        )
    return jnp.stack([sigma_less, sigma_more])


def _pick(mask, x, axis):
    return jnp.sum(jnp.where(mask, x, 0.0), axis=axis, keepdims=True)


def _weights_from_products(prod):
    size_n = HIST
    row = lax.broadcasted_iota(jnp.int32, prod.shape, 0)
    col = lax.broadcasted_iota(jnp.int32, prod.shape, 1)
    rows, cols = prod.shape
    down = pltpu.roll(prod, rows - 1, 0)
    right = pltpu.roll(prod, cols - 1, 1)
    diag = pltpu.roll(down, cols - 1, 1)
    inside = (row < size_n) & (col < size_n)
    system = jnp.where(inside, prod - right - down + diag, 0.0)
    target = _pick((col == 0) & (row < size_n), prod - down, 1)
    eye = inside & (row == col)
    trace = jnp.sum(jnp.where(eye, system, 0.0), keepdims=True)
    ridge = ridge_share * trace / size_n + 1e-06
    a = system + jnp.where(eye, ridge, 0.0)
    lower = jnp.zeros_like(a)
    upper = jnp.zeros_like(a)
    diagonal = []
    for j in range(size_n):
        head = _pick((row == j) & (col == j), a, None).reshape(1, 1)
        pivot = jnp.sqrt(head)
        diagonal.append(head / pivot)
        lcol = jnp.where(row[:, :1] >= j, _pick(col == j, a, 1) / pivot, 0.0)
        lrow = jnp.where(col[:1, :] >= j, _pick(row == j, a, 0) / pivot, 0.0)
        lower = lower + jnp.where(col == j, lcol, 0.0)
        upper = upper + jnp.where(row == j, lrow, 0.0)
        a = a - lcol * lrow
    row1 = row[:, :1]
    rest = target
    forward = jnp.zeros_like(target)
    for i in range(size_n):
        lii = diagonal[i]
        yi = _pick(row1 == i, rest, 0) / lii
        forward = forward + jnp.where(row1 == i, yi, 0.0)
        rest = rest - jnp.where(row1 > i, _pick(col == i, lower, 1), 0.0) * yi
    rest = forward
    gamma = jnp.zeros_like(target)
    for i in range(size_n - 1, -1, -1):
        lii = diagonal[i]
        gi = _pick(row1 == i, rest, 0) / lii
        gamma = gamma + jnp.where(row1 == i, gi, 0.0)
        rest = rest - jnp.where(row1 < i, _pick(col == i, upper, 1), 0.0) * gi
    before = pltpu.roll(gamma, 1, 0)
    weights = jnp.where(row1 == 0, 1.0, 0.0) - gamma + before
    return jnp.broadcast_to(weights, prod.shape)


def _permute_square(prod, perm):
    row = lax.broadcasted_iota(jnp.int32, prod.shape, 0)
    col = lax.broadcasted_iota(jnp.int32, prod.shape, 1)
    count = len(perm)
    permcol = jnp.zeros((prod.shape[0], 1), jnp.int32)
    permrow = jnp.zeros((1, prod.shape[1]), jnp.int32)
    for i in range(count):
        permcol = jnp.where(row[:, :1] == i, perm[i], permcol)
        permrow = jnp.where(col[:1, :] == i, perm[i], permrow)
    by_rows = jnp.zeros_like(prod)
    for m in range(count):
        by_rows = by_rows + jnp.where(permcol == m, _pick(row == m, prod, 0), 0.0)
    by_rows = jnp.where(row < count, by_rows, 0.0)
    both = jnp.zeros_like(prod)
    for m in range(count):
        both = both + jnp.where(permrow == m, _pick(col == m, by_rows, 1), 0.0)
    return jnp.where(col < count, both, 0.0)


def _pair_sums(vectors, pairs):
    shape = (8, 128)
    row = lax.broadcasted_iota(jnp.int32, shape, 0)
    col = lax.broadcasted_iota(jnp.int32, shape, 1)
    prod = jnp.zeros(shape, jnp.float32)
    for i, j in pairs:
        value = jnp.sum(vectors[i] * vectors[j], keepdims=True)
        spot = ((row == i) & (col == j)) | ((row == j) & (col == i))
        prod = jnp.where(spot, value, prod)
    return prod


def _pack_rows(prod):
    row = lax.broadcasted_iota(jnp.int32, prod.shape, 0)
    packed = jnp.zeros((1, prod.shape[1]), jnp.float32)
    for i in range(HIST + 1):
        packed = packed + pltpu.roll(_pick(row == i, prod, 0), 8 * i, 1)
    return packed


def _unpack_rows(packed):
    shape = (8, packed.shape[1])
    row = lax.broadcasted_iota(jnp.int32, shape, 0)
    col = lax.broadcasted_iota(jnp.int32, shape, 1)
    prod = jnp.zeros(shape, jnp.float32)
    for i in range(HIST + 1):
        line = pltpu.roll(packed, (shape[1] - 8 * i) % shape[1], 1)
        prod = jnp.where((row == i) & (col <= HIST), line, prod)
    return prod


def _far_first(count):
    return sorted(range(count - 1), key=lambda s: (-min(s + 1, count - s - 1), s))


def _fused_kernel(nk, ne, entries, margin,
                  slot_ref, shift_ref, class_ref, optical_ref, occ_ref, acoustic_ref,
                  chunk_ref, cur_ref, pin_ref, pres_ref, out_ref,
                  ypad, bases, send1, recv1, recv2, acc1, ts, tr, ss1, rs1, ss2, rs2):
    mk = lax.axis_index("kgrp")
    me = lax.axis_index("energy")
    width = chunk_ref.shape[-1]
    rows, padded_len = ypad.shape
    length = padded_len - 2 * margin
    barrier = pltpu.get_barrier_semaphore()
    for s in _far_first(ne):
        pl.semaphore_signal(barrier, 1, device_id=(mk, (me + s + 1) % ne), device_id_type=MESH)
    for s in _far_first(nk):
        pl.semaphore_signal(barrier, 1, device_id=((mk + s + 1) % nk, me), device_id_type=MESH)
    ypad[:, :margin] = jnp.zeros((rows, margin), jnp.float32)
    ypad[:, margin + length :] = jnp.zeros((rows, margin), jnp.float32)
    ypad[:, pl.ds(pl.multiple_of(margin + me * width, width), width)] = chunk_ref[:, me, :]
    pl.semaphore_wait(barrier, nk - 1 + ne - 1)

    copies = [None] * (ne - 1)
    for s in _far_first(ne):
        peer = (me + s + 1) % ne
        c = pltpu.make_async_remote_copy(
            src_ref=chunk_ref.at[:, peer, :],
            dst_ref=ypad.at[:, pl.ds(pl.multiple_of(margin + me * width, width), width)],
            send_sem=ts.at[s],
            recv_sem=tr.at[ne - 2 - s],
            device_id=(mk, peer),
            device_id_type=MESH,
        )
        c.start()
        copies[s] = c
    history = [pres_ref[m] for m in range(HIST)]
    gram = _pair_sums([None] + history, [(i, j) for i in range(1, HIST + 1) for j in range(i, HIST + 1)])
    for q in range(ne - 1):
        source = (me + q + 1) % ne
        pltpu.make_async_remote_copy(
            src_ref=chunk_ref.at[:, me, :],
            dst_ref=ypad.at[:, pl.ds(pl.multiple_of(margin + source * width, width), width)],
            send_sem=ts.at[q],
            recv_sem=tr.at[q],
            device_id=(mk, source),
            device_id_type=MESH,
        ).wait_recv()
    for s in range(ne - 1):
        copies[s].wait_send()

    y = ypad[...]
    row = lax.broadcasted_iota(jnp.int32, (rows, 1), 0)
    lead = 8
    lesser = row % lead < lead // 2
    per_row = rows // 8
    coupling = jnp.zeros((rows, 1), jnp.float32)
    for r in range(per_row):
        coupling = jnp.where(row // lead == r, acoustic_ref[class_ref[me * per_row + r]], coupling)
    sigma = coupling * y[:, margin : margin + length]
    for m in range(2):
        shift = shift_ref[m]
        strength = optical_ref[m]
        number = occ_ref[m]
        ahead = pltpu.roll(y, padded_len - shift, 1)[:, margin : margin + length]
        behind = pltpu.roll(y, shift, 1)[:, margin : margin + length]
        up = jnp.where(lesser, number + 1.0, number)
        down = jnp.where(lesser, number, number + 1.0)
        sigma = sigma + strength * (up * ahead + down * behind)
    res = sigma - cur_ref[...]
    fresh = _pair_sums([res] + history, [(0, j) for j in range(HIST + 1)])
    send1[...] = _pack_rows(fresh + gram)

    def exchange(src, recv, ssem, rsem, count, peer):
        out = [None] * (count - 1)
        for s in _far_first(count):
            c = pltpu.make_async_remote_copy(
                src_ref=src,
                dst_ref=recv.at[count - 2 - s],
                send_sem=ssem.at[s],
                recv_sem=rsem.at[count - 2 - s],
                device_id=peer(s),
                device_id_type=MESH,
            )
            c.start()
            out[s] = c
        return out

    def finish(out):
        for c in out:
            c.wait_recv()
        for c in out:
            c.wait_send()

    def total(own, recv, mine, count):
        acc = jnp.zeros_like(own)
        for idx in range(count):
            slot = jnp.minimum((idx - mine - 1 + count) % count, count - 2)
            acc = acc + jnp.where(idx == mine, own, recv[slot])
        return acc

    pending = exchange(send1, recv1, ss1, rs1, nk, lambda s: ((mk + s + 1) % nk, me))
    for m in range(HIST):
        bases[m] = pin_ref[m] + mixing_share * history[m]
    finish(pending)
    acc1[...] = total(send1[...], recv1, mk, nk)
    finish(exchange(acc1, recv2, ss2, rs2, ne, lambda s: (mk, (me + s + 1) % ne)))
    summed = _unpack_rows(total(acc1[...], recv2, me, ne))
    perm = [0] + [slot_ref[i] + 1 for i in range(HIST)]
    aged = _permute_square(summed / entries, perm)
    weights = _weights_from_products(aged)[:, :1]
    row1 = lax.broadcasted_iota(jnp.int32, weights.shape, 0)
    slot_w = [None] * (HIST + 1)
    for i in range(HIST + 1):
        w_i = _pick(row1 == i, weights, 0)
        for m in range(HIST + 1):
            term = jnp.where(perm[i] == m, w_i, 0.0)
            slot_w[m] = term if slot_w[m] is None else slot_w[m] + term
    mixed = slot_w[0] * (cur_ref[...] + mixing_share * res)
    for m in range(HIST):
        mixed = mixed + slot_w[m + 1] * bases[m]
    out_ref[...] = mixed


def fused_tail(scalars, chunks, cur, pin, pres, nk, ne, entries):
    tile = (1, 128)
    margin = 128
    rows = chunks.shape[0]
    smem = pl.BlockSpec(memory_space=pltpu.SMEM)
    vmem = pl.BlockSpec(memory_space=pltpu.VMEM)
    return pl.pallas_call(
        functools.partial(_fused_kernel, nk, ne, entries, margin),
        out_shape=jax.ShapeDtypeStruct(cur.shape, jnp.float32),
        in_specs=[smem] * len(scalars) + [vmem] * 4,
        out_specs=vmem,
        scratch_shapes=[
            pltpu.VMEM((rows, cur.shape[1] + 2 * margin), jnp.float32),
            pltpu.VMEM((HIST,) + cur.shape, jnp.float32),
            pltpu.VMEM(tile, jnp.float32),
            pltpu.VMEM((nk - 1,) + tile, jnp.float32),
            pltpu.VMEM((ne - 1,) + tile, jnp.float32),
            pltpu.VMEM(tile, jnp.float32),
            pltpu.SemaphoreType.DMA((ne - 1,)),
            pltpu.SemaphoreType.DMA((ne - 1,)),
            pltpu.SemaphoreType.DMA((nk - 1,)),
            pltpu.SemaphoreType.DMA((nk - 1,)),
            pltpu.SemaphoreType.DMA((ne - 1,)),
            pltpu.SemaphoreType.DMA((ne - 1,)),
        ],
        compiler_params=pltpu.CompilerParams(collective_id=0, has_side_effects=True),
    )(*scalars, chunks, cur, pin, pres)


def per_device(
    greens,
    current,
    past_inputs,
    past_residuals,
    slot_order,
    neighbour,
    momentum_class,
    stencil_weight,
    acoustic_coupling,
    optical_coupling,
    occupation,
    phonon_shift,
):
    group_len = greens.shape[3]
    rows_here = current.shape[3]
    group_id = lax.axis_index("kgrp")
    energy_id = lax.axis_index("energy")
    nk = lax.axis_size("kgrp")
    ne = lax.axis_size("energy")
    total_k = group_len * nk
    ends = padded_2(greens, (("kgrp", 3),), group_len, True)
    low = ends[:, :, :, :group_len]
    high = ends[:, :, :, 2 * group_len :]
    local_index = (neighbour - group_id * group_len + group_len) % total_k
    stencil = jnp.sum(
        jnp.where(
            local_index[:, :, None] == jnp.arange(3 * group_len, dtype=jnp.int32)[None, None, :],
            stencil_weight[None, :, None],
            0.0,
        ),
        axis=1,
    )
    lead = greens.shape[:3]
    flat = lambda x: x.reshape((-1,) + x.shape[3:])
    stencil = stencil.reshape(ne, rows_here, 3 * group_len)
    chunks = jnp.zeros((rows_here, flat(greens).shape[0], ne, greens.shape[4]), jnp.float32)
    for part, block in enumerate((low, greens, high)):
        chunks = chunks + jnp.einsum(
            "dkr,bre->kbde",
            stencil[:, :, part * group_len : (part + 1) * group_len],
            flat(block),
            precision=lax.Precision.HIGHEST,
        )
    chunks = chunks.reshape(-1, ne, greens.shape[4])
    lanes = current.shape[-1]
    entries = float(current.size * nk * ne)
    scalars = (slot_order, phonon_shift, momentum_class, optical_coupling, occupation, acoustic_coupling)
    def to_rows(x):
        x = x.reshape((-1, flat(greens).shape[0], rows_here, lanes))
        return jnp.swapaxes(x, 1, 2).reshape((-1, rows_here * flat(greens).shape[0], lanes))

    mixed = fused_tail(
        scalars,
        chunks,
        to_rows(current)[0],
        to_rows(past_inputs),
        to_rows(past_residuals),
        nk,
        ne,
        entries,
    )
    mixed = jnp.swapaxes(mixed.reshape(rows_here, -1, lanes), 0, 1).reshape(current.shape)
    return mixed


def solution(mesh):
    return jax.shard_map(
        per_device,
        mesh=mesh,
        in_specs=(
            P(None, None, None, "kgrp", "energy"),
            P(None, None, None, ("kgrp", "energy"), None),
            P(None, None, None, None, ("kgrp", "energy"), None),
            P(None, None, None, None, ("kgrp", "energy"), None),
            P(),
            P("kgrp", None),
            P("kgrp"),
            P(),
            P(),
            P(),
            P(),
            P(),
        ),
        out_specs=P(None, None, None, ("kgrp", "energy"), None),
        check_vma=False,
    )
```

```python
import functools

import jax
import jax.numpy as jnp
from jax import lax
from jax.experimental import pallas as pl
from jax.experimental.pallas import tpu as pltpu
from jax.sharding import PartitionSpec as P

SHIFT_MAX = 96
HIST = 5

mixing_share = 0.5
ridge_share = 0.1

MESH = pl.DeviceIdType.MESH


def padded_2(block, sides, width, periodic):
    for axis, dim in sides:
        count = lax.axis_size(axis)
        forward = [(i, i + 1) for i in range(count - 1)]
        if periodic:
            forward.append((count - 1, 0))
        backward = [(target, source) for source, target in forward]
        low = lax.ppermute(
            lax.slice_in_dim(block, block.shape[dim] - width, None, axis=dim), axis, forward
        )
        high = lax.ppermute(lax.slice_in_dim(block, 0, width, axis=dim), axis, backward)
        block = jnp.concatenate([low, block, high], axis=dim)
    return block


def emit(padded, margin, length, coupling_row, optical, occupation, shifts):
    lesser = padded[0]
    greater = padded[1]

    def energy_view(source, offset):
        return lax.dynamic_slice_in_dim(source, margin + offset, length, axis=source.ndim - 1)

    sigma_less = coupling_row[:, None] * energy_view(lesser, 0)
    sigma_more = coupling_row[:, None] * energy_view(greater, 0)
    for column in range(2):
        strength = optical[column]
        number = occupation[column]
        offset = shifts[column]
        sigma_less = sigma_less + strength * (
            (number + 1.0) * energy_view(lesser, offset) + number * energy_view(lesser, -offset)
        )
        sigma_more = sigma_more + strength * (
            (number + 1.0) * energy_view(greater, -offset) + number * energy_view(greater, offset)
        )
    return jnp.stack([sigma_less, sigma_more])


def _pick(mask, x, axis):
    return jnp.sum(jnp.where(mask, x, 0.0), axis=axis, keepdims=True)


def _weights_from_products(prod):
    size_n = HIST
    row = lax.broadcasted_iota(jnp.int32, prod.shape, 0)
    col = lax.broadcasted_iota(jnp.int32, prod.shape, 1)
    rows, cols = prod.shape
    down = pltpu.roll(prod, rows - 1, 0)
    right = pltpu.roll(prod, cols - 1, 1)
    diag = pltpu.roll(down, cols - 1, 1)
    inside = (row < size_n) & (col < size_n)
    system = jnp.where(inside, prod - right - down + diag, 0.0)
    target = _pick((col == 0) & (row < size_n), prod - down, 1)
    eye = inside & (row == col)
    trace = jnp.sum(jnp.where(eye, system, 0.0), keepdims=True)
    ridge = ridge_share * trace / size_n + 1e-06
    a = system + jnp.where(eye, ridge, 0.0)
    lower = jnp.zeros_like(a)
    upper = jnp.zeros_like(a)
    diagonal = []
    for j in range(size_n):
        head = _pick((row == j) & (col == j), a, None).reshape(1, 1)
        pivot = jnp.sqrt(head)
        diagonal.append(head / pivot)
        lcol = jnp.where(row[:, :1] >= j, _pick(col == j, a, 1) / pivot, 0.0)
        lrow = jnp.where(col[:1, :] >= j, _pick(row == j, a, 0) / pivot, 0.0)
        lower = lower + jnp.where(col == j, lcol, 0.0)
        upper = upper + jnp.where(row == j, lrow, 0.0)
        a = a - lcol * lrow
    row1 = row[:, :1]
    rest = target
    forward = jnp.zeros_like(target)
    for i in range(size_n):
        lii = diagonal[i]
        yi = _pick(row1 == i, rest, 0) / lii
        forward = forward + jnp.where(row1 == i, yi, 0.0)
        rest = rest - jnp.where(row1 > i, _pick(col == i, lower, 1), 0.0) * yi
    rest = forward
    gamma = jnp.zeros_like(target)
    for i in range(size_n - 1, -1, -1):
        lii = diagonal[i]
        gi = _pick(row1 == i, rest, 0) / lii
        gamma = gamma + jnp.where(row1 == i, gi, 0.0)
        rest = rest - jnp.where(row1 < i, _pick(col == i, upper, 1), 0.0) * gi
    before = pltpu.roll(gamma, 1, 0)
    weights = jnp.where(row1 == 0, 1.0, 0.0) - gamma + before
    return jnp.broadcast_to(weights, prod.shape)


def _permute_square(prod, perm):
    row = lax.broadcasted_iota(jnp.int32, prod.shape, 0)
    col = lax.broadcasted_iota(jnp.int32, prod.shape, 1)
    count = len(perm)
    permcol = jnp.zeros((prod.shape[0], 1), jnp.int32)
    permrow = jnp.zeros((1, prod.shape[1]), jnp.int32)
    for i in range(count):
        permcol = jnp.where(row[:, :1] == i, perm[i], permcol)
        permrow = jnp.where(col[:1, :] == i, perm[i], permrow)
    by_rows = jnp.zeros_like(prod)
    for m in range(count):
        by_rows = by_rows + jnp.where(permcol == m, _pick(row == m, prod, 0), 0.0)
    by_rows = jnp.where(row < count, by_rows, 0.0)
    both = jnp.zeros_like(prod)
    for m in range(count):
        both = both + jnp.where(permrow == m, _pick(col == m, by_rows, 1), 0.0)
    return jnp.where(col < count, both, 0.0)


def _pair_sums(vectors, pairs):
    shape = (8, 128)
    row = lax.broadcasted_iota(jnp.int32, shape, 0)
    col = lax.broadcasted_iota(jnp.int32, shape, 1)
    prod = jnp.zeros(shape, jnp.float32)
    for i, j in pairs:
        value = jnp.sum(vectors[i] * vectors[j], keepdims=True)
        spot = ((row == i) & (col == j)) | ((row == j) & (col == i))
        prod = jnp.where(spot, value, prod)
    return prod


def _pack_rows(prod):
    row = lax.broadcasted_iota(jnp.int32, prod.shape, 0)
    packed = jnp.zeros((1, prod.shape[1]), jnp.float32)
    for i in range(HIST + 1):
        packed = packed + pltpu.roll(_pick(row == i, prod, 0), 8 * i, 1)
    return packed


def _unpack_rows(packed):
    shape = (8, packed.shape[1])
    row = lax.broadcasted_iota(jnp.int32, shape, 0)
    col = lax.broadcasted_iota(jnp.int32, shape, 1)
    prod = jnp.zeros(shape, jnp.float32)
    for i in range(HIST + 1):
        line = pltpu.roll(packed, (shape[1] - 8 * i) % shape[1], 1)
        prod = jnp.where((row == i) & (col <= HIST), line, prod)
    return prod


def _far_first(count):
    return sorted(range(count - 1), key=lambda s: (-min(s + 1, count - s - 1), s))


def _far_first_grid(count, inner):
    if count % inner:
        return _far_first(count)

    def ring(d, size):
        return min(d % size, size - d % size)

    outer = count // inner
    return sorted(
        range(count - 1),
        key=lambda s: (-(ring(s + 1, inner) + ring((s + 1) // inner, outer)), s),
    )


def _fused_kernel(nk, ne, entries, margin,
                  slot_ref, shift_ref, class_ref, optical_ref, occ_ref, acoustic_ref,
                  chunk_ref, cur_ref, pin_ref, pres_ref, out_ref,
                  ypad, bases, send1, recv1, recv2, acc1, ts, tr, ss1, rs1, ss2, rs2):
    mk = lax.axis_index("kgrp")
    me = lax.axis_index("energy")
    width = chunk_ref.shape[-1]
    rows, padded_len = ypad.shape
    length = padded_len - 2 * margin
    barrier = pltpu.get_barrier_semaphore()
    for s in _far_first(ne):
        pl.semaphore_signal(barrier, 1, device_id=(mk, (me + s + 1) % ne), device_id_type=MESH)
    for s in _far_first_grid(nk, 4):
        pl.semaphore_signal(barrier, 1, device_id=((mk + s + 1) % nk, me), device_id_type=MESH)
    ypad[:, :margin] = jnp.zeros((rows, margin), jnp.float32)
    ypad[:, margin + length :] = jnp.zeros((rows, margin), jnp.float32)
    ypad[:, pl.ds(pl.multiple_of(margin + me * width, width), width)] = chunk_ref[:, me, :]
    pl.semaphore_wait(barrier, nk - 1 + ne - 1)

    copies = [None] * (ne - 1)
    for s in _far_first(ne):
        peer = (me + s + 1) % ne
        c = pltpu.make_async_remote_copy(
            src_ref=chunk_ref.at[:, peer, :],
            dst_ref=ypad.at[:, pl.ds(pl.multiple_of(margin + me * width, width), width)],
            send_sem=ts.at[s],
            recv_sem=tr.at[ne - 2 - s],
            device_id=(mk, peer),
            device_id_type=MESH,
        )
        c.start()
        copies[s] = c
    history = [pres_ref[m] for m in range(HIST)]
    gram = _pair_sums([None] + history, [(i, j) for i in range(1, HIST + 1) for j in range(i, HIST + 1)])
    for q in range(ne - 1):
        source = (me + q + 1) % ne
        pltpu.make_async_remote_copy(
            src_ref=chunk_ref.at[:, me, :],
            dst_ref=ypad.at[:, pl.ds(pl.multiple_of(margin + source * width, width), width)],
            send_sem=ts.at[q],
            recv_sem=tr.at[q],
            device_id=(mk, source),
            device_id_type=MESH,
        ).wait_recv()
    for s in range(ne - 1):
        copies[s].wait_send()

    y = ypad[...]
    row = lax.broadcasted_iota(jnp.int32, (rows, 1), 0)
    lead = 8
    lesser = row % lead < lead // 2
    per_row = rows // 8
    coupling = jnp.zeros((rows, 1), jnp.float32)
    for r in range(per_row):
        coupling = jnp.where(row // lead == r, acoustic_ref[class_ref[me * per_row + r]], coupling)
    sigma = coupling * y[:, margin : margin + length]
    for m in range(2):
        shift = shift_ref[m]
        strength = optical_ref[m]
        number = occ_ref[m]
        ahead = pltpu.roll(y, padded_len - shift, 1)[:, margin : margin + length]
        behind = pltpu.roll(y, shift, 1)[:, margin : margin + length]
        up = jnp.where(lesser, number + 1.0, number)
        down = jnp.where(lesser, number, number + 1.0)
        sigma = sigma + strength * (up * ahead + down * behind)
    res = sigma - cur_ref[...]
    fresh = _pair_sums([res] + history, [(0, j) for j in range(HIST + 1)])
    send1[...] = _pack_rows(fresh + gram)

    def exchange(src, recv, ssem, rsem, count, peer, order):
        out = [None] * (count - 1)
        for s in order:
            c = pltpu.make_async_remote_copy(
                src_ref=src,
                dst_ref=recv.at[count - 2 - s],
                send_sem=ssem.at[s],
                recv_sem=rsem.at[count - 2 - s],
                device_id=peer(s),
                device_id_type=MESH,
            )
            c.start()
            out[s] = c
        return out

    def finish(out):
        for c in out:
            c.wait_recv()
        for c in out:
            c.wait_send()

    def total(own, recv, mine, count):
        acc = jnp.zeros_like(own)
        for idx in range(count):
            slot = jnp.minimum((idx - mine - 1 + count) % count, count - 2)
            acc = acc + jnp.where(idx == mine, own, recv[slot])
        return acc

    pending = exchange(send1, recv1, ss1, rs1, nk, lambda s: ((mk + s + 1) % nk, me), _far_first_grid(nk, 4))
    for m in range(HIST):
        bases[m] = pin_ref[m] + mixing_share * history[m]
    finish(pending)
    acc1[...] = total(send1[...], recv1, mk, nk)
    finish(exchange(acc1, recv2, ss2, rs2, ne, lambda s: (mk, (me + s + 1) % ne), _far_first(ne)))
    summed = _unpack_rows(total(acc1[...], recv2, me, ne))
    perm = [0] + [slot_ref[i] + 1 for i in range(HIST)]
    aged = _permute_square(summed / entries, perm)
    weights = _weights_from_products(aged)[:, :1]
    row1 = lax.broadcasted_iota(jnp.int32, weights.shape, 0)
    slot_w = [None] * (HIST + 1)
    for i in range(HIST + 1):
        w_i = _pick(row1 == i, weights, 0)
        for m in range(HIST + 1):
            term = jnp.where(perm[i] == m, w_i, 0.0)
            slot_w[m] = term if slot_w[m] is None else slot_w[m] + term
    mixed = slot_w[0] * (cur_ref[...] + mixing_share * res)
    for m in range(HIST):
        mixed = mixed + slot_w[m + 1] * bases[m]
    out_ref[...] = mixed


def fused_tail(scalars, chunks, cur, pin, pres, nk, ne, entries):
    tile = (1, 128)
    margin = 128
    rows = chunks.shape[0]
    smem = pl.BlockSpec(memory_space=pltpu.SMEM)
    vmem = pl.BlockSpec(memory_space=pltpu.VMEM)
    return pl.pallas_call(
        functools.partial(_fused_kernel, nk, ne, entries, margin),
        out_shape=jax.ShapeDtypeStruct(cur.shape, jnp.float32),
        in_specs=[smem] * len(scalars) + [vmem] * 4,
        out_specs=vmem,
        scratch_shapes=[
            pltpu.VMEM((rows, cur.shape[1] + 2 * margin), jnp.float32),
            pltpu.VMEM((HIST,) + cur.shape, jnp.float32),
            pltpu.VMEM(tile, jnp.float32),
            pltpu.VMEM((nk - 1,) + tile, jnp.float32),
            pltpu.VMEM((ne - 1,) + tile, jnp.float32),
            pltpu.VMEM(tile, jnp.float32),
            pltpu.SemaphoreType.DMA((ne - 1,)),
            pltpu.SemaphoreType.DMA((ne - 1,)),
            pltpu.SemaphoreType.DMA((nk - 1,)),
            pltpu.SemaphoreType.DMA((nk - 1,)),
            pltpu.SemaphoreType.DMA((ne - 1,)),
            pltpu.SemaphoreType.DMA((ne - 1,)),
        ],
        compiler_params=pltpu.CompilerParams(collective_id=0, has_side_effects=True),
    )(*scalars, chunks, cur, pin, pres)


def per_device(
    greens,
    current,
    past_inputs,
    past_residuals,
    slot_order,
    neighbour,
    momentum_class,
    stencil_weight,
    acoustic_coupling,
    optical_coupling,
    occupation,
    phonon_shift,
):
    group_len = greens.shape[3]
    rows_here = current.shape[3]
    group_id = lax.axis_index("kgrp")
    energy_id = lax.axis_index("energy")
    nk = lax.axis_size("kgrp")
    ne = lax.axis_size("energy")
    total_k = group_len * nk
    ends = padded_2(greens, (("kgrp", 3),), group_len, True)
    low = ends[:, :, :, :group_len]
    high = ends[:, :, :, 2 * group_len :]
    local_index = (neighbour - group_id * group_len + group_len) % total_k
    stencil = jnp.sum(
        jnp.where(
            local_index[:, :, None] == jnp.arange(3 * group_len, dtype=jnp.int32)[None, None, :],
            stencil_weight[None, :, None],
            0.0,
        ),
        axis=1,
    )
    lead = greens.shape[:3]
    flat = lambda x: x.reshape((-1,) + x.shape[3:])
    stencil = stencil.reshape(ne, rows_here, 3 * group_len)
    chunks = jnp.zeros((rows_here, flat(greens).shape[0], ne, greens.shape[4]), jnp.float32)
    for part, block in enumerate((low, greens, high)):
        chunks = chunks + jnp.einsum(
            "dkr,bre->kbde",
            stencil[:, :, part * group_len : (part + 1) * group_len],
            flat(block),
            precision=lax.Precision.HIGHEST,
        )
    chunks = chunks.reshape(-1, ne, greens.shape[4])
    lanes = current.shape[-1]
    entries = float(current.size * nk * ne)
    scalars = (slot_order, phonon_shift, momentum_class, optical_coupling, occupation, acoustic_coupling)
    def to_rows(x):
        x = x.reshape((-1, flat(greens).shape[0], rows_here, lanes))
        return jnp.swapaxes(x, 1, 2).reshape((-1, rows_here * flat(greens).shape[0], lanes))

    mixed = fused_tail(
        scalars,
        chunks,
        to_rows(current)[0],
        to_rows(past_inputs),
        to_rows(past_residuals),
        nk,
        ne,
        entries,
    )
    mixed = jnp.swapaxes(mixed.reshape(rows_here, -1, lanes), 0, 1).reshape(current.shape)
    return mixed


def solution(mesh):
    return jax.shard_map(
        per_device,
        mesh=mesh,
        in_specs=(
            P(None, None, None, "kgrp", "energy"),
            P(None, None, None, ("kgrp", "energy"), None),
            P(None, None, None, None, ("kgrp", "energy"), None),
            P(None, None, None, None, ("kgrp", "energy"), None),
            P(),
            P("kgrp", None),
            P("kgrp"),
            P(),
            P(),
            P(),
            P(),
            P(),
        ),
        out_specs=P(None, None, None, ("kgrp", "energy"), None),
        check_vma=False,
    )
```

```python
import functools

import jax
import jax.numpy as jnp
from jax import lax
from jax.experimental import pallas as pl
from jax.experimental.pallas import tpu as pltpu
from jax.sharding import PartitionSpec as P

SHIFT_MAX = 96
HIST = 5

mixing_share = 0.5
ridge_share = 0.1

MESH = pl.DeviceIdType.MESH


def padded_2(block, sides, width, periodic):
    for axis, dim in sides:
        count = lax.axis_size(axis)
        forward = [(i, i + 1) for i in range(count - 1)]
        if periodic:
            forward.append((count - 1, 0))
        backward = [(target, source) for source, target in forward]
        low = lax.ppermute(
            lax.slice_in_dim(block, block.shape[dim] - width, None, axis=dim), axis, forward
        )
        high = lax.ppermute(lax.slice_in_dim(block, 0, width, axis=dim), axis, backward)
        block = jnp.concatenate([low, block, high], axis=dim)
    return block


def emit(padded, margin, length, coupling_row, optical, occupation, shifts):
    lesser = padded[0]
    greater = padded[1]

    def energy_view(source, offset):
        return lax.dynamic_slice_in_dim(source, margin + offset, length, axis=source.ndim - 1)

    sigma_less = coupling_row[:, None] * energy_view(lesser, 0)
    sigma_more = coupling_row[:, None] * energy_view(greater, 0)
    for column in range(2):
        strength = optical[column]
        number = occupation[column]
        offset = shifts[column]
        sigma_less = sigma_less + strength * (
            (number + 1.0) * energy_view(lesser, offset) + number * energy_view(lesser, -offset)
        )
        sigma_more = sigma_more + strength * (
            (number + 1.0) * energy_view(greater, -offset) + number * energy_view(greater, offset)
        )
    return jnp.stack([sigma_less, sigma_more])


def _pick(mask, x, axis):
    return jnp.sum(jnp.where(mask, x, 0.0), axis=axis, keepdims=True)


def _weights_from_products(prod):
    size_n = HIST
    row = lax.broadcasted_iota(jnp.int32, prod.shape, 0)
    col = lax.broadcasted_iota(jnp.int32, prod.shape, 1)
    rows, cols = prod.shape
    down = pltpu.roll(prod, rows - 1, 0)
    right = pltpu.roll(prod, cols - 1, 1)
    diag = pltpu.roll(down, cols - 1, 1)
    inside = (row < size_n) & (col < size_n)
    system = jnp.where(inside, prod - right - down + diag, 0.0)
    target = _pick((col == 0) & (row < size_n), prod - down, 1)
    eye = inside & (row == col)
    trace = jnp.sum(jnp.where(eye, system, 0.0), keepdims=True)
    ridge = ridge_share * trace / size_n + 1e-06
    a = system + jnp.where(eye, ridge, 0.0)
    lower = jnp.zeros_like(a)
    upper = jnp.zeros_like(a)
    diagonal = []
    for j in range(size_n):
        head = _pick((row == j) & (col == j), a, None).reshape(1, 1)
        pivot = jnp.sqrt(head)
        diagonal.append(head / pivot)
        lcol = jnp.where(row[:, :1] >= j, _pick(col == j, a, 1) / pivot, 0.0)
        lrow = jnp.where(col[:1, :] >= j, _pick(row == j, a, 0) / pivot, 0.0)
        lower = lower + jnp.where(col == j, lcol, 0.0)
        upper = upper + jnp.where(row == j, lrow, 0.0)
        a = a - lcol * lrow
    row1 = row[:, :1]
    rest = target
    forward = jnp.zeros_like(target)
    for i in range(size_n):
        lii = diagonal[i]
        yi = _pick(row1 == i, rest, 0) / lii
        forward = forward + jnp.where(row1 == i, yi, 0.0)
        rest = rest - jnp.where(row1 > i, _pick(col == i, lower, 1), 0.0) * yi
    rest = forward
    gamma = jnp.zeros_like(target)
    for i in range(size_n - 1, -1, -1):
        lii = diagonal[i]
        gi = _pick(row1 == i, rest, 0) / lii
        gamma = gamma + jnp.where(row1 == i, gi, 0.0)
        rest = rest - jnp.where(row1 < i, _pick(col == i, upper, 1), 0.0) * gi
    before = pltpu.roll(gamma, 1, 0)
    weights = jnp.where(row1 == 0, 1.0, 0.0) - gamma + before
    return jnp.broadcast_to(weights, prod.shape)


def _permute_square(prod, perm):
    row = lax.broadcasted_iota(jnp.int32, prod.shape, 0)
    col = lax.broadcasted_iota(jnp.int32, prod.shape, 1)
    count = len(perm)
    permcol = jnp.zeros((prod.shape[0], 1), jnp.int32)
    permrow = jnp.zeros((1, prod.shape[1]), jnp.int32)
    for i in range(count):
        permcol = jnp.where(row[:, :1] == i, perm[i], permcol)
        permrow = jnp.where(col[:1, :] == i, perm[i], permrow)
    by_rows = jnp.zeros_like(prod)
    for m in range(count):
        by_rows = by_rows + jnp.where(permcol == m, _pick(row == m, prod, 0), 0.0)
    by_rows = jnp.where(row < count, by_rows, 0.0)
    both = jnp.zeros_like(prod)
    for m in range(count):
        both = both + jnp.where(permrow == m, _pick(col == m, by_rows, 1), 0.0)
    return jnp.where(col < count, both, 0.0)


def _pair_sums(vectors, pairs):
    shape = (8, 128)
    row = lax.broadcasted_iota(jnp.int32, shape, 0)
    col = lax.broadcasted_iota(jnp.int32, shape, 1)
    prod = jnp.zeros(shape, jnp.float32)
    for i, j in pairs:
        value = jnp.sum(vectors[i] * vectors[j], keepdims=True)
        spot = ((row == i) & (col == j)) | ((row == j) & (col == i))
        prod = jnp.where(spot, value, prod)
    return prod


def _pack_rows(prod):
    row = lax.broadcasted_iota(jnp.int32, prod.shape, 0)
    packed = jnp.zeros((1, prod.shape[1]), jnp.float32)
    for i in range(HIST + 1):
        packed = packed + pltpu.roll(_pick(row == i, prod, 0), 8 * i, 1)
    return packed


def _unpack_rows(packed):
    shape = (8, packed.shape[1])
    row = lax.broadcasted_iota(jnp.int32, shape, 0)
    col = lax.broadcasted_iota(jnp.int32, shape, 1)
    prod = jnp.zeros(shape, jnp.float32)
    for i in range(HIST + 1):
        line = pltpu.roll(packed, (shape[1] - 8 * i) % shape[1], 1)
        prod = jnp.where((row == i) & (col <= HIST), line, prod)
    return prod


def _far_first(count):
    return sorted(range(count - 1), key=lambda s: (-min(s + 1, count - s - 1), s))


def _fused_kernel(nk, ne, entries, margin,
                  slot_ref, shift_ref, class_ref, optical_ref, occ_ref, acoustic_ref,
                  chunk_ref, cur_ref, pin_ref, pres_ref, out_ref,
                  ypad, bases, send1, recv1, recv2, acc1, ts, tr, ss1, rs1, ss2, rs2):
    mk = lax.axis_index("kgrp")
    me = lax.axis_index("energy")
    width = chunk_ref.shape[-1]
    rows, padded_len = ypad.shape
    length = padded_len - 2 * margin
    barrier = pltpu.get_barrier_semaphore()
    for s in _far_first(ne):
        pl.semaphore_signal(barrier, 1, device_id=(mk, (me + s + 1) % ne), device_id_type=MESH)
    for s in _far_first(nk):
        pl.semaphore_signal(barrier, 1, device_id=((mk + s + 1) % nk, me), device_id_type=MESH)
    ypad[:, :margin] = jnp.zeros((rows, margin), jnp.float32)
    ypad[:, margin + length :] = jnp.zeros((rows, margin), jnp.float32)
    ypad[:, pl.ds(pl.multiple_of(margin + me * width, width), width)] = chunk_ref[:, me, :]
    pl.semaphore_wait(barrier, nk - 1 + ne - 1)

    copies = [None] * (ne - 1)
    odd = me % 2
    for s in _far_first(ne):
        mirrored = odd * (ne - 2 - s) + (1 - odd) * s
        peer = (me + mirrored + 1) % ne
        c = pltpu.make_async_remote_copy(
            src_ref=chunk_ref.at[:, peer, :],
            dst_ref=ypad.at[:, pl.ds(pl.multiple_of(margin + me * width, width), width)],
            send_sem=ts.at[mirrored],
            recv_sem=tr.at[ne - 2 - mirrored],
            device_id=(mk, peer),
            device_id_type=MESH,
        )
        c.start()
        copies[s] = c
    history = [pres_ref[m] for m in range(HIST)]
    gram = _pair_sums([None] + history, [(i, j) for i in range(1, HIST + 1) for j in range(i, HIST + 1)])
    for q in range(ne - 1):
        source = (me + q + 1) % ne
        pltpu.make_async_remote_copy(
            src_ref=chunk_ref.at[:, me, :],
            dst_ref=ypad.at[:, pl.ds(pl.multiple_of(margin + source * width, width), width)],
            send_sem=ts.at[q],
            recv_sem=tr.at[q],
            device_id=(mk, source),
            device_id_type=MESH,
        ).wait_recv()
    for s in range(ne - 1):
        copies[s].wait_send()

    y = ypad[...]
    row = lax.broadcasted_iota(jnp.int32, (rows, 1), 0)
    lead = 8
    lesser = row % lead < lead // 2
    per_row = rows // 8
    coupling = jnp.zeros((rows, 1), jnp.float32)
    for r in range(per_row):
        coupling = jnp.where(row // lead == r, acoustic_ref[class_ref[me * per_row + r]], coupling)
    sigma = coupling * y[:, margin : margin + length]
    for m in range(2):
        shift = shift_ref[m]
        strength = optical_ref[m]
        number = occ_ref[m]
        ahead = pltpu.roll(y, padded_len - shift, 1)[:, margin : margin + length]
        behind = pltpu.roll(y, shift, 1)[:, margin : margin + length]
        up = jnp.where(lesser, number + 1.0, number)
        down = jnp.where(lesser, number, number + 1.0)
        sigma = sigma + strength * (up * ahead + down * behind)
    res = sigma - cur_ref[...]
    fresh = _pair_sums([res] + history, [(0, j) for j in range(HIST + 1)])
    send1[...] = _pack_rows(fresh + gram)

    def exchange(src, recv, ssem, rsem, count, peer):
        out = [None] * (count - 1)
        for s in _far_first(count):
            c = pltpu.make_async_remote_copy(
                src_ref=src,
                dst_ref=recv.at[count - 2 - s],
                send_sem=ssem.at[s],
                recv_sem=rsem.at[count - 2 - s],
                device_id=peer(s),
                device_id_type=MESH,
            )
            c.start()
            out[s] = c
        return out

    def finish(out):
        for c in out:
            c.wait_recv()
        for c in out:
            c.wait_send()

    def total(own, recv, mine, count):
        acc = jnp.zeros_like(own)
        for idx in range(count):
            slot = jnp.minimum((idx - mine - 1 + count) % count, count - 2)
            acc = acc + jnp.where(idx == mine, own, recv[slot])
        return acc

    pending = exchange(send1, recv1, ss1, rs1, nk, lambda s: ((mk + s + 1) % nk, me))
    for m in range(HIST):
        bases[m] = pin_ref[m] + mixing_share * history[m]
    finish(pending)
    acc1[...] = total(send1[...], recv1, mk, nk)
    finish(exchange(acc1, recv2, ss2, rs2, ne, lambda s: (mk, (me + s + 1) % ne)))
    summed = _unpack_rows(total(acc1[...], recv2, me, ne))
    perm = [0] + [slot_ref[i] + 1 for i in range(HIST)]
    aged = _permute_square(summed / entries, perm)
    weights = _weights_from_products(aged)[:, :1]
    row1 = lax.broadcasted_iota(jnp.int32, weights.shape, 0)
    slot_w = [None] * (HIST + 1)
    for i in range(HIST + 1):
        w_i = _pick(row1 == i, weights, 0)
        for m in range(HIST + 1):
            term = jnp.where(perm[i] == m, w_i, 0.0)
            slot_w[m] = term if slot_w[m] is None else slot_w[m] + term
    mixed = slot_w[0] * (cur_ref[...] + mixing_share * res)
    for m in range(HIST):
        mixed = mixed + slot_w[m + 1] * bases[m]
    out_ref[...] = mixed


def fused_tail(scalars, chunks, cur, pin, pres, nk, ne, entries):
    tile = (1, 128)
    margin = 128
    rows = chunks.shape[0]
    smem = pl.BlockSpec(memory_space=pltpu.SMEM)
    vmem = pl.BlockSpec(memory_space=pltpu.VMEM)
    return pl.pallas_call(
        functools.partial(_fused_kernel, nk, ne, entries, margin),
        out_shape=jax.ShapeDtypeStruct(cur.shape, jnp.float32),
        in_specs=[smem] * len(scalars) + [vmem] * 4,
        out_specs=vmem,
        scratch_shapes=[
            pltpu.VMEM((rows, cur.shape[1] + 2 * margin), jnp.float32),
            pltpu.VMEM((HIST,) + cur.shape, jnp.float32),
            pltpu.VMEM(tile, jnp.float32),
            pltpu.VMEM((nk - 1,) + tile, jnp.float32),
            pltpu.VMEM((ne - 1,) + tile, jnp.float32),
            pltpu.VMEM(tile, jnp.float32),
            pltpu.SemaphoreType.DMA((ne - 1,)),
            pltpu.SemaphoreType.DMA((ne - 1,)),
            pltpu.SemaphoreType.DMA((nk - 1,)),
            pltpu.SemaphoreType.DMA((nk - 1,)),
            pltpu.SemaphoreType.DMA((ne - 1,)),
            pltpu.SemaphoreType.DMA((ne - 1,)),
        ],
        compiler_params=pltpu.CompilerParams(collective_id=0, has_side_effects=True),
    )(*scalars, chunks, cur, pin, pres)


def per_device(
    greens,
    current,
    past_inputs,
    past_residuals,
    slot_order,
    neighbour,
    momentum_class,
    stencil_weight,
    acoustic_coupling,
    optical_coupling,
    occupation,
    phonon_shift,
):
    group_len = greens.shape[3]
    rows_here = current.shape[3]
    group_id = lax.axis_index("kgrp")
    energy_id = lax.axis_index("energy")
    nk = lax.axis_size("kgrp")
    ne = lax.axis_size("energy")
    total_k = group_len * nk
    ends = padded_2(greens, (("kgrp", 3),), group_len, True)
    low = ends[:, :, :, :group_len]
    high = ends[:, :, :, 2 * group_len :]
    local_index = (neighbour - group_id * group_len + group_len) % total_k
    stencil = jnp.sum(
        jnp.where(
            local_index[:, :, None] == jnp.arange(3 * group_len, dtype=jnp.int32)[None, None, :],
            stencil_weight[None, :, None],
            0.0,
        ),
        axis=1,
    )
    lead = greens.shape[:3]
    flat = lambda x: x.reshape((-1,) + x.shape[3:])
    stencil = stencil.reshape(ne, rows_here, 3 * group_len)
    chunks = jnp.zeros((rows_here, flat(greens).shape[0], ne, greens.shape[4]), jnp.float32)
    for part, block in enumerate((low, greens, high)):
        chunks = chunks + jnp.einsum(
            "dkr,bre->kbde",
            stencil[:, :, part * group_len : (part + 1) * group_len],
            flat(block),
            precision=lax.Precision.HIGHEST,
        )
    chunks = chunks.reshape(-1, ne, greens.shape[4])
    lanes = current.shape[-1]
    entries = float(current.size * nk * ne)
    scalars = (slot_order, phonon_shift, momentum_class, optical_coupling, occupation, acoustic_coupling)
    def to_rows(x):
        x = x.reshape((-1, flat(greens).shape[0], rows_here, lanes))
        return jnp.swapaxes(x, 1, 2).reshape((-1, rows_here * flat(greens).shape[0], lanes))

    mixed = fused_tail(
        scalars,
        chunks,
        to_rows(current)[0],
        to_rows(past_inputs),
        to_rows(past_residuals),
        nk,
        ne,
        entries,
    )
    mixed = jnp.swapaxes(mixed.reshape(rows_here, -1, lanes), 0, 1).reshape(current.shape)
    return mixed


def solution(mesh):
    return jax.shard_map(
        per_device,
        mesh=mesh,
        in_specs=(
            P(None, None, None, "kgrp", "energy"),
            P(None, None, None, ("kgrp", "energy"), None),
            P(None, None, None, None, ("kgrp", "energy"), None),
            P(None, None, None, None, ("kgrp", "energy"), None),
            P(),
            P("kgrp", None),
            P("kgrp"),
            P(),
            P(),
            P(),
            P(),
            P(),
        ),
        out_specs=P(None, None, None, ("kgrp", "energy"), None),
        check_vma=False,
    )
```
